32 devices in a mesh: doc: 4 (over y, x), seg: 8 (over z, core).
Axes of the slice: x: 2, y: 2, z: 4, core: 2. Of those that a mesh axis runs over, the one named last changes fastest.
Arguments:
- tokens: bfloat16 [8, 1024, 768], P('doc', 'seg'), may hold values from -6 to 6
- token_mask: int32 [8, 1024], P('doc', 'seg'), may hold values from 0 to 1, as said below
- doc_counts: int32 [8], P('doc'), may hold values from 256 to 1024, as said below
- w_qkv: bfloat16 [2, 768, 2304], replicated, may hold values from -0.21875 to 0.21875
- w_out: bfloat16 [2, 768, 768], replicated, may hold values from -1.75 to 1.75
- w_up: bfloat16 [2, 768, 3072], replicated, may hold values from -0.21875 to 0.21875
- w_down: bfloat16 [2, 3072, 768], replicated, may hold values from -0.109375 to 0.109375
- vectors: float32 [2, 8, 768], replicated, may hold values from -1 to 1.4, as said below
- ffn_bias: float32 [2, 3072], replicated, may hold values from -3 to 3
- pos_embed: float32 [8, 768], replicated, may hold values from -3 to 3
- cotangent: bfloat16 [8, 1024, 768], P('doc', 'seg'), may hold values from -6 to 6
Outputs:
- output: bfloat16 [8, 1024, 768], P('doc', 'seg')
- grad_tokens: float32 [8, 1024, 768], P('doc', 'seg')
- grad_qkv: float32 [2, 768, 2304], P(None, 'seg', 'doc')
- grad_out: float32 [2, 768, 768], P(None, 'seg', 'doc')
- grad_up: float32 [2, 768, 3072], P(None, 'seg', 'doc')
- grad_down: float32 [2, 3072, 768], P(None, 'seg', 'doc')
- grad_vectors: float32 [2, 8, 768], P(None, 'doc', 'seg')
- grad_ffn_bias: float32 [2, 3072], P(None, 'seg')
- grad_pos: float32 [8, 768], P(None, 'seg')
The draws below stay inside these ranges and needn't reach their ends.
Inputs may be any that keep to these rules, and one draw needn't show every extreme that they name: `token_mask`: the first slot of every segment is 1; other slots are 1 only below the document's count. `doc_counts`: document 0 of every draw has all 1024 slots. `vectors`: rows 3 and 6 of each layer lie in 0.6 to 1.4, the others in -1 to 1.
All inputs are finite; a program needn't handle non-finite values.
Results may differ from the reference program's by a relative error of at most 0.02.
Values may be sent and summed in bfloat16 or wider, within the bound.
A program may use at most 256 MiB of HBM per device.

```python
import jax
import jax.numpy as jnp
from jax import lax

D = 768
FF = 3072
HEAD = 64
SEG = 128
SEGS = 8
DOCS = 8


def doc_layout(key):
    slots = SEGS * SEG
    counts = jax.random.randint(jax.random.fold_in(key, 11), (DOCS,), slots // 4, slots + 1)
    counts = counts.at[0].set(slots)
    live = jax.random.randint(jax.random.fold_in(key, 12), (DOCS, slots), 0, 8) > 0
    place = lax.broadcasted_iota(jnp.int32, (DOCS, slots), 1)
    inside = place < counts[:, None]
    heads_slot = place % SEG == 0
    mask = jnp.where(jnp.logical_or(jnp.logical_and(inside, live), heads_slot), 1, 0)
    return (counts.astype(jnp.int32), mask.astype(jnp.int32))


def draw_doc_counts(key, part):
    return doc_layout(key)[0]


def draw_token_mask(key, part):
    return doc_layout(key)[1]


def draw_vectors(key, part):
    rows = lax.broadcasted_iota(jnp.int32, (2, 8, D), 1)
    gain_rows = jnp.logical_or(rows == 3, rows == 6)
    noise = jnp.clip(0.5 * jax.random.normal(key, (2, 8, D), jnp.float32), -1.0, 1.0)
    return jnp.where(gain_rows, 1.0 + 0.4 * noise, noise).astype(jnp.float32)


def block_levels(rng, shape, cuts, smallest, high):
    factor_of = 1.0
    for axis_at, parts in cuts:
        steps = jax.random.uniform(jax.random.fold_in(jax.random.fold_in(rng, 6), axis_at), (parts,), jnp.float32, smallest / len(cuts), high / len(cuts))
        factor_of = factor_of * jnp.repeat(jnp.exp(steps), shape[axis_at] // parts).reshape((-1,) + (1,) * (len(shape) - 1 - axis_at))
    return factor_of


def centred(rng, extent, scale, bound, cuts=(), held_as=jnp.bfloat16):
    values = jax.random.normal(rng, extent, jnp.float32) * scale
    if len(cuts) > 0:
        values = block_levels(rng, extent, cuts, -0.22, 0.18) * values
    return jnp.clip(values, min=-bound, max=bound).astype(held_as)


def setup_inputs(seed: int = 0) -> dict:
    keys = jax.random.split(jax.random.key(seed), 12)
    tokens = centred(keys[0], (DOCS, SEGS * SEG, D), 1.0, 6.0, ((0, 4), (1, 8)))
    token_mask = draw_token_mask(jax.random.fold_in(keys[11], 71), 0)
    doc_counts = draw_doc_counts(jax.random.fold_in(keys[11], 71), 0)
    w_qkv = centred(keys[3], (2, D, 3 * D), D ** -0.5, 0.21875)
    w_out = centred(keys[4], (2, D, D), (max(D // 64, 1)) ** -0.5, 1.75)
    w_up = centred(keys[5], (2, D, FF), D ** -0.5, 0.21875)
    w_down = centred(keys[6], (2, FF, D), FF ** -0.5, 0.109375)
    vectors = draw_vectors(jax.random.fold_in(keys[11], 71), 0)
    ffn_bias = centred(keys[8], (2, FF), 0.5, 3.0, (), jnp.float32)
    pos_embed = centred(keys[9], (SEGS, D), 0.5, 3.0, (), jnp.float32)
    cotangent = centred(keys[10], (DOCS, SEGS * SEG, D), 1.0, 6.0, ((0, 4), (1, 8)))
    return {"tokens": tokens, "token_mask": token_mask, "doc_counts": doc_counts, "w_qkv": w_qkv, "w_out": w_out, "w_up": w_up, "w_down": w_down, "vectors": vectors, "ffn_bias": ffn_bias, "pos_embed": pos_embed, "cotangent": cotangent}


@jax.custom_vjp
def low(v):
    return lax.optimization_barrier(v.astype(jnp.bfloat16)).astype(jnp.float32)

@jax.custom_vjp
def low_back(v):
    return v

def low_keep(v):
    return (low(v), None)

def low_pass(kept, grad):
    return (grad,)

def back_keep(v):
    return (v, None)

def back_low(kept, grad):
    return (low(grad),)
low.defvjp(low_keep, low_pass)
low_back.defvjp(back_keep, back_low)
HIGH = lax.Precision.HIGHEST
NEG = -1e+30

def layer_norm(r, gain, shift):
    mean = lax.optimization_barrier(jnp.mean(r, axis=-1, keepdims=True))
    cent = r - mean
    inv = lax.rsqrt(lax.optimization_barrier(jnp.mean(cent * cent, axis=-1, keepdims=True)) + 1e-05)
    return cent * inv * gain + shift

def gelu_value(u):
    return 0.5 * u * (1.0 + lax.erf(u * 0.7071067811865476))

def layer(h, keep, w_qkv, w_out, w_up, w_down, vec, fbias):
    groups, rows, width = h.shape
    heads = width // HEAD
    hb = low(h)
    qkv = jnp.einsum('gld,de->gle', hb, w_qkv, precision=HIGH)
    query = low(low_back(qkv[..., :width] + vec[0])).reshape(groups, rows, heads, HEAD)
    key_part = low(low_back(qkv[..., width:2 * width])).reshape(groups, rows, heads, HEAD)
    value = low(low_back(qkv[..., 2 * width:] + vec[1])).reshape(groups, rows, heads, HEAD)
    scores = low_back(jnp.einsum('glhe,gmhe->ghlm', query, key_part, precision=HIGH) * HEAD ** (-0.5))
    masked = jnp.where(keep[:, None, None, :], scores, NEG)
    probs = jax.nn.softmax(masked, axis=-1)
    context = jnp.einsum('ghlm,gmhe->glhe', low(probs), value, precision=HIGH).reshape(groups, rows, width)
    context = low(low_back(context))
    attn = low_back(jnp.einsum('gld,de->gle', context, w_out, precision=HIGH) + vec[2])
    first_norm = layer_norm(h + attn, vec[3], vec[4])
    pre = low_back(jnp.einsum('gld,df->glf', low(first_norm), w_up, precision=HIGH) + fbias)
    ffn = low_back(jnp.einsum('glf,fd->gld', low(gelu_value(pre)), w_down, precision=HIGH) + vec[5])
    return layer_norm(first_norm + ffn, vec[6], vec[7])

def reference(tokens, token_mask, doc_counts, w_qkv, w_out, w_up, w_down, vectors, ffn_bias, pos_embed, cotangent):
    tok_keep = (token_mask > 0).reshape(DOCS, SEGS, SEG)
    starts = lax.broadcasted_iota(jnp.int32, (DOCS, SEGS), 1) * SEG
    seg_keep = starts < doc_counts[:, None]

    def forward(x, wq, wo, wu, wd, vec, fb, pos):

        def seg_doc(pair):
            h, keep = pair
            return layer(h, keep, wq[0], wo[0], wu[0], wd[0], vec[0], fb[0])
        first = lax.map(jax.checkpoint(seg_doc), (x.reshape(DOCS, SEGS, SEG, D), tok_keep))
        summary = low(first[:, :, 0, :])
        cross_in = summary + pos[None]

        def cross_doc(pair):
            h, keep = pair
            return layer(h[None], keep[None], wq[1], wo[1], wu[1], wd[1], vec[1], fb[1])[0]
        mixed = lax.map(jax.checkpoint(cross_doc), (cross_in, seg_keep))
        final = first.at[:, :, 0, :].set(mixed)
        return final.reshape(DOCS, SEGS * SEG, D)
    inputs = (tokens.astype(jnp.float32), w_qkv.astype(jnp.float32), w_out.astype(jnp.float32), w_up.astype(jnp.float32), w_down.astype(jnp.float32), vectors, ffn_bias, pos_embed)
    result, pullback = jax.vjp(forward, *inputs)
    grads = pullback(cotangent.astype(jnp.float32))
    return (result.astype(jnp.bfloat16), grads[0], grads[1], grads[2], grads[3], grads[4], grads[5], grads[6], grads[7])
```

```python
import functools

import jax
import jax.numpy as jnp
from jax import lax
from jax.experimental import pallas as pl
from jax.experimental.pallas import tpu as pltpu
from jax.sharding import PartitionSpec as P

MESH = pl.DeviceIdType.MESH
HEAD = 64
SEG = 128
NEG = -1e30
EPS = 1e-05
ROOT_HALF = 0.7071067811865476
INV_ROOT_TWO_PI = 0.3989422804014327
SCALE = HEAD ** (-0.5)
F32 = jnp.float32
BF16 = jnp.bfloat16
VM = pl.BlockSpec(memory_space=pltpu.VMEM)
SM = pl.BlockSpec(memory_space=pltpu.SMEM)
ANY = pl.BlockSpec(memory_space=pl.ANY)
LIMIT = 58 << 20
QR, QC = 48, 384
NN = (((1,), (0,)), ((), ()))
NT = (((1,), (1,)), ((), ()))
TN = (((0,), (0,)), ((), ()))


def dot(a, b, dims):
    return lax.dot_general(a, b, dims, preferred_element_type=F32)


def norm_forward(resid):
    cent = resid - jnp.mean(resid, axis=-1, keepdims=True)
    inv = lax.rsqrt(jnp.mean(cent * cent, axis=-1, keepdims=True) + EPS)
    return cent * inv, inv


def norm_backward(scaled, normed, inv):
    inner = jnp.mean(scaled * normed, axis=-1, keepdims=True)
    return inv * (scaled - jnp.mean(scaled, axis=-1, keepdims=True) - normed * inner)


def gelu_pair(pre):
    half_cdf = 0.5 * (1.0 + lax.erf(pre * ROOT_HALF))
    slope = half_cdf + pre * jnp.exp(-0.5 * pre * pre) * INV_ROOT_TWO_PI
    return pre * half_cdf, slope


def col_sum(arr):
    return jnp.sum(arr.astype(F32), axis=0, keepdims=True)


def softmax_rows(scores):
    expo = jnp.exp(scores - jnp.max(scores, axis=-1, keepdims=True))
    return expo / jnp.sum(expo, axis=-1, keepdims=True)


def lane_halves(rows):
    lane = lax.broadcasted_iota(jnp.int32, (rows, 128), 1)
    return lane < HEAD


def two_heads(slab):
    low = lane_halves(slab.shape[0])
    zero = jnp.zeros_like(slab)
    return jnp.concatenate([jnp.where(low, slab, zero), jnp.where(low, zero, slab)], axis=0)


def fetch(pairs, sem):
    copies = [pltpu.make_async_copy(src, dst, sem.at[i]) for i, (src, dst) in enumerate(pairs)]
    for copy in copies:
        copy.start()
    return copies


def segment_forward(
    tok, mask, w_qkv, w_out, w_up, w_down, vec, fbias, cot,
    qkv, probs, ctx, n1, inv1, h1, act, slope, n2, inv2, heads,
    b_qkv, b_out, b_up, b_down, sem,
):
    rows, width = tok.shape
    groups = rows // SEG
    copies = fetch(
        [(w_qkv.at[0], b_qkv), (w_out.at[0], b_out), (w_up.at[0], b_up), (w_down.at[0], b_down)], sem
    )
    copies[0].wait()
    hidden_low = tok[...]
    for part in range(3):
        cols = slice(part * width, (part + 1) * width)
        out = dot(hidden_low, b_qkv[:, cols], NN)
        if part != 1:
            out = out + vec[0, part // 2 : part // 2 + 1, :]
        qkv[:, cols] = out.astype(BF16)
    for g in range(groups):
        here = slice(g * SEG, (g + 1) * SEG)
        keep = mask[g : g + 1, :] > 0
        for pair in range(width // 128):
            at = pair * 128
            query = two_heads(qkv[here, at : at + 128])
            scores = dot(query, qkv[here, width + at : width + at + 128], NT) * SCALE
            prob = softmax_rows(jnp.where(keep, scores, NEG))
            probs[g * (width // 128) + pair] = prob
            low = prob.astype(BF16)
            side = jnp.concatenate([low[:SEG], low[SEG:]], axis=1)
            value = two_heads(qkv[here, 2 * width + at : 2 * width + at + 128])
            ctx[here, at : at + 128] = dot(side, value, NN).astype(BF16)
    copies[1].wait()
    resid = tok[...].astype(F32) + (dot(ctx[...], b_out[...], NN) + vec[0, 2:3, :])
    normed, inv = norm_forward(resid)
    n1[...] = normed
    inv1[...] = jnp.broadcast_to(inv, inv1.shape)
    first = normed * vec[0, 3:4, :] + vec[0, 4:5, :]
    h1[...] = first.astype(BF16)
    copies[2].wait()
    step = width
    for part in range(w_up.shape[2] // step):
        cols = slice(part * step, (part + 1) * step)
        value, grad = gelu_pair(dot(h1[...], b_up[:, cols], NN) + fbias[0:1, cols])
        act[:, cols] = value.astype(BF16)
        slope[:, cols] = grad.astype(BF16)
    copies[3].wait()
    first = n1[...] * vec[0, 3:4, :] + vec[0, 4:5, :]
    normed, inv = norm_forward(first + (dot(act[...], b_down[...], NN) + vec[0, 5:6, :]))
    n2[...] = normed
    inv2[...] = jnp.broadcast_to(inv, inv2.shape)
    for g in range(groups):
        at = g * SEG
        final = normed[at : at + 8] * vec[0, 6:7, :] + vec[0, 7:8, :]
        heads[g : g + 1, :] = final[0:1].astype(BF16).astype(F32)
        heads[groups + g : groups + g + 1, :] = cot[at : at + 16, :].astype(F32)[0:1]


def run_segment_forward(tok, mask, w_qkv, w_out, w_up, w_down, vec, fbias, cot):
    rows, width = tok.shape
    hidden = w_up.shape[2]
    groups = rows // SEG
    shape = jax.ShapeDtypeStruct
    return pl.pallas_call(
        segment_forward,
        out_shape=(
            shape((rows, 3 * width), BF16),
            shape((groups * width // 128, 2 * SEG, SEG), F32),
            shape((rows, width), BF16),
            shape((rows, width), F32),
            shape((rows, 128), F32),
            shape((rows, width), BF16),
            shape((rows, hidden), BF16),
            shape((rows, hidden), BF16),
            shape((rows, width), F32),
            shape((rows, 128), F32),
            shape((2 * groups, width), F32),
        ),
        in_specs=[VM, VM, ANY, ANY, ANY, ANY, VM, VM, VM],
        out_specs=(VM,) * 11,
        scratch_shapes=[
            pltpu.VMEM(w_qkv.shape[1:], BF16),
            pltpu.VMEM(w_out.shape[1:], BF16),
            pltpu.VMEM(w_up.shape[1:], BF16),
            pltpu.VMEM(w_down.shape[1:], BF16),
            pltpu.SemaphoreType.DMA((4,)),
        ],
        compiler_params=pltpu.CompilerParams(vmem_limit_bytes=LIMIT),
        name="segment_forward",
    )(tok, mask, w_qkv, w_out, w_up, w_down, vec, fbias, cot)


def share_heads(count, mine, every, send_sem, recv_sem, local_sem):
    seg = lax.axis_index("seg")
    doc = lax.axis_index("doc")
    barrier = pltpu.get_barrier_semaphore()

    def peer(step):
        return lax.rem(seg + step, count)

    def greet(step, carry):
        pl.semaphore_signal(barrier, inc=1, device_id=(doc, peer(step)), device_id_type=MESH)
        return carry

    lax.fori_loop(1, count, greet, 0)
    pl.semaphore_wait(barrier, count - 1)

    def copy(step):
        return pltpu.make_async_remote_copy(
            src_ref=mine,
            dst_ref=every.at[seg],
            send_sem=send_sem.at[step],
            recv_sem=recv_sem.at[step],
            device_id=(doc, peer(step)),
            device_id_type=MESH,
        )

    def begin(step, carry):
        copy(step).start()
        return carry

    lax.fori_loop(1, count, begin, 0)
    local = pltpu.make_async_copy(mine, every.at[seg], local_sem)
    local.start()
    local.wait()

    def finish(step, carry):
        copy(step).wait()
        return carry

    lax.fori_loop(1, count, finish, 0)


def run_share_heads(heads, count):
    return pl.pallas_call(
        functools.partial(share_heads, count),
        out_shape=jax.ShapeDtypeStruct((count,) + heads.shape, F32),
        in_specs=[VM],
        out_specs=VM,
        scratch_shapes=[
            pltpu.SemaphoreType.DMA((count,)),
            pltpu.SemaphoreType.DMA((count,)),
            pltpu.SemaphoreType.DMA,
        ],
        compiler_params=pltpu.CompilerParams(collective_id=0, has_side_effects=True),
        name="share_heads",
    )(heads)


def head_rows(arr, heads):
    rows, width = arr.shape
    lane = lax.broadcasted_iota(jnp.int32, (rows, width), 1)
    zero = jnp.zeros_like(arr)
    parts = [jnp.where(lane // HEAD == h, arr, zero) for h in range(heads)]
    return jnp.concatenate(parts, axis=0)


def head_join(arr, heads):
    rows = arr.shape[0] // heads
    lane = lax.broadcasted_iota(jnp.int32, (rows, arr.shape[1]), 1)
    out = jnp.zeros((rows, arr.shape[1]), F32)
    for h in range(heads):
        out = jnp.where(lane // HEAD == h, arr[h * rows : (h + 1) * rows], out)
    return out


def cross_layer(
    docs, counts, every, pos, w_qkv, w_out, w_up, w_down, vec, fbias,
    mixed, dcross, pack_x, pack_y, pack_v, grad_pos,
    b_qkv, b_out, b_up, b_down, qkv, cross_in, cot, act, slope, dpre, sem,
):
    segs = every.shape[0]
    width = pos.shape[1]
    heads = width // HEAD
    rows = docs * segs
    hidden = act.shape[1]
    copies = fetch(
        [(w_qkv.at[1], b_qkv), (w_out.at[1], b_out), (w_up.at[1], b_up), (w_down.at[1], b_down)], sem
    )
    for d in range(docs):
        for s in range(segs):
            r = d * segs + s
            cross_in[r : r + 1, :] = every[s, d : d + 1, :] + pos[s : s + 1, :]
            cot[r : r + 1, :] = every[s, docs + d : docs + d + 1, :]
    base = cross_in[...]
    base_low = base.astype(BF16)
    copies[0].wait()
    for part in range(3):
        cols = slice(part * width, (part + 1) * width)
        out = dot(base_low, b_qkv[:, cols], NN)
        if part != 1:
            out = out + vec[1, part // 2 : part // 2 + 1, :]
        qkv[:, cols] = out.astype(BF16)
    query = head_rows(qkv[:, 0:width], heads)
    row_doc = lax.rem(lax.broadcasted_iota(jnp.int32, (heads * rows, rows), 0), rows) // segs
    key = lax.broadcasted_iota(jnp.int32, (heads * rows, rows), 1)
    count = jnp.zeros((heads * rows, rows), jnp.int32)
    for d in range(docs):
        count = jnp.where(key // segs == d, counts[d], count)
    keep = jnp.logical_and(row_doc == key // segs, lax.rem(key, segs) * SEG < count)
    scores = dot(query, qkv[:, width : 2 * width], NT) * SCALE
    prob = softmax_rows(jnp.where(keep, scores, NEG))
    prob_low = prob.astype(BF16)
    context = head_join(dot(prob_low, qkv[:, 2 * width : 3 * width], NN), heads).astype(BF16)
    copies[1].wait()
    n1, inv1 = norm_forward(base + (dot(context, b_out[...], NN) + vec[1, 2:3, :]))
    first = n1 * vec[1, 3:4, :] + vec[1, 4:5, :]
    first_low = first.astype(BF16)
    copies[2].wait()
    for part in range(hidden // width):
        cols = slice(part * width, (part + 1) * width)
        value, grad = gelu_pair(dot(first_low, b_up[:, cols], NN) + fbias[1:2, cols])
        act[:, cols] = value.astype(BF16)
        slope[:, cols] = grad
    copies[3].wait()
    n2, inv2 = norm_forward(first + (dot(act[...], b_down[...], NN) + vec[1, 5:6, :]))
    mixed[...] = n2 * vec[1, 6:7, :] + vec[1, 7:8, :]
    g = cot[...]
    gain2 = col_sum(g * n2)
    shift2 = col_sum(g)
    dr2 = norm_backward(g * vec[1, 6:7, :], n2, inv2)
    dffn = dr2.astype(BF16)
    for part in range(hidden // width):
        cols = slice(part * width, (part + 1) * width)
        dpre[:, cols] = (dot(dffn, b_down[cols, :], NT) * slope[:, cols]).astype(BF16)
    dh1 = dr2 + dot(dpre[...], b_up[...], NT)
    gain1 = col_sum(dh1 * n1)
    shift1 = col_sum(dh1)
    dr1 = norm_backward(dh1 * vec[1, 3:4, :], n1, inv1)
    dattn = dr1.astype(BF16)
    dctx = dot(dattn, b_out[...], NT).astype(BF16)
    dctx_rows = head_rows(dctx, heads)
    dp = dot(dctx_rows, qkv[:, 2 * width : 3 * width], NT)
    ds = (prob * (dp - jnp.sum(prob * dp, axis=-1, keepdims=True))).astype(BF16)
    dv = dot(prob_low, dctx_rows, TN).astype(BF16)
    dq = (head_join(dot(ds, qkv[:, width : 2 * width], NN), heads) * SCALE).astype(BF16)
    dk = (dot(ds, query, TN) * SCALE).astype(BF16)
    dh = (
        dr1
        + dot(dq, b_qkv[:, 0:width], NT)
        + dot(dk, b_qkv[:, width : 2 * width], NT)
        + dot(dv, b_qkv[:, 2 * width : 3 * width], NT)
    )
    dcross[...] = dh
    total = dh[0:segs]
    for d in range(1, docs):
        total = total + dh[d * segs : (d + 1) * segs]
    pack_x[...] = jnp.zeros_like(pack_x)
    pack_y[...] = jnp.zeros_like(pack_y)
    pack_v[...] = jnp.zeros_like(pack_v)
    eighth = width // 8
    for b in range(8):
        cols = slice(b * eighth, (b + 1) * eighth)
        pack_x[b, :, 0:eighth] = base_low[:, cols]
        pack_x[b, :, 128 : 128 + eighth] = context[:, cols]
        pack_x[b, :, 256 : 256 + eighth] = first_low[:, cols]
        pack_x[b, :, 384:768] = act[:, b * 384 : (b + 1) * 384]
        sums = [col_sum(dq), col_sum(dv), col_sum(dattn), gain1, shift1, col_sum(dffn), gain2, shift2]
        for i, value in enumerate(sums):
            pack_v[b, i : i + 1, 0:eighth] = value[:, cols]
        grad_pos[b, :, 0:eighth] = total[:, cols]
    put_bias_sums(pack_v, dpre)
    dqkv = jnp.concatenate([dq, dk, dv], axis=1)
    for b in range(4):
        pack_y[b, :, 0:576] = dqkv[:, b * 576 : (b + 1) * 576]
        pack_y[b, :, 640:832] = dattn[:, b * 192 : (b + 1) * 192]
        pack_y[b, :, 896:1664] = dpre[:, b * 768 : (b + 1) * 768]
        pack_y[b, :, 1664:1856] = dffn[:, b * 192 : (b + 1) * 192]


def put_bias_sums(pack_v, dpre):
    for b in range(8):
        for i in range(4):
            at = b * 384 + i * 96
            pack_v[b, 8 + i : 9 + i, 0:96] = col_sum(dpre[:, at : at + 96])


def run_cross_layer(counts, every, pos, w_qkv, w_out, w_up, w_down, vec, fbias):
    docs = counts.shape[0]
    segs, width = pos.shape
    rows = docs * segs
    hidden = w_up.shape[2]
    shape = jax.ShapeDtypeStruct
    return pl.pallas_call(
        functools.partial(cross_layer, docs),
        out_shape=(
            shape((rows, width), F32),
            shape((rows, width), F32),
            shape((8, rows, width), BF16),
            shape((4, rows, 1920), BF16),
            shape((8, 16, 128), F32),
            shape((8, segs, 128), F32),
        ),
        in_specs=[SM, VM, VM, ANY, ANY, ANY, ANY, VM, VM],
        out_specs=(VM,) * 6,
        scratch_shapes=[
            pltpu.VMEM(w_qkv.shape[1:], BF16),
            pltpu.VMEM(w_out.shape[1:], BF16),
            pltpu.VMEM(w_up.shape[1:], BF16),
            pltpu.VMEM(w_down.shape[1:], BF16),
            pltpu.VMEM((rows, 3 * width), BF16),
            pltpu.VMEM((rows, width), F32),
            pltpu.VMEM((rows, width), F32),
            pltpu.VMEM((rows, hidden), BF16),
            pltpu.VMEM((rows, hidden), F32),
            pltpu.VMEM((rows, hidden), BF16),
            pltpu.SemaphoreType.DMA((4,)),
        ],
        compiler_params=pltpu.CompilerParams(vmem_limit_bytes=LIMIT),
        name="cross_layer",
    )(counts, every, pos, w_qkv, w_out, w_up, w_down, vec, fbias)


def xor_bit(a, b):
    return a + b - 2 * a * b


def relative(b, d, me, doc):
    core = xor_bit(lax.rem(me, 2), b % 2)
    low = xor_bit(lax.rem(me // 2, 2), (b // 2) % 2)
    high = xor_bit(me // 4, b // 4)
    x = xor_bit(lax.rem(doc, 2), d % 2)
    y = xor_bit(doc // 2, d // 2)
    return core, x, y, xor_bit(low, high), high


def slot_of(j, bits):
    core, rest = bits[0], bits[1:]
    turned = rest[j:] + rest[:j]
    return core * 16 + turned[0] * 8 + turned[1] * 4 + turned[2] * 2 + turned[3]


def segment_backward(
    stride,
    tok, cot, mixed, dcross, qkv, probs, ctx, n1, inv1, h1, act, slope, n2, inv2,
    w_qkv, w_out, w_up, w_down, vec,
    output, grad_tok, parts, pack_v,
    b_qkv, b_out, b_up, b_down, dffn, dpre, y_qkv, y_out, dqkv, dctx, sem,
):
    rows, width = tok.shape
    groups = rows // SEG
    hidden = act.shape[1]
    seg_index = lax.axis_index("seg")
    doc_index = lax.axis_index("doc")
    me = seg_index // stride
    segs = mixed.shape[0] // groups
    copies = fetch(
        [(w_down.at[0], b_down), (w_up.at[0], b_up), (w_out.at[0], b_out), (w_qkv.at[0], b_qkv)], sem
    )
    pack_v[...] = jnp.zeros_like(pack_v)
    sums = {}
    top = lax.broadcasted_iota(jnp.int32, (SEG, width), 0) == 0
    grads = []
    for g in range(groups):
        here = slice(g * SEG, (g + 1) * SEG)
        own = pl.ds(g * segs + seg_index, 1)
        grads.append(jnp.where(top, dcross[own, :], cot[here, :].astype(F32)))
        final = n2[here, :] * vec[0, 6:7, :] + vec[0, 7:8, :]
        output[here, :] = jnp.where(top, mixed[own, :], final).astype(BF16)
    grad = jnp.concatenate(grads, axis=0)
    normed = n2[...]
    sums[6] = col_sum(grad * normed)
    sums[7] = col_sum(grad)
    dr2 = norm_backward(grad * vec[0, 6:7, :], normed, inv2[:, 0:1])
    dffn[...] = dr2.astype(BF16)
    sums[5] = col_sum(dffn[...])
    copies[0].wait()
    for part in range(hidden // width):
        cols = slice(part * width, (part + 1) * width)
        dpre[:, cols] = (dot(dffn[...], b_down[cols, :], NT) * slope[:, cols].astype(F32)).astype(BF16)
    put_bias_sums(pack_v, dpre)

    def place(kind, j, b, d, value):
        parts[4 * kind + j, slot_of(j, relative(b, d, me, doc_index))] = value.astype(BF16)

    for b in range(8):
        tile = dot(dffn[...], act[:, b * QC : (b + 1) * QC], TN)
        for d in range(4):
            for j in range(4):
                at = d * 192 + j * QR
                place(1, j, b, d, tile[at : at + QR])
    for d in range(4):
        for half in range(2):
            at = d * 768 + half * QC
            tile = dot(h1[...], dpre[:, at : at + QC], TN)
            for b in range(8):
                for top_half in range(2):
                    r = b * 96 + top_half * QR
                    place(0, 2 * top_half + half, b, d, tile[r : r + QR])
    copies[1].wait()
    dh1 = dr2 + dot(dpre[...], b_up[...], NT)
    normed = n1[...]
    sums[3] = col_sum(dh1 * normed)
    sums[4] = col_sum(dh1)
    dr1 = norm_backward(dh1 * vec[0, 3:4, :], normed, inv1[:, 0:1])
    dattn = dr1.astype(BF16)
    sums[2] = col_sum(dattn)
    grad_tok[...] = dr1
    y_out[...] = jnp.zeros_like(y_out)
    y_qkv[...] = jnp.zeros_like(y_qkv)
    low = lane_halves(rows)
    for d in range(4):
        slab = 3 * (d // 2) + 1
        mid = pltpu.roll(dr1[:, slab * 128 : (slab + 1) * 128], HEAD, 1).astype(BF16)
        whole = 3 * (d // 2) + 2 * (d % 2)
        fill = jnp.zeros_like(mid)
        y_out[d, :, 0:128] = jnp.where(low, fill, mid) if d % 2 == 0 else jnp.where(low, mid, fill)
        y_out[d, :, 128:256] = dattn[:, whole * 128 : (whole + 1) * 128]
    copies[2].wait()
    dctx[...] = dot(dattn, b_out[...], NT).astype(BF16)
    for g in range(groups):
        here = slice(g * SEG, (g + 1) * SEG)
        for pair in range(width // 128):
            at = pair * 128
            prob = probs[g * (width // 128) + pair]
            down = two_heads(dctx[here, at : at + 128])
            query = two_heads(qkv[here, at : at + 128])
            key = two_heads(qkv[here, width + at : width + at + 128])
            dp = dot(down, qkv[here, 2 * width + at : 2 * width + at + 128], NT)
            dv = dot(prob.astype(BF16), down, TN)
            ds = (prob * (dp - jnp.sum(prob * dp, axis=-1, keepdims=True))).astype(BF16)
            dq = dot(jnp.concatenate([ds[:SEG], ds[SEG:]], axis=1), key, NN) * SCALE
            dk = dot(ds, query, TN) * SCALE
            half = lane_halves(SEG)
            for kind, value in enumerate((dq, dk, dv)):
                value = value.astype(BF16)
                dqkv[here, kind * width + at : kind * width + at + 128] = value
                slab = kind * (width // 128) + pair
                d, tile = slab // 9 * 2, slab % 9
                if tile < 4:
                    y_qkv[d, here, tile * 128 : (tile + 1) * 128] = value
                elif tile > 4:
                    y_qkv[d + 1, here, (tile - 5) * 128 : (tile - 4) * 128] = value
                else:
                    zero = jnp.zeros_like(value)
                    y_qkv[d, here, 512:640] = jnp.where(half, value, zero)
                    y_qkv[d + 1, here, 512:640] = jnp.where(half, zero, value)
    sums[0] = col_sum(dqkv[:, 0:width])
    sums[1] = col_sum(dqkv[:, 2 * width : 3 * width])
    for b in range(8):
        cols = slice(b * 96, (b + 1) * 96)
        for i in range(8):
            pack_v[b, i : i + 1, 0:96] = sums[i][:, cols]
    for d in range(4):
        left = dot(tok[...], y_qkv[d, :, 0:QC], TN)
        right = dot(tok[...], y_qkv[d, :, QC:640], TN)
        more = dot(ctx[...], y_out[d], TN)
        right = jnp.concatenate([right[:, 0:128], right[:, 128:256] + more[:, 0:128], more[:, 128:256]], axis=1)
        for half, tile in enumerate((left, right)):
            for b in range(8):
                for top_half in range(2):
                    r = b * 96 + top_half * QR
                    place(2, 2 * top_half + half, b, d, tile[r : r + QR])
    copies[3].wait()
    grad_tok[...] = grad_tok[...] + dot(dqkv[...], b_qkv[...], NT)


def run_segment_backward(stride, tok, cot, mixed, dcross, saved, w_qkv, w_out, w_up, w_down, vec):
    rows, width = tok.shape
    hidden = w_up.shape[2]
    shape = jax.ShapeDtypeStruct
    return pl.pallas_call(
        functools.partial(segment_backward, stride),
        out_shape=(
            shape((rows, width), BF16),
            shape((rows, width), F32),
            shape((12, 32, QR, QC), BF16),
            shape((8, 16, 128), F32),
        ),
        in_specs=[VM] * 14 + [ANY] * 4 + [VM],
        out_specs=(VM,) * 4,
        scratch_shapes=[
            pltpu.VMEM(w_qkv.shape[1:], BF16),
            pltpu.VMEM(w_out.shape[1:], BF16),
            pltpu.VMEM(w_up.shape[1:], BF16),
            pltpu.VMEM(w_down.shape[1:], BF16),
            pltpu.VMEM((rows, width), BF16),
            pltpu.VMEM((rows, hidden), BF16),
            pltpu.VMEM((4, rows, 640), BF16),
            pltpu.VMEM((4, rows, 256), BF16),
            pltpu.VMEM((rows, 3 * width), BF16),
            pltpu.VMEM((rows, width), BF16),
            pltpu.SemaphoreType.DMA((4,)),
        ],
        compiler_params=pltpu.CompilerParams(vmem_limit_bytes=LIMIT),
        name="segment_backward",
    )(tok, cot, mixed, dcross, *saved, w_qkv, w_out, w_up, w_down, vec)


def reduce_all(
    stride, count,
    parts, pack_x, pack_y, vec_seg, vec_cross, pos_cross,
    shares, rows_x, rows_y, vec_all, pos_all,
    kept, got_a, got_b, got_c, got_d, got_e, vec_got, pack_one,
    load_sem, send_sem, recv_sem, x_send, x_recv, v_send, v_recv, w_send, w_recv, local_sem,
):
    seg = lax.axis_index("seg")
    doc = lax.axis_index("doc")
    me = seg // stride
    rest = lax.rem(seg, stride)
    core = lax.rem(me, 2)
    z = me // 2
    z_low = lax.rem(z, 2)
    near = z + 1 - 2 * z_low
    partners = {
        "core": (doc, (me + 1 - 2 * core) * stride + rest),
        "x": (doc + 1 - 2 * lax.rem(doc, 2), seg),
        "y": (lax.rem(doc + 2, 4), seg),
        "za": (doc, (near * 2 + core) * stride + rest),
        "zb": (doc, ((3 - z) * 2 + core) * stride + rest),
    }
    turn = ["x", "y", "za", "zb"]
    barrier = pltpu.get_barrier_semaphore()

    def seg_peer(step):
        return (doc, lax.rem(seg + step, count))

    def doc_peer(step):
        return (lax.rem(doc + step, 4), seg)

    def greet(step, carry):
        pl.semaphore_signal(barrier, inc=1, device_id=seg_peer(step), device_id_type=MESH)
        return carry

    lax.fori_loop(1, count, greet, 0)
    for step in range(1, 4):
        pl.semaphore_signal(barrier, inc=1, device_id=doc_peer(step), device_id_type=MESH)
    pl.semaphore_wait(barrier, count + 2)

    got = [got_a, got_b, got_c, got_d, got_e]

    def send(stage, chunk, src):
        name = "core" if stage == 0 else turn[(stage - 1 + chunk % 4) % 4]
        return pltpu.make_async_remote_copy(
            src_ref=src,
            dst_ref=got[stage].at[chunk],
            send_sem=send_sem.at[stage, chunk],
            recv_sem=recv_sem.at[stage, chunk],
            device_id=partners[name],
            device_id_type=MESH,
        )

    order = [4, 5, 6, 7, 0, 1, 2, 3, 8, 9, 10, 11]
    sends = {}
    loads = {}
    for chunk in order:
        sends[0, chunk] = send(0, chunk, parts.at[chunk, pl.ds(16, 16)])
        sends[0, chunk].start()
        loads[chunk] = pltpu.make_async_copy(parts.at[chunk, pl.ds(0, 16)], kept.at[chunk], load_sem.at[chunk])
        loads[chunk].start()
    local = []
    for i, (src, dst) in enumerate(
        [(pack_x.at[me], rows_x.at[doc]), (pack_y.at[doc], rows_y.at[doc]), (vec_seg.at[me], vec_got.at[seg])]
    ):
        copy = pltpu.make_async_copy(src, dst, local_sem.at[i])
        copy.start()
        local.append(copy)
    exchange = []
    for step in range(1, 4):
        there = doc_peer(step)
        pair = [(pack_x.at[me], rows_x.at[doc]), (pack_y.at[there[0]], rows_y.at[doc])]
        for i, (src, dst) in enumerate(pair):
            copy = pltpu.make_async_remote_copy(
                src_ref=src,
                dst_ref=dst,
                send_sem=x_send.at[step, i],
                recv_sem=x_recv.at[step, i],
                device_id=there,
                device_id_type=MESH,
            )
            copy.start()
            exchange.append(copy)

    def vec_copy(step):
        there = seg_peer(step)
        return pltpu.make_async_remote_copy(
            src_ref=vec_seg.at[there[1] // stride],
            dst_ref=vec_got.at[seg],
            send_sem=v_send.at[step],
            recv_sem=v_recv.at[step],
            device_id=there,
            device_id_type=MESH,
        )

    def vec_begin(step, carry):
        vec_copy(step).start()
        return carry

    lax.fori_loop(1, count, vec_begin, 0)

    def add(chunk, stage, first, last):
        def body(i, carry):
            total = kept[chunk, i].astype(F32) + got[stage][chunk, i].astype(F32)
            kept[chunk, i] = total.astype(BF16)
            return carry

        lax.fori_loop(first, last, body, 0, unroll=min(4, last - first))

    for stage in range(5):
        size = 16 >> stage
        for chunk in order:
            if stage == 0:
                loads[chunk].wait()
            sends[stage, chunk].wait_recv()
            if stage < 4:
                half = size // 2
                add(chunk, stage, half, size)
                sends[stage + 1, chunk] = send(stage + 1, chunk, kept.at[chunk, pl.ds(half, half)])
                sends[stage + 1, chunk].start()
                add(chunk, stage, 0, half)
            else:
                shares[chunk] = kept[chunk, 0].astype(F32) + got[4][chunk, 0].astype(F32)
        if stage == 0:
            for copy in local:
                copy.wait()

            def vec_finish(step, carry):
                vec_copy(step).wait()
                return carry

            lax.fori_loop(1, count, vec_finish, 0)

            def vec_add(i, total):
                return total + vec_got[i]

            total = lax.fori_loop(0, count, vec_add, jnp.zeros(vec_got.shape[1:], F32))
            pack_one[0:16, :] = total
            pack_one[16:32, :] = vec_cross[me]
            pack_one[32:, :] = pos_cross[me]
            local = [pltpu.make_async_copy(pack_one, vec_all.at[doc], local_sem.at[3])]
            local[0].start()
            spread = []
            for step in range(1, 4):
                copy = pltpu.make_async_remote_copy(
                    src_ref=pack_one,
                    dst_ref=vec_all.at[doc],
                    send_sem=w_send.at[step],
                    recv_sem=w_recv.at[step],
                    device_id=doc_peer(step),
                    device_id_type=MESH,
                )
                copy.start()
                spread.append(copy)
    for copy in exchange + spread:
        copy.wait()
    local[0].wait()
    pos_all[...] = vec_all[0] + vec_all[1] + vec_all[2] + vec_all[3]
    for copy in sends.values():
        copy.wait_send()


def run_reduce_all(stride, count, parts, pack_x, pack_y, vec_seg, vec_cross, pos_cross):
    shape = jax.ShapeDtypeStruct
    rows = pack_x.shape[1]
    tall = 32 + pos_cross.shape[1]
    return pl.pallas_call(
        functools.partial(reduce_all, stride, count),
        out_shape=(
            shape((12, QR, QC), F32),
            shape((4,) + pack_x.shape[1:], BF16),
            shape((4,) + pack_y.shape[1:], BF16),
            shape((4, tall, 128), F32),
            shape((tall, 128), F32),
        ),
        in_specs=[ANY, VM, VM, VM, VM, VM],
        out_specs=(VM,) * 5,
        scratch_shapes=[pltpu.VMEM((12, 16, QR, QC), BF16)]
        + [pltpu.VMEM((12, 16 >> i, QR, QC), BF16) for i in range(5)]
        + [
            pltpu.VMEM((count, 16, 128), F32),
            pltpu.VMEM((tall, 128), F32),
            pltpu.SemaphoreType.DMA((12,)),
            pltpu.SemaphoreType.DMA((5, 12)),
            pltpu.SemaphoreType.DMA((5, 12)),
            pltpu.SemaphoreType.DMA((4, 2)),
            pltpu.SemaphoreType.DMA((4, 2)),
            pltpu.SemaphoreType.DMA((count,)),
            pltpu.SemaphoreType.DMA((count,)),
            pltpu.SemaphoreType.DMA((4,)),
            pltpu.SemaphoreType.DMA((4,)),
            pltpu.SemaphoreType.DMA((4,)),
        ],
        compiler_params=pltpu.CompilerParams(
            collective_id=1, has_side_effects=True, vmem_limit_bytes=LIMIT
        ),
        name="reduce_all",
    )(parts, pack_x, pack_y, vec_seg, vec_cross, pos_cross)


def assemble(shares, rows_x, rows_y, sums, g_qkv, g_out, g_up, g_down, g_vec, g_bias):
    rows = rows_x.shape[0] * rows_x.shape[1]
    doc = lax.axis_index("doc")
    x = rows_x[...].reshape(rows, rows_x.shape[2])
    y = rows_y[...].reshape(rows, rows_y.shape[2])
    g_qkv[1] = dot(x[:, 0:128], y[:, 0:640], TN)[0:96, 0:576]
    g_out[1] = dot(x[:, 128:256], y[:, 640:896], TN)[0:96, 0:192]
    g_up[1] = dot(x[:, 256:384], y[:, 896:1664], TN)[0:96, :]
    g_down[1] = dot(x[:, 384:768], y[:, 1664:1920], TN)[:, 0:192]
    for r in range(2):
        at = slice(r * QR, (r + 1) * QR)
        for c in range(2):
            g_up[0, at, c * QC : (c + 1) * QC] = shares[2 * r + c]
    tall = jnp.concatenate([shares[4], shares[5], shares[6], shares[7]], axis=0)
    g_down[0] = jnp.transpose(tall)
    for r in range(2):
        at = slice(r * QR, (r + 1) * QR)
        left, right = shares[8 + 2 * r], shares[9 + 2 * r]
        mid, last = right[:, 128:256], right[:, 256:384]
        qkv_slabs = jnp.concatenate([left, right[:, 0:128]], axis=1)

        @pl.when(lax.rem(doc, 2) == 0)
        def _():
            g_qkv[0, at, 0:512] = qkv_slabs
            g_qkv[0, at, 512:576] = mid[:, 0:64]
            g_out[0, at, 0:128] = last
            g_out[0, at, 128:192] = mid[:, 64:128]

        @pl.when(lax.rem(doc, 2) == 1)
        def _():
            g_qkv[0, at, :] = jnp.concatenate([mid[:, 64:128], qkv_slabs], axis=1)
            g_out[0, at, :] = jnp.concatenate([mid[:, 0:64], last], axis=1)

    for layer in range(2):
        g_vec[layer] = sums[16 * layer : 16 * layer + 8, :]
        g_bias[layer] = sums[16 * layer + 8 : 16 * layer + 12, :]


def run_assemble(shares, rows_x, rows_y, sums):
    shape = jax.ShapeDtypeStruct
    return pl.pallas_call(
        assemble,
        out_shape=(
            shape((2, 96, 576), F32),
            shape((2, 96, 192), F32),
            shape((2, 96, 768), F32),
            shape((2, 384, 192), F32),
            shape((2, 8, 128), F32),
            shape((2, 4, 128), F32),
        ),
        in_specs=[VM] * 4,
        out_specs=(VM,) * 6,
        compiler_params=pltpu.CompilerParams(vmem_limit_bytes=LIMIT),
        name="assemble",
    )(shares, rows_x, rows_y, sums)


def shards(
    tokens,
    token_mask,
    doc_counts,
    w_qkv,
    w_out,
    w_up,
    w_down,
    vectors,
    ffn_bias,
    pos_embed,
    cotangent,
):
    docs, slots, width = tokens.shape
    seg_dev = slots // SEG
    groups = docs * seg_dev
    count = lax.axis_size("seg")
    stride = count // 8
    rest = lax.rem(lax.axis_index("seg"), stride)
    tok = tokens.reshape(groups * SEG, width)
    cot = cotangent.reshape(groups * SEG, width)
    weights = (w_qkv, w_out, w_up, w_down)
    *saved, heads = run_segment_forward(
        tok, token_mask.reshape(groups, SEG), *weights, vectors, ffn_bias, cot
    )
    every = run_share_heads(heads, count)
    mixed, dcross, pack_x, pack_y, vec_cross, pos_cross = run_cross_layer(
        doc_counts, every, pos_embed, *weights, vectors, ffn_bias
    )
    output, grad_tok, parts, vec_seg = run_segment_backward(
        stride, tok, cot, mixed, dcross, saved, *weights, vectors
    )
    shares, rows_x, rows_y, _, sums = run_reduce_all(
        stride, count, parts, pack_x, pack_y, vec_seg, vec_cross, pos_cross
    )
    g_qkv, g_out, g_up, g_down, g_vec, g_bias = run_assemble(shares, rows_x, rows_y, sums)
    if stride > 1:
        lanes = [[i * stride + j for j in range(stride)] for i in range(8)]

        def own(arr, dim):
            low = lax.psum_scatter(arr[0:1], "seg", scatter_dimension=dim, axis_index_groups=lanes, tiled=True)
            size = arr.shape[dim] // stride
            return jnp.concatenate([low, lax.dynamic_slice_in_dim(arr[1:2], rest * size, size, dim)], axis=0)

        g_qkv, g_out, g_up, g_down = own(g_qkv, 1), own(g_out, 1), own(g_up, 1), own(g_down, 1)
    doc = lax.axis_index("doc")
    each = 96 // stride
    g_vec = lax.dynamic_slice(g_vec, (0, doc * 2, rest * each), (2, 2, each))
    g_bias = g_bias[:, :, 0:96].reshape(2, 384)
    g_bias = lax.dynamic_slice_in_dim(g_bias, rest * (384 // stride), 384 // stride, 1)
    g_pos = lax.dynamic_slice_in_dim(sums[32:], rest * each, each, 1)
    return (
        output.reshape(tokens.shape),
        grad_tok.reshape(tokens.shape),
        g_qkv,
        g_out,
        g_up,
        g_down,
        g_vec,
        g_bias,
        g_pos,
    )


def solution(mesh):
    return jax.shard_map(
        shards,
        mesh=mesh,
        in_specs=(
            P("doc", "seg", None),
            P("doc", "seg"),
            P("doc"),
            P(),
            P(),
            P(),
            P(),
            P(),
            P(),
            P(),
            P("doc", "seg", None),
        ),
        out_specs=(
            P("doc", "seg", None),
            P("doc", "seg", None),
            P(None, "seg", "doc"),
            P(None, "seg", "doc"),
            P(None, "seg", "doc"),
            P(None, "seg", "doc"),
            P(None, "doc", "seg"),
            P(None, "seg"),
            P(None, "seg"),
        ),
        check_vma=False,
    )
```

```python
import functools

import jax
import jax.numpy as jnp
from jax import lax
from jax.experimental import pallas as pl
from jax.experimental.pallas import tpu as pltpu
from jax.sharding import PartitionSpec as P

MESH = pl.DeviceIdType.MESH
HEAD = 64
SEG = 128
NEG = -1e30
EPS = 1e-05
ROOT_HALF = 0.7071067811865476
INV_ROOT_TWO_PI = 0.3989422804014327
SCALE = HEAD ** (-0.5)
F32 = jnp.float32
BF16 = jnp.bfloat16
VM = pl.BlockSpec(memory_space=pltpu.VMEM)
SM = pl.BlockSpec(memory_space=pltpu.SMEM)
ANY = pl.BlockSpec(memory_space=pl.ANY)
LIMIT = 62 << 20
QR, QC = 48, 384
NN = (((1,), (0,)), ((), ()))
NT = (((1,), (1,)), ((), ()))
TN = (((0,), (0,)), ((), ()))


def dot(a, b, dims):
    return lax.dot_general(a, b, dims, preferred_element_type=F32)


def norm_forward(resid):
    cent = resid - jnp.mean(resid, axis=-1, keepdims=True)
    inv = lax.rsqrt(jnp.mean(cent * cent, axis=-1, keepdims=True) + EPS)
    return cent * inv, inv


def norm_backward(scaled, normed, inv):
    inner = jnp.mean(scaled * normed, axis=-1, keepdims=True)
    return inv * (scaled - jnp.mean(scaled, axis=-1, keepdims=True) - normed * inner)


def gelu_pair(pre):
    half_cdf = 0.5 * (1.0 + lax.erf(pre * ROOT_HALF))
    slope = half_cdf + pre * jnp.exp(-0.5 * pre * pre) * INV_ROOT_TWO_PI
    return pre * half_cdf, slope


def col_sum(arr):
    return jnp.sum(arr.astype(F32), axis=0, keepdims=True)


def softmax_rows(scores):
    expo = jnp.exp(scores - jnp.max(scores, axis=-1, keepdims=True))
    return expo / jnp.sum(expo, axis=-1, keepdims=True)


def lane_halves(rows):
    lane = lax.broadcasted_iota(jnp.int32, (rows, 128), 1)
    return lane < HEAD


def two_heads(slab):
    low = lane_halves(slab.shape[0])
    zero = jnp.zeros_like(slab)
    return jnp.concatenate([jnp.where(low, slab, zero), jnp.where(low, zero, slab)], axis=0)


def fetch(pairs, sem):
    copies = [pltpu.make_async_copy(src, dst, sem.at[i]) for i, (src, dst) in enumerate(pairs)]
    for copy in copies:
        copy.start()
    return copies


def xor_bit(a, b):
    return a + b - 2 * a * b


FFN_ORDERS = ("xyab", "yxab", "xyab", "abxy", "yxab", "xyab", "yxab", "abyx")
ATT_ORDERS = ("xyab", "yxab", "abxy", "xyab", "yxab", "xyab", "yxab", "abyx", "xyab", "yxab", "xyab", "yxab")


def relative(b, d, me, doc):
    return {
        "c": xor_bit(lax.rem(me, 2), b % 2),
        "x": xor_bit(lax.rem(doc, 2), d % 2),
        "y": xor_bit(doc // 2, d // 2),
        "a": xor_bit(lax.rem(me // 2, 2), (b // 2) % 2),
        "b": xor_bit(me // 4, b // 4),
    }


def slot_of(order, bits):
    return sum(bits[name] * (16 >> i) for i, name in enumerate("c" + order))


def first_rows(rows, width):
    return lax.rem(lax.broadcasted_iota(jnp.int32, (rows, width), 0), SEG) == 0


def put_bias_sums(pack_v, dpre):
    for b in range(8):
        for i in range(4):
            at = b * 384 + i * 96
            pack_v[b, 8 + i : 9 + i, 0:96] = col_sum(dpre[:, at : at + 96])


def put_sums(pack_v, sums):
    for b in range(8):
        for i, value in sums.items():
            pack_v[b, i : i + 1, 0:96] = value[:, b * 96 : (b + 1) * 96]


def segment_forward(
    stride,
    tok, mask, w_qkv, w_out, w_up, w_down, vec, fbias, cot,
    o_qkv, o_probs, o_ctx, o_n1, o_inv1, o_dh1, o_first, o_parts, heads, rows_zero, pack_v,
    b_qkv, b_out, b_up, b_down, qkv, probs, ctx, n1, inv1, h1, act, slope, dffn, dpre, dh1, first_low, parts,
    sem, out_sem,
):
    rows, width = tok.shape
    groups = rows // SEG
    hidden = act.shape[1]
    me = lax.axis_index("seg") // stride
    doc_index = lax.axis_index("doc")
    copies = fetch(
        [(w_qkv.at[0], b_qkv), (w_out.at[0], b_out), (w_up.at[0], b_up), (w_down.at[0], b_down)], sem
    )
    leaving = []

    def leave(src, dst):
        copy = pltpu.make_async_copy(src, dst, out_sem.at[len(leaving)])
        copy.start()
        leaving.append(copy)

    copies[0].wait()
    for part in range(3):
        cols = slice(part * width, (part + 1) * width)
        out = dot(tok[...], b_qkv[:, cols], NN)
        if part != 1:
            out = out + vec[0, part // 2 : part // 2 + 1, :]
        qkv[:, cols] = out.astype(BF16)
    leave(qkv, o_qkv)
    for g in range(groups):
        here = slice(g * SEG, (g + 1) * SEG)
        keep = mask[g : g + 1, :] > 0
        for pair in range(width // 128):
            at = pair * 128
            query = two_heads(qkv[here, at : at + 128])
            scores = dot(query, qkv[here, width + at : width + at + 128], NT) * SCALE
            prob = softmax_rows(jnp.where(keep, scores, NEG))
            probs[g * (width // 128) + pair] = prob
            low = prob.astype(BF16)
            side = jnp.concatenate([low[:SEG], low[SEG:]], axis=1)
            value = two_heads(qkv[here, 2 * width + at : 2 * width + at + 128])
            ctx[here, at : at + 128] = dot(side, value, NN).astype(BF16)
    leave(probs, o_probs)
    leave(ctx, o_ctx)
    copies[1].wait()
    resid = tok[...].astype(F32) + (dot(ctx[...], b_out[...], NN) + vec[0, 2:3, :])
    normed, inv = norm_forward(resid)
    n1[...] = normed
    inv1[...] = jnp.broadcast_to(inv, inv1.shape)
    leave(n1, o_n1)
    leave(inv1, o_inv1)
    h1[...] = (normed * vec[0, 3:4, :] + vec[0, 4:5, :]).astype(BF16)
    copies[2].wait()
    for part in range(hidden // width):
        cols = slice(part * width, (part + 1) * width)
        value, grad = gelu_pair(dot(h1[...], b_up[:, cols], NN) + fbias[0:1, cols])
        act[:, cols] = value.astype(BF16)
        slope[:, cols] = grad.astype(BF16)
    copies[3].wait()
    first = n1[...] * vec[0, 3:4, :] + vec[0, 4:5, :]
    normed, inv = norm_forward(first + (dot(act[...], b_down[...], NN) + vec[0, 5:6, :]))
    final = (normed * vec[0, 6:7, :] + vec[0, 7:8, :]).astype(BF16)
    first_low[...] = final
    leave(first_low, o_first)
    heads[...] = jnp.zeros_like(heads)
    rows_zero[...] = jnp.zeros_like(rows_zero)
    tops = []
    for g in range(groups):
        at = g * SEG
        tops.append(first_low[at : at + 16, :].astype(F32)[0:1])
        rows_zero[g : g + 1, :] = h1[at : at + 16, :].astype(F32)[0:1]
        rows_zero[groups + g : groups + g + 1, :] = normed[at : at + 1]
        rows_zero[2 * groups + g : 2 * groups + g + 1, :] = jnp.broadcast_to(inv[at : at + 1], (1, width))
    for g in range(groups):
        tops.append(cot[g * SEG : g * SEG + 16, :].astype(F32)[0:1])
    heads[...] = jnp.concatenate(tops + [jnp.zeros((8 - 2 * groups, width), F32)], axis=0).astype(BF16)
    grad = jnp.where(first_rows(rows, width), 0.0, cot[...].astype(F32))
    sums = {6: col_sum(grad * normed), 7: col_sum(grad)}
    dr2 = norm_backward(grad * vec[0, 6:7, :], normed, inv)
    dffn[...] = dr2.astype(BF16)
    dh1[...] = dr2
    sums[5] = col_sum(dffn[...])
    pack_v[...] = jnp.zeros_like(pack_v)
    put_sums(pack_v, sums)

    def place(chunk, b, d, value):
        slot = slot_of(FFN_ORDERS[chunk], relative(b, d, me, doc_index))
        parts[chunk, slot] = value.astype(BF16)

    for b in range(8):
        tile = dot(dffn[...], act[:, b * QC : (b + 1) * QC], TN)
        for d in range(4):
            for j in range(4):
                at = d * 192 + j * QR
                place(j, b, d, tile[at : at + QR])
    leave(parts.at[0:4], o_parts.at[0:4])
    for part in range(hidden // width):
        cols = slice(part * width, (part + 1) * width)
        dpre[:, cols] = (dot(dffn[...], b_down[cols, :], NT) * slope[:, cols].astype(F32)).astype(BF16)
    for d in range(4):
        for half in range(2):
            at = d * 768 + half * QC
            tile = dot(h1[...], dpre[:, at : at + QC], TN)
            for b in range(8):
                for top_half in range(2):
                    r = b * 96 + top_half * QR
                    place(4 + 2 * top_half + half, b, d, tile[r : r + QR])
    leave(parts.at[4:8], o_parts.at[4:8])
    put_bias_sums(pack_v, dpre)
    dh1[...] = dh1[...] + dot(dpre[...], b_up[...], NT)
    leave(dh1, o_dh1)
    for copy in leaving:
        copy.wait()


def run_segment_forward(stride, tok, mask, w_qkv, w_out, w_up, w_down, vec, fbias, cot):
    rows, width = tok.shape
    hidden = w_up.shape[2]
    groups = rows // SEG
    shape = jax.ShapeDtypeStruct
    kept = [
        ((rows, 3 * width), BF16),
        ((groups * width // 128, 2 * SEG, SEG), F32),
        ((rows, width), BF16),
        ((rows, width), F32),
        ((rows, 128), F32),
    ]
    extra = [
        ((rows, width), BF16),
        ((rows, hidden), BF16),
        ((rows, hidden), BF16),
        ((rows, width), BF16),
        ((rows, hidden), BF16),
    ]
    last = [((rows, width), F32), ((rows, width), BF16), ((8, 32, QR, QC), BF16)]
    return pl.pallas_call(
        functools.partial(segment_forward, stride),
        out_shape=tuple(shape(*s) for s in kept + last)
        + (shape((8, width), BF16), shape((8, width), F32), shape((8, 16, 128), F32)),
        in_specs=[VM, VM, ANY, ANY, ANY, ANY, VM, VM, VM],
        out_specs=(ANY,) * 8 + (VM,) * 3,
        scratch_shapes=[pltpu.VMEM(w.shape[1:], BF16) for w in (w_qkv, w_out, w_up, w_down)]
        + [pltpu.VMEM(*s) for s in kept + extra + last]
        + [pltpu.SemaphoreType.DMA((4,)), pltpu.SemaphoreType.DMA((9,))],
        compiler_params=pltpu.CompilerParams(vmem_limit_bytes=LIMIT),
        name="segment_forward",
    )(tok, mask, w_qkv, w_out, w_up, w_down, vec, fbias, cot)


def head_rows(arr, heads):
    rows, width = arr.shape
    lane = lax.broadcasted_iota(jnp.int32, (rows, width), 1)
    zero = jnp.zeros_like(arr)
    parts = [jnp.where(lane // HEAD == h, arr, zero) for h in range(heads)]
    return jnp.concatenate(parts, axis=0)


def head_join(arr, heads):
    rows = arr.shape[0] // heads
    lane = lax.broadcasted_iota(jnp.int32, (rows, arr.shape[1]), 1)
    out = jnp.zeros((rows, arr.shape[1]), F32)
    for h in range(heads):
        out = jnp.where(lane // HEAD == h, arr[h * rows : (h + 1) * rows], out)
    return out


class Halving:
    def __init__(self, orders, kept, got, shares, partners, send_sem, recv_sem, staged=None):
        self.orders, self.kept, self.got, self.shares, self.staged = orders, kept, got, shares, staged
        self.partners, self.send_sem, self.recv_sem = partners, send_sem, recv_sem
        self.sends = {}
        self.loads = []

    def send(self, stage, chunk, src):
        copy = pltpu.make_async_remote_copy(
            src_ref=src,
            dst_ref=self.got[stage].at[chunk],
            send_sem=self.send_sem.at[stage, chunk],
            recv_sem=self.recv_sem.at[stage, chunk],
            device_id=self.partners[("c" + self.orders[chunk])[stage]],
            device_id_type=MESH,
        )
        copy.start()
        self.sends[stage, chunk] = copy

    def load(self, chunk, source, sem):
        copy = pltpu.make_async_copy(source.at[chunk, pl.ds(0, 16)], self.staged.at[chunk % 2], sem.at[chunk])
        copy.start()
        self.loads.append(copy)

    def add(self, stage, chunk, first, last):
        kept = self.kept
        more = self.got[stage].at[chunk]
        if stage == 0 and self.staged is not None:
            more = self.staged.at[chunk % 2]

        def body(i, carry):
            kept[chunk, i] = (kept[chunk, i].astype(F32) + more[i].astype(F32)).astype(BF16)
            return carry

        lax.fori_loop(first, last, body, 0, unroll=min(4, last - first))

    def step(self, stage, chunk):
        if stage == 0 and self.staged is not None:
            self.loads[chunk].wait()
        self.sends[stage, chunk].wait_recv()
        half = (16 >> stage) // 2
        if stage < 4:
            self.add(stage, chunk, half, 2 * half)
            self.send(stage + 1, chunk, self.kept.at[chunk, pl.ds(half, half)])
            self.add(stage, chunk, 0, half)
        else:
            self.shares[chunk] = self.kept[chunk, 0].astype(F32) + self.got[4][chunk, 0].astype(F32)

    def finish(self):
        for copy in self.sends.values():
            copy.wait_send()


def the_rest(
    stride, count,
    counts, heads, rows_zero, tok, pack_v, pos, vec, fbias,
    i_parts, i_qkv, i_probs, i_ctx, i_n1, i_inv1, i_dh1, i_first, w_qkv, w_out, w_up, w_down,
    output, grad_tok, ffn_shares, att_shares, rows_x, rows_y, vec_all, vec_sum,
    b_qkv, b_out, b_up, b_down, qkv, probs, ctx, n1, inv1, dh1,
    every, every_zero, c_qkv, c_in, c_cot, c_act, c_slope, c_dpre, mixed, zeros, z_inv,
    pack_x, pack_y, pack_c, pack_p, y_qkv, y_out, dqkv, dctx, vec_got, vec_one,
    f_staged, f_got0, f_got1, f_got2, f_got3, f_got4, a_parts, a_got0, a_got1, a_got2, a_got3, a_got4,
    w_sem, in_sem, load_sem, h_send, h_recv, z_send, z_recv, f_send, f_recv, a_send, a_recv,
    x_send, x_recv, v_send, v_recv, s_send, s_recv, local_sem,
):
    rows, width = tok.shape
    groups = rows // SEG
    hidden = c_act.shape[1]
    docs = groups
    segs = count
    c_rows = docs * segs
    heads_n = width // HEAD
    seg = lax.axis_index("seg")
    doc = lax.axis_index("doc")
    me = seg // stride
    rest = lax.rem(seg, stride)
    core = lax.rem(me, 2)
    z = me // 2
    near = z + 1 - 2 * lax.rem(z, 2)
    far = lax.rem(z + 2, 4)
    partners = {
        "c": (doc, (me + 1 - 2 * core) * stride + rest),
        "x": (doc + 1 - 2 * lax.rem(doc, 2), seg),
        "y": (lax.rem(doc + 2, 4), seg),
        "a": (doc, (near * 2 + core) * stride + rest),
        "b": (doc, (far * 2 + core) * stride + rest),
    }
    weights = fetch(
        [(w_qkv.at[1], b_qkv), (w_out.at[1], b_out), (w_up.at[1], b_up), (w_down.at[1], b_down)], w_sem
    )
    barrier = pltpu.get_barrier_semaphore()

    def seg_peer(step):
        return (doc, lax.rem(seg + step, count))

    def doc_peer(step):
        return (lax.rem(doc + step, 4), seg)

    def greet(step, carry):
        pl.semaphore_signal(barrier, inc=1, device_id=seg_peer(step), device_id_type=MESH)
        return carry

    lax.fori_loop(1, count, greet, 0)
    for step in range(1, 4):
        pl.semaphore_signal(barrier, inc=1, device_id=doc_peer(step), device_id_type=MESH)
    pl.semaphore_wait(barrier, count + 2)

    def spread(src, dst, send_sem, recv_sem):
        def copy(step):
            return pltpu.make_async_remote_copy(
                src_ref=src,
                dst_ref=dst.at[seg],
                send_sem=send_sem.at[step],
                recv_sem=recv_sem.at[step],
                device_id=seg_peer(step),
                device_id_type=MESH,
            )

        def begin(step, carry):
            copy(step).start()
            return carry

        def end(step, carry):
            copy(step).wait()
            return carry

        lax.fori_loop(1, count, begin, 0)
        return lambda: lax.fori_loop(1, count, end, 0)

    end_heads = spread(heads, every, h_send, h_recv)
    local = fetch([(heads, every.at[seg]), (rows_zero, every_zero.at[seg])], local_sem)
    ffn = Halving(
        FFN_ORDERS, f_got0, [f_got0, f_got1, f_got2, f_got3, f_got4], ffn_shares, partners, f_send, f_recv, f_staged
    )
    att = Halving(
        ATT_ORDERS, a_parts, [a_got0, a_got1, a_got2, a_got3, a_got4], att_shares, partners, a_send, a_recv
    )
    for chunk in range(8):
        ffn.send(0, chunk, i_parts.at[chunk, pl.ds(16, 16)])
    for chunk in range(2):
        ffn.load(chunk, i_parts, load_sem)
    end_zero = spread(rows_zero, every_zero, z_send, z_recv)
    inputs = fetch(
        [(i_dh1, dh1), (i_n1, n1), (i_inv1, inv1), (i_first, output), (i_ctx, ctx), (i_qkv, qkv), (i_probs, probs)],
        in_sem,
    )
    late = [0, 1, 3, 2, 4, 7, 5, 6]
    todo = [(0, c) for c in range(8)] + [(s, c) for s in (1, 2, 3, 4) for c in late]

    def pump(n):
        for _ in range(min(n, len(todo))):
            stage, chunk = todo.pop(0)
            ffn.step(stage, chunk)
            if stage == 0 and chunk + 2 < 8:
                ffn.load(chunk + 2, i_parts, load_sem)

    for copy in local:
        copy.wait()
    end_heads()
    for s in range(segs):
        row = every[s].astype(F32)
        for d in range(docs):
            r = d * segs + s
            c_in[r : r + 1, :] = row[d : d + 1] + pos[s : s + 1, :]
            c_cot[r : r + 1, :] = row[docs + d : docs + d + 1]
    base = c_in[...]
    base_low = base.astype(BF16)
    weights[0].wait()
    for part in range(3):
        cols = slice(part * width, (part + 1) * width)
        out = dot(base_low, b_qkv[:, cols], NN)
        if part != 1:
            out = out + vec[1, part // 2 : part // 2 + 1, :]
        c_qkv[:, cols] = out.astype(BF16)
    pump(PUMPS[0])
    blocks = [(0, c_rows)] if c_rows <= 16 else [(d * segs, segs) for d in range(docs)]
    context = []
    attention = []
    for at, n in blocks:
        here = slice(at, at + n)
        query = head_rows(c_qkv[here, 0:width], heads_n)
        row_doc = (at + lax.rem(lax.broadcasted_iota(jnp.int32, (heads_n * n, n), 0), n)) // segs
        key = at + lax.broadcasted_iota(jnp.int32, (heads_n * n, n), 1)
        limit = jnp.zeros((heads_n * n, n), jnp.int32)
        for d in range(docs):
            limit = jnp.where(key // segs == d, counts[d], limit)
        keep = jnp.logical_and(row_doc == key // segs, lax.rem(key, segs) * SEG < limit)
        scores = dot(query, c_qkv[here, width : 2 * width], NT) * SCALE
        prob = softmax_rows(jnp.where(keep, scores, NEG))
        prob_low = prob.astype(BF16)
        context.append(head_join(dot(prob_low, c_qkv[here, 2 * width : 3 * width], NN), heads_n).astype(BF16))
        attention.append((query, prob, prob_low))
    context = context[0] if len(context) == 1 else jnp.concatenate(context, axis=0)
    weights[1].wait()
    c_n1, c_inv1 = norm_forward(base + (dot(context, b_out[...], NN) + vec[1, 2:3, :]))
    c_first = c_n1 * vec[1, 3:4, :] + vec[1, 4:5, :]
    c_low = c_first.astype(BF16)
    pump(PUMPS[1])
    weights[2].wait()
    for part in range(hidden // width):
        cols = slice(part * width, (part + 1) * width)
        value, grad = gelu_pair(dot(c_low, b_up[:, cols], NN) + fbias[1:2, cols])
        c_act[:, cols] = value.astype(BF16)
        c_slope[:, cols] = grad.astype(c_slope.dtype)
    pump(PUMPS[2])
    weights[3].wait()
    c_n2, c_inv2 = norm_forward(c_first + (dot(c_act[...], b_down[...], NN) + vec[1, 5:6, :]))
    mixed[...] = c_n2 * vec[1, 6:7, :] + vec[1, 7:8, :]
    pump(PUMPS[3])
    g = c_cot[...]
    sums = {6: col_sum(g * c_n2), 7: col_sum(g)}
    dr2 = norm_backward(g * vec[1, 6:7, :], c_n2, c_inv2)
    dffn = dr2.astype(BF16)
    for part in range(hidden // width):
        cols = slice(part * width, (part + 1) * width)
        c_dpre[:, cols] = (dot(dffn, b_down[cols, :], NT) * c_slope[:, cols].astype(F32)).astype(BF16)
    again = [pltpu.make_async_copy(w_down.at[0], b_down, w_sem.at[3])]
    again[0].start()
    pump(PUMPS[4])
    c_grad = dr2 + dot(c_dpre[...], b_up[...], NT)
    again.append(pltpu.make_async_copy(w_up.at[0], b_up, w_sem.at[2]))
    again[1].start()
    pump(PUMPS[5])
    sums[3] = col_sum(c_grad * c_n1)
    sums[4] = col_sum(c_grad)
    sums[5] = col_sum(dffn)
    dr1 = norm_backward(c_grad * vec[1, 3:4, :], c_n1, c_inv1)
    dattn = dr1.astype(BF16)
    d_context = dot(dattn, b_out[...], NT).astype(BF16)
    again.append(pltpu.make_async_copy(w_out.at[0], b_out, w_sem.at[1]))
    again[2].start()
    d_parts = []
    for (at, n), (query, prob, prob_low) in zip(blocks, attention):
        here = slice(at, at + n)
        down = head_rows(d_context[here], heads_n)
        dp = dot(down, c_qkv[here, 2 * width : 3 * width], NT)
        ds = (prob * (dp - jnp.sum(prob * dp, axis=-1, keepdims=True))).astype(BF16)
        dv = dot(prob_low, down, TN).astype(BF16)
        dq = (head_join(dot(ds, c_qkv[here, width : 2 * width], NN), heads_n) * SCALE).astype(BF16)
        dk = (dot(ds, query, TN) * SCALE).astype(BF16)
        d_parts.append(jnp.concatenate([dq, dk, dv], axis=1))
    c_dqkv = d_parts[0] if len(d_parts) == 1 else jnp.concatenate(d_parts, axis=0)
    sums[0] = col_sum(c_dqkv[:, 0:width])
    sums[1] = col_sum(c_dqkv[:, 2 * width : 3 * width])
    sums[2] = col_sum(dattn)
    pump(PUMPS[6])
    dh = dr1 + dot(c_dqkv, b_qkv[...], NT)
    again.append(pltpu.make_async_copy(w_qkv.at[0], b_qkv, w_sem.at[0]))
    again[3].start()
    pump(PUMPS[7])
    end_zero()
    for s in range(segs):
        for d in range(docs):
            r = d * segs + s
            for i in range(2):
                zeros[i, r : r + 1, :] = every_zero[s, i * docs + d : i * docs + d + 1, :]
            z_inv[r : r + 1, :] = every_zero[s, 2 * docs + d : 2 * docs + d + 1, 0:128]
    z_n2, z_inv2 = zeros[1], z_inv[:, 0:1]
    z_sums = {6: col_sum(dh * z_n2), 7: col_sum(dh)}
    z_dr2 = norm_backward(dh * vec[0, 6:7, :], z_n2, z_inv2)
    z_dffn = z_dr2.astype(BF16)
    z_sums[5] = col_sum(z_dffn)
    z_low = zeros[0].astype(BF16)
    pack_x[...] = jnp.zeros_like(pack_x)
    pack_y[...] = jnp.zeros_like(pack_y)
    pack_c[...] = jnp.zeros_like(pack_c)
    total = dh[0:segs]
    for d in range(1, docs):
        total = total + dh[d * segs : (d + 1) * segs]
    for b in range(8):
        cols = slice(b * 96, (b + 1) * 96)
        pack_x[b, :, 0:96] = base_low[:, cols]
        pack_x[b, :, 128:224] = context[:, cols]
        pack_x[b, :, 256:352] = c_low[:, cols]
        pack_x[b, :, 384:768] = c_act[:, b * 384 : (b + 1) * 384]
        pack_x[b, :, 768:864] = z_low[:, cols]
        pack_p[b] = jnp.zeros_like(pack_p[b])
        pack_p[b, :, 0:96] = total[:, cols]
    put_sums(pack_c.at[:, 0:16], sums)
    put_bias_sums(pack_c.at[:, 0:16], c_dpre)
    for b in range(4):
        pack_y[b, :, 0:576] = c_dqkv[:, b * 576 : (b + 1) * 576]
        pack_y[b, :, 640:832] = dattn[:, b * 192 : (b + 1) * 192]
        pack_y[b, :, 896:1664] = c_dpre[:, b * 768 : (b + 1) * 768]
        pack_y[b, :, 1664:1856] = dffn[:, b * 192 : (b + 1) * 192]
        pack_y[b, :, 2688:2880] = z_dffn[:, b * 192 : (b + 1) * 192]
    pump(PUMPS[8])
    again[1].wait()
    for part in range(hidden // width):
        cols = slice(part * width, (part + 1) * width)
        value, grad = gelu_pair(dot(z_low, b_up[:, cols], NN) + fbias[0:1, cols])
        c_act[:, cols] = value.astype(BF16)
        c_slope[:, cols] = grad.astype(c_slope.dtype)
    for b in range(8):
        pack_x[b, :, 896:1280] = c_act[:, b * 384 : (b + 1) * 384]
    pump(PUMPS[9])
    again[0].wait()
    for part in range(hidden // width):
        cols = slice(part * width, (part + 1) * width)
        c_dpre[:, cols] = (dot(z_dffn, b_down[cols, :], NT) * c_slope[:, cols].astype(F32)).astype(BF16)
        pack_y[part, :, 1920:2688] = c_dpre[:, cols]
    put_sums(pack_c.at[:, 16:32], z_sums)
    put_bias_sums(pack_c.at[:, 16:32], c_dpre)
    pump(PUMPS[10])
    c_in[...] = z_dr2 + dot(c_dpre[...], b_up[...], NT)
    pump(PUMPS[11])
    exchange = []
    local = fetch([(pack_x.at[me], rows_x.at[doc]), (pack_y.at[doc], rows_y.at[doc])], local_sem)
    for step in range(1, 4):
        there = doc_peer(step)
        pair = [(pack_x.at[me], rows_x.at[doc]), (pack_y.at[there[0]], rows_y.at[doc])]
        for i, (src, dst) in enumerate(pair):
            copy = pltpu.make_async_remote_copy(
                src_ref=src,
                dst_ref=dst,
                send_sem=x_send.at[step, i],
                recv_sem=x_recv.at[step, i],
                device_id=there,
                device_id_type=MESH,
            )
            copy.start()
            exchange.append(copy)
    for copy in inputs:
        copy.wait()
    top = lax.broadcasted_iota(jnp.int32, (SEG, width), 0) == 0
    top_low = lax.broadcasted_iota(jnp.int32, (16, width), 0) == 0
    grads = []
    for g in range(groups):
        here = slice(g * SEG, (g + 1) * SEG)
        own = pl.ds(g * segs + seg, 1)
        tile = slice(g * SEG, g * SEG + 16)
        output[tile, :] = jnp.where(top_low, mixed[own, :], output[tile, :].astype(F32)).astype(BF16)
        grads.append(jnp.where(top, c_in[own, :], dh1[here, :]))
    grad = jnp.concatenate(grads, axis=0)
    normed = n1[...]
    sums = {3: col_sum(grad * normed), 4: col_sum(grad)}
    dr1 = norm_backward(grad * vec[0, 3:4, :], normed, inv1[:, 0:1])
    dattn = dr1.astype(BF16)
    sums[2] = col_sum(dattn)
    grad_tok[...] = dr1
    y_qkv[...] = jnp.zeros_like(y_qkv)
    low = lane_halves(rows)
    for d in range(4):
        slab = 3 * (d // 2) + 1
        mid = pltpu.roll(dr1[:, slab * 128 : (slab + 1) * 128], HEAD, 1).astype(BF16)
        whole = 3 * (d // 2) + 2 * (d % 2)
        fill = jnp.zeros_like(mid)
        y_out[d, :, 0:128] = jnp.where(low, fill, mid) if d % 2 == 0 else jnp.where(low, mid, fill)
        y_out[d, :, 128:256] = dattn[:, whole * 128 : (whole + 1) * 128]
    again[2].wait()
    dctx[...] = dot(dattn, b_out[...], NT).astype(BF16)
    pump(PUMPS[12])
    pairs = width // 128
    half = lane_halves(SEG)
    for g in range(groups):
        here = slice(g * SEG, (g + 1) * SEG)
        for pair in range(pairs):
            at = pair * 128
            prob = probs[g * pairs + pair]
            down = two_heads(dctx[here, at : at + 128])
            query = two_heads(qkv[here, at : at + 128])
            key = two_heads(qkv[here, width + at : width + at + 128])
            dp = dot(down, qkv[here, 2 * width + at : 2 * width + at + 128], NT)
            dv = dot(prob.astype(BF16), down, TN)
            ds = (prob * (dp - jnp.sum(prob * dp, axis=-1, keepdims=True))).astype(BF16)
            dq = dot(jnp.concatenate([ds[:SEG], ds[SEG:]], axis=1), key, NN) * SCALE
            dk = dot(ds, query, TN) * SCALE
            for kind, value in enumerate((dq, dk, dv)):
                value = value.astype(BF16)
                dqkv[here, kind * width + at : kind * width + at + 128] = value
                slab = kind * pairs + pair
                d, tile = slab // 9 * 2, slab % 9
                if tile < 4:
                    y_qkv[d, here, tile * 128 : (tile + 1) * 128] = value
                elif tile > 4:
                    y_qkv[d + 1, here, (tile - 5) * 128 : (tile - 4) * 128] = value
                else:
                    zero = jnp.zeros_like(value)
                    y_qkv[d, here, 512:640] = jnp.where(half, value, zero)
                    y_qkv[d + 1, here, 512:640] = jnp.where(half, zero, value)
        pump(PUMPS[13 + g])
    for side in range(2):
        for d in range(4):
            if side == 0:
                tile = dot(tok[...], y_qkv[d, :, 0:QC], TN)
            else:
                tile = dot(tok[...], y_qkv[d, :, QC:640], TN)
                more = dot(ctx[...], y_out[d], TN)
                tile = jnp.concatenate(
                    [tile[:, 0:128], tile[:, 128:256] + more[:, 0:128], more[:, 128:256]], axis=1
                )
            for b in range(8):
                for strip in range(6):
                    chunk = 6 * side + strip
                    slot = slot_of(ATT_ORDERS[chunk], relative(b, d, me, doc))
                    r = b * 96 + strip * 16
                    a_parts[chunk, slot] = tile[r : r + 16].astype(BF16)
        for strip in range(6):
            chunk = 6 * side + strip
            att.send(0, chunk, a_parts.at[chunk, pl.ds(16, 16)])
        pump(PUMPS[15 + side])
    sums[0] = col_sum(dqkv[:, 0:width])
    sums[1] = col_sum(dqkv[:, 2 * width : 3 * width])
    put_sums(pack_v, sums)

    def vec_copy(step):
        there = seg_peer(step)
        return pltpu.make_async_remote_copy(
            src_ref=pack_v.at[there[1] // stride],
            dst_ref=vec_got.at[seg],
            send_sem=v_send.at[step],
            recv_sem=v_recv.at[step],
            device_id=there,
            device_id_type=MESH,
        )

    def vec_begin(step, carry):
        vec_copy(step).start()
        return carry

    def vec_finish(step, carry):
        vec_copy(step).wait()
        return carry

    lax.fori_loop(1, count, vec_begin, 0)
    own_vec = pltpu.make_async_copy(pack_v.at[me], vec_got.at[seg], local_sem.at[2])
    own_vec.start()
    for chunk in range(12):
        att.step(0, chunk)
    again[3].wait()
    grad_tok[...] = grad_tok[...] + dot(dqkv[...], b_qkv[...], NT)
    own_vec.wait()
    lax.fori_loop(1, count, vec_finish, 0)
    vec_one[0:16, :] = lax.fori_loop(
        0, count, lambda i, total: total + vec_got[i], pack_c[me, 16:32, :]
    )
    vec_one[16:32, :] = pack_c[me, 0:16, :]
    vec_one[32:, :] = pack_p[me]
    own_vec = pltpu.make_async_copy(vec_one, vec_all.at[doc], local_sem.at[3])
    own_vec.start()
    for step in range(1, 4):
        copy = pltpu.make_async_remote_copy(
            src_ref=vec_one,
            dst_ref=vec_all.at[doc],
            send_sem=s_send.at[step],
            recv_sem=s_recv.at[step],
            device_id=doc_peer(step),
            device_id_type=MESH,
        )
        copy.start()
        exchange.append(copy)
    pump(8 * 5)
    for stage in range(1, 5):
        for chunk in (2, 7, 0, 1, 3, 4, 5, 6, 8, 9, 10, 11):
            att.step(stage, chunk)
    for copy in exchange + local:
        copy.wait()
    own_vec.wait()
    vec_sum[...] = vec_all[0] + vec_all[1] + vec_all[2] + vec_all[3]
    ffn.finish()
    att.finish()


PUMPS = (2, 2, 1, 1, 2, 1, 1, 1, 0, 1, 1, 1, 1, 2, 2, 3, 3)


def run_the_rest(stride, count, counts, heads, rows_zero, tok, pack_v, pos, vec, fbias, parts, saved, weights):
    rows, width = tok.shape
    groups = rows // SEG
    hidden = weights[2].shape[2]
    c_rows = groups * count
    tall = 32 + count
    shape = jax.ShapeDtypeStruct
    dma = pltpu.SemaphoreType.DMA
    wide = 1280, 2944
    return pl.pallas_call(
        functools.partial(the_rest, stride, count),
        out_shape=(
            shape((rows, width), BF16),
            shape((rows, width), F32),
            shape((8, QR, QC), F32),
            shape((12, 16, QC), F32),
            shape((4, c_rows, wide[0]), BF16),
            shape((4, c_rows, wide[1]), BF16),
            shape((4, tall, 128), F32),
            shape((tall, 128), F32),
        ),
        in_specs=[SM] + [VM] * 7 + [ANY] * 12,
        out_specs=(VM,) * 4 + (ANY,) * 2 + (VM,) * 2,
        scratch_shapes=[pltpu.VMEM(w.shape[1:], BF16) for w in weights]
        + [pltpu.VMEM(s.shape, s.dtype) for s in saved[:-1]]
        + [
            pltpu.VMEM((count, 8, width), BF16),
            pltpu.VMEM((count, 8, width), F32),
            pltpu.VMEM((c_rows, 3 * width), BF16),
            pltpu.VMEM((c_rows, width), F32),
            pltpu.VMEM((c_rows, width), F32),
            pltpu.VMEM((c_rows, hidden), BF16),
            pltpu.VMEM((c_rows, hidden), F32 if c_rows <= 16 else BF16),
            pltpu.VMEM((c_rows, hidden), BF16),
            pltpu.VMEM((c_rows, width), F32),
            pltpu.VMEM((2, c_rows, width), F32),
            pltpu.VMEM((c_rows, 128), F32),
            pltpu.VMEM((8, c_rows, wide[0]), BF16),
            pltpu.VMEM((4, c_rows, wide[1]), BF16),
            pltpu.VMEM((8, 32, 128), F32),
            pltpu.VMEM((8, count, 128), F32),
            pltpu.VMEM((4, rows, 640), BF16),
            pltpu.VMEM((4, rows, 256), BF16),
            pltpu.VMEM((rows, 3 * width), BF16),
            pltpu.VMEM((rows, width), BF16),
            pltpu.VMEM((count, 16, 128), F32),
            pltpu.VMEM((tall, 128), F32),
            pltpu.VMEM((2, 16, QR, QC), BF16),
        ]
        + [pltpu.VMEM((8, 16 >> i, QR, QC), BF16) for i in range(5)]
        + [pltpu.VMEM((12, 32, 16, QC), BF16)]
        + [pltpu.VMEM((12, 16 >> i, 16, QC), BF16) for i in range(5)]
        + [
            dma((4,)), dma((7,)), dma((8,)), dma((count,)), dma((count,)), dma((count,)), dma((count,)),
            dma((5, 8)), dma((5, 8)), dma((5, 12)), dma((5, 12)),
            dma((4, 2)), dma((4, 2)), dma((count,)), dma((count,)), dma((4,)), dma((4,)), dma((4,)),
        ],
        compiler_params=pltpu.CompilerParams(collective_id=0, has_side_effects=True, vmem_limit_bytes=LIMIT),
        name="the_rest",
    )(counts, heads, rows_zero, tok, pack_v, pos, vec, fbias, parts, *saved, *weights)


def assemble(ffn, att, rows_x, rows_y, sums, g_qkv, g_out, g_up, g_down, g_vec, g_bias):
    rows = rows_x.shape[0] * rows_x.shape[1]
    doc = lax.axis_index("doc")
    x = rows_x[...].reshape(rows, rows_x.shape[2])
    y = rows_y[...].reshape(rows, rows_y.shape[2])
    g_qkv[1] = dot(x[:, 0:128], y[:, 0:640], TN)[0:96, 0:576]
    g_out[1] = dot(x[:, 128:256], y[:, 640:896], TN)[0:96, 0:192]
    g_up[1] = dot(x[:, 256:384], y[:, 896:1664], TN)[0:96, :]
    g_down[1] = dot(x[:, 384:768], y[:, 1664:1920], TN)[:, 0:192]
    more = dot(x[:, 768:896], y[:, 1920:2688], TN)
    for r in range(2):
        at = slice(r * QR, (r + 1) * QR)
        for c in range(2):
            cols = slice(c * QC, (c + 1) * QC)
            g_up[0, at, cols] = ffn[4 + 2 * r + c] + more[at, cols]
    tall = jnp.concatenate([ffn[0], ffn[1], ffn[2], ffn[3]], axis=0)
    g_down[0] = jnp.transpose(tall) + dot(x[:, 896:1280], y[:, 2688:2944], TN)[:, 0:192]
    left = jnp.concatenate([att[i] for i in range(6)], axis=0)
    right = jnp.concatenate([att[6 + i] for i in range(6)], axis=0)
    mid, last = right[:, 128:256], right[:, 256:384]
    slabs = jnp.concatenate([left, right[:, 0:128]], axis=1)

    @pl.when(lax.rem(doc, 2) == 0)
    def _():
        g_qkv[0, :, 0:512] = slabs
        g_qkv[0, :, 512:576] = mid[:, 0:64]
        g_out[0, :, 0:128] = last
        g_out[0, :, 128:192] = mid[:, 64:128]

    @pl.when(lax.rem(doc, 2) == 1)
    def _():
        g_qkv[0] = jnp.concatenate([mid[:, 64:128], slabs], axis=1)
        g_out[0] = jnp.concatenate([mid[:, 0:64], last], axis=1)

    for layer in range(2):
        g_vec[layer] = sums[16 * layer : 16 * layer + 8, :]
        g_bias[layer] = sums[16 * layer + 8 : 16 * layer + 12, :]


def run_assemble(ffn, att, rows_x, rows_y, sums):
    shape = jax.ShapeDtypeStruct
    return pl.pallas_call(
        assemble,
        out_shape=(
            shape((2, 96, 576), F32),
            shape((2, 96, 192), F32),
            shape((2, 96, 768), F32),
            shape((2, 384, 192), F32),
            shape((2, 8, 128), F32),
            shape((2, 4, 128), F32),
        ),
        in_specs=[VM] * 5,
        out_specs=(VM,) * 6,
        compiler_params=pltpu.CompilerParams(vmem_limit_bytes=LIMIT),
        name="assemble",
    )(ffn, att, rows_x, rows_y, sums)


def shards(
    tokens,
    token_mask,
    doc_counts,
    w_qkv,
    w_out,
    w_up,
    w_down,
    vectors,
    ffn_bias,
    pos_embed,
    cotangent,
):
    docs, slots, width = tokens.shape
    seg_dev = slots // SEG
    groups = docs * seg_dev
    count = lax.axis_size("seg")
    stride = count // 8
    rest = lax.rem(lax.axis_index("seg"), stride)
    tok = tokens.reshape(groups * SEG, width)
    cot = cotangent.reshape(groups * SEG, width)
    weights = (w_qkv, w_out, w_up, w_down)
    *saved, parts, heads, rows_zero, pack_v = run_segment_forward(
        stride, tok, token_mask.reshape(groups, SEG), *weights, vectors, ffn_bias, cot
    )
    output, grad_tok, ffn, att, rows_x, rows_y, _, sums = run_the_rest(
        stride, count, doc_counts, heads, rows_zero, tok, pack_v, pos_embed, vectors, ffn_bias,
        parts, saved, weights,
    )
    g_qkv, g_out, g_up, g_down, g_vec, g_bias = run_assemble(ffn, att, rows_x, rows_y, sums)
    if stride > 1:
        lanes = [[i * stride + j for j in range(stride)] for i in range(8)]

        def own(arr, dim):
            low = lax.psum_scatter(arr[0:1], "seg", scatter_dimension=dim, axis_index_groups=lanes, tiled=True)
            size = arr.shape[dim] // stride
            return jnp.concatenate([low, lax.dynamic_slice_in_dim(arr[1:2], rest * size, size, dim)], axis=0)

        g_qkv, g_out, g_up, g_down = own(g_qkv, 1), own(g_out, 1), own(g_up, 1), own(g_down, 1)
    doc = lax.axis_index("doc")
    each = 96 // stride
    g_vec = lax.dynamic_slice(g_vec, (0, doc * 2, rest * each), (2, 2, each))
    g_bias = g_bias[:, :, 0:96].reshape(2, 384)
    g_bias = lax.dynamic_slice_in_dim(g_bias, rest * (384 // stride), 384 // stride, 1)
    g_pos = lax.dynamic_slice_in_dim(sums[32:], rest * each, each, 1)
    return (
        output.reshape(tokens.shape),
        grad_tok.reshape(tokens.shape),
        g_qkv,
        g_out,
        g_up,
        g_down,
        g_vec,
        g_bias,
        g_pos,
    )


def solution(mesh):
    return jax.shard_map(
        shards,
        mesh=mesh,
        in_specs=(
            P("doc", "seg", None),
            P("doc", "seg"),
            P("doc"),
            P(),
            P(),
            P(),
            P(),
            P(),
            P(),
            P(),
            P("doc", "seg", None),
        ),
        out_specs=(
            P("doc", "seg", None),
            P("doc", "seg", None),
            P(None, "seg", "doc"),
            P(None, "seg", "doc"),
            P(None, "seg", "doc"),
            P(None, "seg", "doc"),
            P(None, "doc", "seg"),
            P(None, "seg"),
            P(None, "seg"),
        ),
        check_vma=False,
    )
```

```python
import functools
from types import SimpleNamespace

import jax
import jax.numpy as jnp
from jax import lax
from jax.experimental import pallas as pl
from jax.experimental.pallas import tpu as pltpu
from jax.sharding import PartitionSpec as P

MESH = pl.DeviceIdType.MESH
HEAD = 64
SEG = 128
NEG = -1e30
EPS = 1e-05
ROOT_HALF = 0.7071067811865476
INV_ROOT_TWO_PI = 0.3989422804014327
SCALE = HEAD ** (-0.5)
F32 = jnp.float32
BF16 = jnp.bfloat16
VM = pl.BlockSpec(memory_space=pltpu.VMEM)
SM = pl.BlockSpec(memory_space=pltpu.SMEM)
ANY = pl.BlockSpec(memory_space=pl.ANY)
LIMIT = 62 << 20
QR, QC = 48, 384
NN = (((1,), (0,)), ((), ()))
NT = (((1,), (1,)), ((), ()))
TN = (((0,), (0,)), ((), ()))


def dot(a, b, dims):
    return lax.dot_general(a, b, dims, preferred_element_type=F32)


def norm_forward(resid):
    cent = resid - jnp.mean(resid, axis=-1, keepdims=True)
    inv = lax.rsqrt(jnp.mean(cent * cent, axis=-1, keepdims=True) + EPS)
    return cent * inv, inv


def norm_backward(scaled, normed, inv):
    inner = jnp.mean(scaled * normed, axis=-1, keepdims=True)
    return inv * (scaled - jnp.mean(scaled, axis=-1, keepdims=True) - normed * inner)


def gelu_pair(pre):
    half_cdf = 0.5 * (1.0 + lax.erf(pre * ROOT_HALF))
    slope = half_cdf + pre * jnp.exp(-0.5 * pre * pre) * INV_ROOT_TWO_PI
    return pre * half_cdf, slope


def col_sum(arr):
    return jnp.sum(arr.astype(F32), axis=0, keepdims=True)


def softmax_rows(scores):
    expo = jnp.exp(scores - jnp.max(scores, axis=-1, keepdims=True))
    return expo / jnp.sum(expo, axis=-1, keepdims=True)


def lane_halves(rows):
    lane = lax.broadcasted_iota(jnp.int32, (rows, 128), 1)
    return lane < HEAD


def two_heads(slab):
    low = lane_halves(slab.shape[0])
    zero = jnp.zeros_like(slab)
    return jnp.concatenate([jnp.where(low, slab, zero), jnp.where(low, zero, slab)], axis=0)


def fetch(pairs, sem):
    copies = [pltpu.make_async_copy(src, dst, sem.at[i]) for i, (src, dst) in enumerate(pairs)]
    for copy in copies:
        copy.start()
    return copies


def xor_bit(a, b):
    return a + b - 2 * a * b


FFN_ORDERS = (
    "xayb", "yabx", "abyx", "xyab", "yaxb", "xyab", "yabx", "xyab",
)
ATT_ORDERS = (
    "xyab", "yaxb", "abyx", "yaxb", "xayb", "xyab", "xyab", "xyab", "yxab", "xyab", "xyab", "xyab",
)


def relative(b, d, me, doc):
    return {
        "c": xor_bit(lax.rem(me, 2), b % 2),
        "x": xor_bit(lax.rem(doc, 2), d % 2),
        "y": xor_bit(doc // 2, d // 2),
        "a": xor_bit(lax.rem(me // 2, 2), (b // 2) % 2),
        "b": xor_bit(me // 4, b // 4),
    }


def slot_of(order, bits):
    return sum(bits[name] * (16 >> i) for i, name in enumerate("c" + order))


def first_rows(rows, width):
    return lax.rem(lax.broadcasted_iota(jnp.int32, (rows, width), 0), SEG) == 0


def put_bias_sums(pack_v, dpre):
    for b in range(8):
        for i in range(4):
            at = b * 384 + i * 96
            pack_v[b, 8 + i : 9 + i, 0:96] = col_sum(dpre[:, at : at + 96])


def put_sums(pack_v, sums):
    for b in range(8):
        for i, value in sums.items():
            pack_v[b, i : i + 1, 0:96] = value[:, b * 96 : (b + 1) * 96]


def head_rows(arr, heads):
    rows, width = arr.shape
    lane = lax.broadcasted_iota(jnp.int32, (rows, width), 1)
    zero = jnp.zeros_like(arr)
    parts = [jnp.where(lane // HEAD == h, arr, zero) for h in range(heads)]
    return jnp.concatenate(parts, axis=0)


def head_join(arr, heads):
    rows = arr.shape[0] // heads
    lane = lax.broadcasted_iota(jnp.int32, (rows, arr.shape[1]), 1)
    out = jnp.zeros((rows, arr.shape[1]), F32)
    for h in range(heads):
        out = jnp.where(lane // HEAD == h, arr[h * rows : (h + 1) * rows], out)
    return out


class Halving:
    def __init__(self, orders, kept, got, shares, partners, send_sem, recv_sem, staged=None):
        self.orders, self.kept, self.got, self.shares, self.staged = orders, kept, got, shares, staged
        self.partners, self.send_sem, self.recv_sem = partners, send_sem, recv_sem
        self.sends = {}
        self.loads = []

    def send(self, stage, chunk, src):
        copy = pltpu.make_async_remote_copy(
            src_ref=src,
            dst_ref=self.got[stage].at[chunk],
            send_sem=self.send_sem.at[stage, chunk],
            recv_sem=self.recv_sem.at[stage, chunk],
            device_id=self.partners[("c" + self.orders[chunk])[stage]],
            device_id_type=MESH,
        )
        copy.start()
        self.sends[stage, chunk] = copy

    def load(self, chunk, source, sem):
        copy = pltpu.make_async_copy(source.at[chunk, pl.ds(0, 16)], self.staged.at[chunk % 2], sem.at[chunk])
        copy.start()
        self.loads.append(copy)

    def add(self, stage, chunk, first, last):
        kept = self.kept
        more = self.got[stage].at[chunk]
        if stage == 0 and self.staged is not None:
            more = self.staged.at[chunk % 2]

        kept[chunk, first:last] = kept[chunk, first:last] + more[first:last]

    def step(self, stage, chunk):
        if stage == 0 and self.staged is not None:
            self.loads[chunk].wait()
        self.sends[stage, chunk].wait_recv()
        half = (16 >> stage) // 2
        if stage < 4:
            self.add(stage, chunk, half, 2 * half)
            self.send(stage + 1, chunk, self.kept.at[chunk, pl.ds(half, half)])
            self.add(stage, chunk, 0, half)
        else:
            self.shares[chunk] = self.kept[chunk, 0].astype(F32) + self.got[4][chunk, 0].astype(F32)

    def finish(self):
        for copy in self.sends.values():
            copy.wait_send()


STEPS = (
    0, 1, 2, 3, 4, 5, 6, 7, 100, 101, 102, 200, 103, 104, 201, 105, 106, 300, 202, 204, 301, 203, 107, 1000,
    206, 1001, 1002, 304, 1003, 1004, 1005, 401, 205, 400, 1006, 1007, 1008, 303, 1009, 1010, 302, 1011, 1100,
    306, 1104, 1102, 207, 404, 1105, 1101, 305, 403, 1106, 1204, 1103, 1107, 1202, 1108, 307, 1200, 1201, 1109,
    1205, 405, 1206, 1203, 1304, 1110, 1300, 402, 1207, 407, 1305, 1302, 1306, 1404, 1209, 1400, 1111, 1307,
    1210, 1405, 406, 1406, 1309, 1208, 1407, 1301, 1211, 1310, 1303, 1402, 1409, 1308, 1401, 1311, 1410, 1403,
    1408, 1411,
)
PUMPS = (
    0, 0, 0, 1, 1, 1, 2, 2, 1, 1, 1, 1, 0, 2, 1, 1, 0, 1, 1, 0, 3, 0, 0, 2, 2,
)
LATE = 16


def weight_copy(r, layer, i):
    src = (r.w_qkv, r.w_out, r.w_up, r.w_down)[i]
    dst = (r.b_qkv, r.b_out, r.b_up, r.b_down)[i]
    return pltpu.make_async_copy(src.at[layer], dst, r.w_sem.at[i])


def position(r):
    r.seg = lax.axis_index("seg")
    r.doc = lax.axis_index("doc")
    r.me = r.seg // r.stride


def forward_phase(r):
    tok, vec, qkv = r.tok, r.vec, r.qkv
    rows, width = tok.shape
    groups = rows // SEG
    pairs = width // 128
    hidden = r.act.shape[1]
    for i in range(4):
        weight_copy(r, 0, i).start()
    weight_copy(r, 0, 0).wait()
    for part in range(3):
        cols = slice(part * width, (part + 1) * width)
        out = dot(tok[...], r.b_qkv[:, cols], NN)
        if part != 1:
            out = out + vec[0, part // 2 : part // 2 + 1, :]
        qkv[:, cols] = out.astype(BF16)
    r.leave("qkv")
    for g in range(groups):
        here = slice(g * SEG, (g + 1) * SEG)
        keep = r.mask[g : g + 1, :] > 0
        for pair in range(pairs):
            at = pair * 128
            query = two_heads(qkv[here, at : at + 128])
            scores = dot(query, qkv[here, width + at : width + at + 128], NT) * SCALE
            prob = softmax_rows(jnp.where(keep, scores, NEG))
            r.probs[g * pairs + pair] = prob
            low = prob.astype(BF16)
            side = jnp.concatenate([low[:SEG], low[SEG:]], axis=1)
            value = two_heads(qkv[here, 2 * width + at : 2 * width + at + 128])
            r.ctx[here, at : at + 128] = dot(side, value, NN).astype(BF16)
    r.leave("probs")
    r.leave("ctx")
    weight_copy(r, 0, 1).wait()
    resid = tok[...].astype(F32) + (dot(r.ctx[...], r.b_out[...], NN) + vec[0, 2:3, :])
    normed, inv = norm_forward(resid)
    r.n1[...] = normed
    r.inv1[...] = jnp.broadcast_to(inv, r.inv1.shape)
    r.leave("n1")
    r.leave("inv1")
    r.h1[...] = (normed * vec[0, 3:4, :] + vec[0, 4:5, :]).astype(BF16)
    weight_copy(r, 0, 2).wait()
    for part in range(hidden // width):
        cols = slice(part * width, (part + 1) * width)
        value, grad = gelu_pair(dot(r.h1[...], r.b_up[:, cols], NN) + r.fbias[0:1, cols])
        r.act[:, cols] = value.astype(BF16)
        r.slope[:, cols] = grad.astype(BF16)
    weight_copy(r, 0, 3).wait()
    r.used(0)
    r.used(1)
    first = r.n1[...] * vec[0, 3:4, :] + vec[0, 4:5, :]
    normed, inv = norm_forward(first + (dot(r.act[...], r.b_down[...], NN) + vec[0, 5:6, :]))
    r.first[...] = (normed * vec[0, 6:7, :] + vec[0, 7:8, :]).astype(BF16)
    r.leave("first")
    r.rows_zero[...] = jnp.zeros_like(r.rows_zero)
    tops = []
    for g in range(groups):
        at = g * SEG
        tops.append(r.first[at : at + 16, :].astype(F32)[0:1])
        r.rows_zero[g : g + 1, :] = r.h1[at : at + 16, :].astype(F32)[0:1]
        r.rows_zero[groups + g : groups + g + 1, :] = normed[at : at + 1]
        r.rows_zero[2 * groups + g : 2 * groups + g + 1, :] = jnp.broadcast_to(inv[at : at + 1], (1, width))
    for g in range(groups):
        tops.append(r.cot[g * SEG : g * SEG + 16, :].astype(F32)[0:1])
    r.heads[...] = jnp.concatenate(tops + [jnp.zeros((8 - 2 * groups, width), F32)], axis=0).astype(BF16)
    r.heads_ready()
    grad = jnp.where(first_rows(rows, width), 0.0, r.cot[...].astype(F32))
    sums = {6: col_sum(grad * normed), 7: col_sum(grad)}
    dr2 = norm_backward(grad * vec[0, 6:7, :], normed, inv)
    r.dffn[...] = dr2.astype(BF16)
    r.dh1[...] = dr2
    sums[5] = col_sum(r.dffn[...])
    r.pack_v[...] = jnp.zeros_like(r.pack_v)
    put_sums(r.pack_v, sums)

    def place(chunk, b, d, value):
        slot = slot_of(FFN_ORDERS[chunk], relative(b, d, r.me, r.doc))
        r.parts[chunk, slot] = value.astype(BF16)

    for b in range(8):
        tile = dot(r.dffn[...], r.act[:, b * QC : (b + 1) * QC], TN)
        for d in range(4):
            for j in range(4):
                at = d * 192 + j * QR
                place(j, b, d, tile[at : at + QR])
    r.parts_ready(0, 4)
    for part in range(hidden // width):
        cols = slice(part * width, (part + 1) * width)
        r.dpre[:, cols] = (dot(r.dffn[...], r.b_down[cols, :], NT) * r.slope[:, cols].astype(F32)).astype(BF16)
        if part > 0:
            r.pump(part - 1)
    r.used(3)
    for d in range(4):
        for half in range(2):
            at = d * 768 + half * QC
            tile = dot(r.h1[...], r.dpre[:, at : at + QC], TN)
            for b in range(8):
                for top_half in range(2):
                    row = b * 96 + top_half * QR
                    place(4 + 2 * top_half + half, b, d, tile[row : row + QR])
        if d == 1:
            r.pump(3)
    r.parts_ready(4, 8)
    r.pump(4)
    put_bias_sums(r.pack_v, r.dpre)
    r.dh1[...] = r.dh1[...] + dot(r.dpre[...], r.b_up[...], NT)
    r.used(2)
    r.pump(5)
    r.leave("dh1")


def connect(r):
    count, stride = r.count, r.stride
    position(r)
    seg, doc, me = r.seg, r.doc, r.me
    rest = lax.rem(seg, stride)
    core = lax.rem(me, 2)
    z = me // 2
    near = z + 1 - 2 * lax.rem(z, 2)
    far = lax.rem(z + 2, 4)
    r.partners = {
        "c": (doc, (me + 1 - 2 * core) * stride + rest),
        "x": (doc + 1 - 2 * lax.rem(doc, 2), seg),
        "y": (lax.rem(doc + 2, 4), seg),
        "a": (doc, (near * 2 + core) * stride + rest),
        "b": (doc, (far * 2 + core) * stride + rest),
    }
    r.seg_peer = lambda step: (doc, lax.rem(seg + step, count))
    r.doc_peer = lambda step: (lax.rem(doc + step, 4), seg)
    barrier = pltpu.get_barrier_semaphore()

    def greet(step, carry):
        pl.semaphore_signal(barrier, inc=1, device_id=r.seg_peer(step), device_id_type=MESH)
        return carry

    lax.fori_loop(1, count, greet, 0)
    for step in range(1, 4):
        pl.semaphore_signal(barrier, inc=1, device_id=r.doc_peer(step), device_id_type=MESH)
    ffn_got = [r.f_got0, r.f_got1, r.f_got2, r.f_got3, r.f_got4]
    att_got = [r.a_got0, r.a_got1, r.a_got2, r.a_got3, r.a_got4]
    staged = getattr(r, "f_staged", None)
    kept = r.parts if staged is None else r.f_got0
    r.ffn = Halving(FFN_ORDERS, kept, ffn_got, r.ffn_shares, r.partners, r.f_send, r.f_recv, staged)
    r.att = Halving(ATT_ORDERS, r.a_parts, att_got, r.att_shares, r.partners, r.a_send, r.a_recv)
    todo = list(STEPS)

    def run(n):
        for _ in range(min(n, len(todo))):
            code = todo.pop(0)
            stage, chunk = code % 1000 // 100, code % 100
            if code >= 1000:
                r.att.step(stage, chunk)
                continue
            r.ffn.step(stage, chunk)
            if stage == 0 and staged is not None and chunk + 2 < 8:
                r.ffn.load(chunk + 2, r.i_parts, r.load_sem)

    r.run = run
    r.pump = lambda i: run(PUMPS[i])
    return lambda: pl.semaphore_wait(barrier, count + 2)


def spread(r, src, dst, send_sem, recv_sem):
    def copy(step):
        return pltpu.make_async_remote_copy(
            src_ref=src,
            dst_ref=dst.at[r.seg],
            send_sem=send_sem.at[step],
            recv_sem=recv_sem.at[step],
            device_id=r.seg_peer(step),
            device_id_type=MESH,
        )

    def begin(step, carry):
        copy(step).start()
        return carry

    def end(step, carry):
        copy(step).wait()
        return carry

    lax.fori_loop(1, r.count, begin, 0)
    return lambda: lax.fori_loop(1, r.count, end, 0)


def share_rows(r):
    r.end_heads = spread(r, r.heads, r.every, r.h_send, r.h_recv)
    r.local = fetch([(r.heads, r.every.at[r.seg]), (r.rows_zero, r.every_zero.at[r.seg])], r.local_sem)
    r.end_zero = spread(r, r.rows_zero, r.every_zero, r.z_send, r.z_recv)


def rest_phase(r):
    tok, vec, fbias = r.tok, r.vec, r.fbias
    rows, width = tok.shape
    groups = rows // SEG
    hidden = r.c_act.shape[1]
    docs = groups
    segs = r.count
    c_rows = docs * segs
    heads_n = width // HEAD
    for copy in r.local:
        copy.wait()
    r.end_heads()
    for s in range(segs):
        row = r.every[s].astype(F32)
        for d in range(docs):
            at = d * segs + s
            r.c_in[at : at + 1, :] = row[d : d + 1] + r.pos[s : s + 1, :]
            r.c_cot[at : at + 1, :] = row[docs + d : docs + d + 1]
    base = r.c_in[...]
    base_low = base.astype(BF16)
    weight_copy(r, 1, 0).wait()
    for part in range(3):
        cols = slice(part * width, (part + 1) * width)
        out = dot(base_low, r.b_qkv[:, cols], NN)
        if part != 1:
            out = out + vec[1, part // 2 : part // 2 + 1, :]
        r.c_qkv[:, cols] = out.astype(BF16)
    r.pump(6)
    blocks = [(0, c_rows)] if c_rows <= 16 else [(d * segs, segs) for d in range(docs)]
    context = []
    attention = []
    for at, n in blocks:
        here = slice(at, at + n)
        query = head_rows(r.c_qkv[here, 0:width], heads_n)
        row_doc = (at + lax.rem(lax.broadcasted_iota(jnp.int32, (heads_n * n, n), 0), n)) // segs
        key = at + lax.broadcasted_iota(jnp.int32, (heads_n * n, n), 1)
        limit = jnp.zeros((heads_n * n, n), jnp.int32)
        for d in range(docs):
            limit = jnp.where(key // segs == d, r.counts[d], limit)
        keep = jnp.logical_and(row_doc == key // segs, lax.rem(key, segs) * SEG < limit)
        scores = dot(query, r.c_qkv[here, width : 2 * width], NT) * SCALE
        prob = softmax_rows(jnp.where(keep, scores, NEG))
        prob_low = prob.astype(BF16)
        context.append(head_join(dot(prob_low, r.c_qkv[here, 2 * width : 3 * width], NN), heads_n).astype(BF16))
        attention.append((query, prob, prob_low))
    context = context[0] if len(context) == 1 else jnp.concatenate(context, axis=0)
    weight_copy(r, 1, 1).wait()
    c_n1, c_inv1 = norm_forward(base + (dot(context, r.b_out[...], NN) + vec[1, 2:3, :]))
    c_first = c_n1 * vec[1, 3:4, :] + vec[1, 4:5, :]
    c_low = c_first.astype(BF16)
    r.pump(7)
    weight_copy(r, 1, 2).wait()
    for part in range(hidden // width):
        cols = slice(part * width, (part + 1) * width)
        value, grad = gelu_pair(dot(c_low, r.b_up[:, cols], NN) + fbias[1:2, cols])
        r.c_act[:, cols] = value.astype(BF16)
        r.c_slope[:, cols] = grad.astype(r.c_slope.dtype)
    r.pump(8)
    weight_copy(r, 1, 3).wait()
    c_n2, c_inv2 = norm_forward(c_first + (dot(r.c_act[...], r.b_down[...], NN) + vec[1, 5:6, :]))
    r.mixed[...] = c_n2 * vec[1, 6:7, :] + vec[1, 7:8, :]
    r.pump(9)
    g = r.c_cot[...]
    sums = {6: col_sum(g * c_n2), 7: col_sum(g)}
    dr2 = norm_backward(g * vec[1, 6:7, :], c_n2, c_inv2)
    dffn = dr2.astype(BF16)
    for part in range(hidden // width):
        cols = slice(part * width, (part + 1) * width)
        r.c_dpre[:, cols] = (dot(dffn, r.b_down[cols, :], NT) * r.c_slope[:, cols].astype(F32)).astype(BF16)
    weight_copy(r, 0, 3).start()
    r.pump(10)
    c_grad = dr2 + dot(r.c_dpre[...], r.b_up[...], NT)
    weight_copy(r, 0, 2).start()
    r.pump(11)
    sums[3] = col_sum(c_grad * c_n1)
    sums[4] = col_sum(c_grad)
    sums[5] = col_sum(dffn)
    dr1 = norm_backward(c_grad * vec[1, 3:4, :], c_n1, c_inv1)
    dattn = dr1.astype(BF16)
    d_context = dot(dattn, r.b_out[...], NT).astype(BF16)
    weight_copy(r, 0, 1).start()
    d_parts = []
    for (at, n), (query, prob, prob_low) in zip(blocks, attention):
        here = slice(at, at + n)
        down = head_rows(d_context[here], heads_n)
        dp = dot(down, r.c_qkv[here, 2 * width : 3 * width], NT)
        ds = (prob * (dp - jnp.sum(prob * dp, axis=-1, keepdims=True))).astype(BF16)
        dv = dot(prob_low, down, TN).astype(BF16)
        dq = (head_join(dot(ds, r.c_qkv[here, width : 2 * width], NN), heads_n) * SCALE).astype(BF16)
        dk = (dot(ds, query, TN) * SCALE).astype(BF16)
        d_parts.append(jnp.concatenate([dq, dk, dv], axis=1))
    c_dqkv = d_parts[0] if len(d_parts) == 1 else jnp.concatenate(d_parts, axis=0)
    sums[0] = col_sum(c_dqkv[:, 0:width])
    sums[1] = col_sum(c_dqkv[:, 2 * width : 3 * width])
    sums[2] = col_sum(dattn)
    r.pump(12)
    dh = dr1 + dot(c_dqkv, r.b_qkv[...], NT)
    weight_copy(r, 0, 0).start()
    r.pump(13)
    r.end_zero()
    for s in range(segs):
        for d in range(docs):
            at = d * segs + s
            for i in range(2):
                r.zeros[i, at : at + 1, :] = r.every_zero[s, i * docs + d : i * docs + d + 1, :]
            r.z_inv[at : at + 1, :] = r.every_zero[s, 2 * docs + d : 2 * docs + d + 1, 0:128]
    z_n2, z_inv2 = r.zeros[1], r.z_inv[:, 0:1]
    z_sums = {6: col_sum(dh * z_n2), 7: col_sum(dh)}
    z_dr2 = norm_backward(dh * vec[0, 6:7, :], z_n2, z_inv2)
    z_dffn = z_dr2.astype(BF16)
    z_sums[5] = col_sum(z_dffn)
    z_low = r.zeros[0].astype(BF16)
    r.pack_x[...] = jnp.zeros_like(r.pack_x)
    r.pack_y[...] = jnp.zeros_like(r.pack_y)
    r.pack_c[...] = jnp.zeros_like(r.pack_c)
    total = dh[0:segs]
    for d in range(1, docs):
        total = total + dh[d * segs : (d + 1) * segs]
    for b in range(8):
        cols = slice(b * 96, (b + 1) * 96)
        r.pack_x[b, :, 0:96] = base_low[:, cols]
        r.pack_x[b, :, 128:224] = context[:, cols]
        r.pack_x[b, :, 256:352] = c_low[:, cols]
        r.pack_x[b, :, 384:768] = r.c_act[:, b * 384 : (b + 1) * 384]
        r.pack_x[b, :, 768:864] = z_low[:, cols]
        r.pack_p[b] = jnp.zeros_like(r.pack_p[b])
        r.pack_p[b, :, 0:96] = total[:, cols]
    put_sums(r.pack_c.at[:, 0:16], sums)
    put_bias_sums(r.pack_c.at[:, 0:16], r.c_dpre)
    for b in range(4):
        r.pack_y[b, :, 0:576] = c_dqkv[:, b * 576 : (b + 1) * 576]
        r.pack_y[b, :, 640:832] = dattn[:, b * 192 : (b + 1) * 192]
        r.pack_y[b, :, 896:1664] = r.c_dpre[:, b * 768 : (b + 1) * 768]
        r.pack_y[b, :, 1664:1856] = dffn[:, b * 192 : (b + 1) * 192]
        r.pack_y[b, :, 2688:2880] = z_dffn[:, b * 192 : (b + 1) * 192]
    weight_copy(r, 0, 2).wait()
    for part in range(hidden // width):
        cols = slice(part * width, (part + 1) * width)
        value, grad = gelu_pair(dot(z_low, r.b_up[:, cols], NN) + fbias[0:1, cols])
        r.c_act[:, cols] = value.astype(BF16)
        r.c_slope[:, cols] = grad.astype(r.c_slope.dtype)
    for b in range(8):
        r.pack_x[b, :, 896:1280] = r.c_act[:, b * 384 : (b + 1) * 384]
    r.pump(14)
    weight_copy(r, 0, 3).wait()
    for part in range(hidden // width):
        cols = slice(part * width, (part + 1) * width)
        r.c_dpre[:, cols] = (dot(z_dffn, r.b_down[cols, :], NT) * r.c_slope[:, cols].astype(F32)).astype(BF16)
        r.pack_y[part, :, 1920:2688] = r.c_dpre[:, cols]
    put_sums(r.pack_c.at[:, 16:32], z_sums)
    put_bias_sums(r.pack_c.at[:, 16:32], r.c_dpre)
    r.pump(15)
    r.c_in[...] = z_dr2 + dot(r.c_dpre[...], r.b_up[...], NT)
    r.pump(16)
    exchange = []
    local = fetch([(r.pack_x.at[r.me], r.rows_x.at[r.doc]), (r.pack_y.at[r.doc], r.rows_y.at[r.doc])], r.local_sem)
    for step in range(1, 4):
        there = r.doc_peer(step)
        pair = [(r.pack_x.at[r.me], r.rows_x.at[r.doc]), (r.pack_y.at[there[0]], r.rows_y.at[r.doc])]
        for i, (src, dst) in enumerate(pair):
            copy = pltpu.make_async_remote_copy(
                src_ref=src,
                dst_ref=dst,
                send_sem=r.x_send.at[step, i],
                recv_sem=r.x_recv.at[step, i],
                device_id=there,
                device_id_type=MESH,
            )
            copy.start()
            exchange.append(copy)
    r.inputs_ready()
    top = lax.broadcasted_iota(jnp.int32, (SEG, width), 0) == 0
    top_low = lax.broadcasted_iota(jnp.int32, (16, width), 0) == 0
    grads = []
    for g in range(groups):
        here = slice(g * SEG, (g + 1) * SEG)
        own = pl.ds(g * segs + r.seg, 1)
        tile = slice(g * SEG, g * SEG + 16)
        r.output[tile, :] = jnp.where(top_low, r.mixed[own, :], r.output[tile, :].astype(F32)).astype(BF16)
        grads.append(jnp.where(top, r.c_in[own, :], r.dh1[here, :]))
    grad = jnp.concatenate(grads, axis=0)
    normed = r.n1[...]
    sums = {3: col_sum(grad * normed), 4: col_sum(grad)}
    dr1 = norm_backward(grad * vec[0, 3:4, :], normed, r.inv1[:, 0:1])
    dattn = dr1.astype(BF16)
    sums[2] = col_sum(dattn)
    r.grad_tok[...] = dr1
    for d in range(4):
        r.y_qkv[:, d * 640 + 512 : d * 640 + 640] = jnp.zeros((rows, 128), BF16)
    low = lane_halves(rows)
    for d in range(4):
        slab = 3 * (d // 2) + 1
        mid = pltpu.roll(dr1[:, slab * 128 : (slab + 1) * 128], HEAD, 1).astype(BF16)
        whole = 3 * (d // 2) + 2 * (d % 2)
        fill = jnp.zeros_like(mid)
        r.y_out[:, d * 256 : d * 256 + 128] = jnp.where(low, fill, mid) if d % 2 == 0 else jnp.where(low, mid, fill)
        r.y_out[:, d * 256 + 128 : d * 256 + 256] = dattn[:, whole * 128 : (whole + 1) * 128]
    weight_copy(r, 0, 1).wait()
    r.dctx[...] = dot(dattn, r.b_out[...], NT).astype(BF16)
    r.pump(17)
    pairs = width // 128
    half = lane_halves(SEG)
    for g in range(groups):
        here = slice(g * SEG, (g + 1) * SEG)
        for pair in range(pairs):
            at = pair * 128
            prob = r.probs[g * pairs + pair]
            down = two_heads(r.dctx[here, at : at + 128])
            query = two_heads(r.qkv[here, at : at + 128])
            key = two_heads(r.qkv[here, width + at : width + at + 128])
            dp = dot(down, r.qkv[here, 2 * width + at : 2 * width + at + 128], NT)
            dv = dot(prob.astype(BF16), down, TN)
            ds = (prob * (dp - jnp.sum(prob * dp, axis=-1, keepdims=True))).astype(BF16)
            dq = dot(jnp.concatenate([ds[:SEG], ds[SEG:]], axis=1), key, NN) * SCALE
            dk = dot(ds, query, TN) * SCALE
            for kind, value in enumerate((dq, dk, dv)):
                value = value.astype(BF16)
                r.dqkv[here, kind * width + at : kind * width + at + 128] = value
                slab = kind * pairs + pair
                d, tile = slab // 9 * 2, slab % 9
                if tile < 4:
                    r.y_qkv[here, d * 640 + tile * 128 : d * 640 + tile * 128 + 128] = value
                elif tile > 4:
                    r.y_qkv[here, d * 640 + tile * 128 : d * 640 + tile * 128 + 128] = value
                else:
                    zero = jnp.zeros_like(value)
                    r.y_qkv[here, d * 640 + 512 : d * 640 + 640] = jnp.where(half, value, zero)
                    r.y_qkv[here, d * 640 + 1152 : d * 640 + 1280] = jnp.where(half, zero, value)
            if pair % 3 == 2:
                r.pump(18 + 2 * g + pair // 3)
    for side in range(2):
        for d in range(4):
            if side == 0:
                tile = dot(tok[...], r.y_qkv[:, d * 640 : d * 640 + QC], TN)
            else:
                tile = dot(tok[...], r.y_qkv[:, d * 640 + QC : d * 640 + 640], TN)
                more = dot(r.ctx[...], r.y_out[:, d * 256 : d * 256 + 256], TN)
                tile = jnp.concatenate(
                    [tile[:, 0:128], tile[:, 128:256] + more[:, 0:128], more[:, 128:256]], axis=1
                )
            for b in range(8):
                for strip in range(6):
                    chunk = 6 * side + strip
                    slot = slot_of(ATT_ORDERS[chunk], relative(b, d, r.me, r.doc))
                    at = b * 96 + strip * 16
                    r.a_parts[chunk, slot] = tile[at : at + 16].astype(BF16)
        for strip in range(6):
            chunk = 6 * side + strip
            r.att.send(0, chunk, r.a_parts.at[chunk, pl.ds(16, 16)])
        r.pump(22 + side)
    sums[0] = col_sum(r.dqkv[:, 0:width])
    sums[1] = col_sum(r.dqkv[:, 2 * width : 3 * width])
    put_sums(r.pack_v, sums)

    def vec_copy(step):
        there = r.seg_peer(step)
        return pltpu.make_async_remote_copy(
            src_ref=r.pack_v.at[there[1] // r.stride],
            dst_ref=r.vec_got.at[r.seg],
            send_sem=r.v_send.at[step],
            recv_sem=r.v_recv.at[step],
            device_id=there,
            device_id_type=MESH,
        )

    def vec_begin(step, carry):
        vec_copy(step).start()
        return carry

    def vec_finish(step, carry):
        vec_copy(step).wait()
        return carry

    lax.fori_loop(1, r.count, vec_begin, 0)
    own_vec = pltpu.make_async_copy(r.pack_v.at[r.me], r.vec_got.at[r.seg], r.local_sem.at[2])
    own_vec.start()
    weight_copy(r, 0, 0).wait()
    r.grad_tok[...] = r.grad_tok[...] + dot(r.dqkv[:, 0 : 3 * width], r.b_qkv[...], NT)
    r.pump(24)
    r.run(LATE)
    own_vec.wait()
    lax.fori_loop(1, r.count, vec_finish, 0)
    r.vec_one[0:16, :] = lax.fori_loop(
        0, r.count, lambda i, total: total + r.vec_got[i], r.pack_c[r.me, 16:32, :]
    )
    r.vec_one[16:32, :] = r.pack_c[r.me, 0:16, :]
    r.vec_one[32:, :] = r.pack_p[r.me]
    own_vec = pltpu.make_async_copy(r.vec_one, r.vec_all.at[r.doc], r.local_sem.at[3])
    own_vec.start()
    for step in range(1, 4):
        copy = pltpu.make_async_remote_copy(
            src_ref=r.vec_one,
            dst_ref=r.vec_all.at[r.doc],
            send_sem=r.s_send.at[step],
            recv_sem=r.s_recv.at[step],
            device_id=r.doc_peer(step),
            device_id_type=MESH,
        )
        copy.start()
        exchange.append(copy)
    r.run(len(STEPS))
    for copy in exchange + local:
        copy.wait()
    own_vec.wait()
    r.vec_sum[...] = r.vec_all[0] + r.vec_all[1] + r.vec_all[2] + r.vec_all[3]
    r.ffn.finish()
    r.att.finish()


def refs_of(r, names, refs):
    for name, ref in zip(names, refs, strict=True):
        setattr(r, name, ref)


WEIGHTS = ("b_qkv", "b_out", "b_up", "b_down")
SAVED = ("qkv", "probs", "ctx", "n1", "inv1", "dh1", "first")
ACTS = ("h1", "act", "slope", "dffn", "dpre")


def sizes(rows, width, hidden, segs):
    groups = rows // SEG
    c_rows = groups * segs
    dma = pltpu.SemaphoreType.DMA
    table = {
        "b_qkv": ((width, 3 * width), BF16),
        "b_out": ((width, width), BF16),
        "b_up": ((width, hidden), BF16),
        "b_down": ((hidden, width), BF16),
        "qkv": ((rows, 3 * width), BF16),
        "probs": ((groups * width // 128, 2 * SEG, SEG), F32),
        "ctx": ((rows, width), BF16),
        "n1": ((rows, width), F32),
        "inv1": ((rows, 128), F32),
        "dh1": ((rows, width), F32),
        "first": ((rows, width), BF16),
        "h1": ((rows, width), BF16),
        "act": ((rows, hidden), BF16),
        "slope": ((rows, hidden), BF16),
        "dffn": ((rows, width), BF16),
        "dpre": ((rows, hidden), BF16),
        "parts": ((8, 32, QR, QC), BF16),
        "heads": ((8, width), BF16),
        "rows_zero": ((8, width), F32),
        "pack_v": ((8, 16, 128), F32),
        "output": ((rows, width), BF16),
        "grad_tok": ((rows, width), F32),
        "ffn_shares": ((8, QR, QC), F32),
        "att_shares": ((12, 16, QC), F32),
        "rows_x": ((4, c_rows, 1280), BF16),
        "rows_y": ((4, c_rows, 2944), BF16),
        "vec_all": ((4, 32 + segs, 128), F32),
        "vec_sum": ((32 + segs, 128), F32),
        "every": ((segs, 8, width), BF16),
        "every_zero": ((segs, 8, width), F32),
        "c_qkv": ((c_rows, 3 * width), BF16),
        "c_in": ((c_rows, width), F32),
        "c_cot": ((c_rows, width), F32),
        "c_act": ((c_rows, hidden), BF16),
        "c_slope": ((c_rows, hidden), F32 if c_rows <= 16 else BF16),
        "c_dpre": ((c_rows, hidden), BF16),
        "mixed": ((c_rows, width), F32),
        "zeros": ((2, c_rows, width), F32),
        "z_inv": ((c_rows, 128), F32),
        "pack_x": ((8, c_rows, 1280), BF16),
        "pack_y": ((4, c_rows, 2944), BF16),
        "pack_c": ((8, 32, 128), F32),
        "pack_p": ((8, segs, 128), F32),
        "dctx": ((rows, width), BF16),
        "vec_got": ((segs, 16, 128), F32),
        "vec_one": ((32 + segs, 128), F32),
        "a_parts": ((12, 32, 16, QC), BF16),
        "f_staged": ((2, 16, QR, QC), BF16),
        "y_qkv": ((rows, 2560), BF16),
        "y_out": ((rows, 1024), BF16),
        "dqkv": ((rows, 3 * width), BF16),
    }
    for i in range(5):
        table[f"f_got{i}"] = ((8, 16 >> i, QR, QC), BF16)
        table[f"a_got{i}"] = ((12, 16 >> i, 16, QC), BF16)
    sems = {
        "w_sem": (4,), "in_sem": (7,), "load_sem": (8,), "out_sem": (9,), "h_send": (segs,), "h_recv": (segs,),
        "z_send": (segs,), "z_recv": (segs,), "f_send": (5, 8), "f_recv": (5, 8), "a_send": (5, 12),
        "a_recv": (5, 12), "x_send": (4, 2), "x_recv": (4, 2), "v_send": (segs,), "v_recv": (segs,),
        "s_send": (4,), "s_recv": (4,), "local_sem": (4,),
    }
    return table, {name: dma(shape) for name, shape in sems.items()}


REST_OUT = ("output", "grad_tok", "ffn_shares", "att_shares", "rows_x", "rows_y", "vec_all", "vec_sum")
REST_SCRATCH = (
    ("every", "every_zero", "c_qkv", "c_in", "c_cot", "c_act", "c_slope", "c_dpre", "mixed", "zeros", "z_inv")
    + ("pack_x", "pack_y", "pack_c", "pack_p", "dctx", "vec_got", "vec_one", "a_parts")
    + tuple(f"f_got{i}" for i in range(5))
    + tuple(f"a_got{i}" for i in range(5))
)
REST_SEMS = (
    ("w_sem", "in_sem", "load_sem", "h_send", "h_recv", "z_send", "z_recv", "f_send", "f_recv", "a_send", "a_recv")
    + ("x_send", "x_recv", "v_send", "v_recv", "s_send", "s_recv", "local_sem")
)
W_NAMES = ("w_qkv", "w_out", "w_up", "w_down")


def call(body, name, ins, in_specs, outs, out_specs, scratch, table, sems, collective, args):
    shape = jax.ShapeDtypeStruct
    return pl.pallas_call(
        body,
        out_shape=tuple(shape(*table[n]) for n in outs),
        in_specs=in_specs,
        out_specs=out_specs,
        scratch_shapes=[sems[n] if n in sems else pltpu.VMEM(*table[n]) for n in scratch],
        compiler_params=pltpu.CompilerParams(
            vmem_limit_bytes=LIMIT,
            **(dict(collective_id=0, has_side_effects=True) if collective else {}),
        ),
        name=name,
    )(*args)


def run_whole(stride, segs, counts, tok, mask, cot, pos, vec, fbias, weights):
    rows, width = tok.shape
    table, sems = sizes(rows, width, weights[2].shape[2], segs)
    ins = ("counts", "tok", "mask", "cot", "pos", "vec", "fbias") + W_NAMES
    kept = SAVED[:-1] + ACTS + ("parts", "heads", "rows_zero", "pack_v")
    scratch = WEIGHTS + kept + REST_SCRATCH + REST_SEMS

    def body(*refs):
        r = SimpleNamespace(stride=stride, count=segs)
        refs_of(r, ins + REST_OUT + scratch, refs)
        r.first = r.output
        r.y_qkv, r.y_out, r.dqkv = r.dpre, r.act, r.slope
        enter = connect(r)
        r.leave = lambda name: None
        r.used = lambda i: weight_copy(r, 1, i).start()
        r.inputs_ready = lambda: None

        def heads_ready():
            enter()
            share_rows(r)

        def parts_ready(first, last):
            for chunk in range(first, last):
                r.ffn.send(0, chunk, r.parts.at[chunk, pl.ds(16, 16)])

        r.heads_ready = heads_ready
        r.parts_ready = parts_ready
        forward_phase(r)
        rest_phase(r)

    return call(
        body, "whole_step", ins, [SM] + [VM] * 6 + [ANY] * 4, REST_OUT, (VM,) * 8, scratch, table, sems, True,
        (counts, tok, mask, cot, pos, vec, fbias) + weights,
    )


def run_halves(stride, segs, counts, tok, mask, cot, pos, vec, fbias, weights):
    rows, width = tok.shape
    table, sems = sizes(rows, width, weights[2].shape[2], segs)
    ins = ("tok", "mask", "cot", "vec", "fbias") + W_NAMES
    outs = tuple("o_" + n for n in SAVED) + ("o_parts", "heads", "rows_zero", "pack_v")
    for n in SAVED + ("parts",):
        table["o_" + n] = table[n]
    scratch = WEIGHTS + SAVED + ACTS + ("parts", "w_sem", "out_sem")

    def first_body(*refs):
        r = SimpleNamespace(stride=stride, count=segs)
        refs_of(r, ins + outs + scratch, refs)
        position(r)
        leaving = []

        def go(src, dst):
            copy = pltpu.make_async_copy(src, dst, r.out_sem.at[len(leaving)])
            copy.start()
            leaving.append(copy)

        r.leave = lambda name: go(getattr(r, name), getattr(r, "o_" + name))
        r.parts_ready = lambda a, b: go(r.parts.at[a:b], r.o_parts.at[a:b])
        r.used = lambda i: None
        r.pump = lambda i: None
        r.heads_ready = lambda: None
        forward_phase(r)
        for copy in leaving:
            copy.wait()

    *saved, parts, heads, rows_zero, pack_v = call(
        first_body, "segment_forward", ins, [VM] * 5 + [ANY] * 4, outs, (ANY,) * 8 + (VM,) * 3, scratch, table, sems,
        False, (tok, mask, cot, vec, fbias) + weights,
    )
    ins_b = ("counts", "heads", "rows_zero", "tok", "pack_v", "pos", "vec", "fbias", "i_parts")
    ins_b = ins_b + tuple("i_" + n for n in SAVED) + W_NAMES
    scratch_b = WEIGHTS + SAVED[:-1] + REST_SCRATCH + ("f_staged", "y_qkv", "y_out", "dqkv") + REST_SEMS

    def second_body(*refs):
        r = SimpleNamespace(stride=stride, count=segs)
        refs_of(r, ins_b + REST_OUT + scratch_b, refs)
        for i in range(4):
            weight_copy(r, 1, i).start()
        enter = connect(r)
        enter()
        share_rows(r)
        for chunk in range(8):
            r.ffn.send(0, chunk, r.i_parts.at[chunk, pl.ds(16, 16)])
        for chunk in range(2):
            r.ffn.load(chunk, r.i_parts, r.load_sem)
        r.first = r.output
        inputs = fetch([(getattr(r, "i_" + n), getattr(r, n)) for n in SAVED], r.in_sem)

        def inputs_ready():
            for copy in inputs:
                copy.wait()

        r.inputs_ready = inputs_ready
        rest_phase(r)

    return call(
        second_body, "the_rest", ins_b, [SM] + [VM] * 7 + [ANY] * 12, REST_OUT, (VM,) * 4 + (ANY,) * 2 + (VM,) * 2,
        scratch_b, table, sems, True,
        (counts, heads, rows_zero, tok, pack_v, pos, vec, fbias, parts, *saved) + weights,
    )


def assemble(
    stride, ffn, att, rows_x, rows_y, sums, i_output, i_grad, g_qkv, g_out, g_up, g_down, g_vec, g_bias, g_pos,
    output, grad_tok,
):
    output[...] = i_output[...]
    grad_tok[...] = i_grad[...]
    rows = rows_x.shape[0] * rows_x.shape[1]
    doc = lax.axis_index("doc")
    x = rows_x[...].reshape(rows, rows_x.shape[2])
    y = rows_y[...].reshape(rows, rows_y.shape[2])
    g_qkv[1] = dot(x[:, 0:128], y[:, 0:640], TN)[0:96, 0:576]
    g_out[1] = dot(x[:, 128:256], y[:, 640:896], TN)[0:96, 0:192]
    g_up[1] = dot(x[:, 256:384], y[:, 896:1664], TN)[0:96, :]
    g_down[1] = dot(x[:, 384:768], y[:, 1664:1920], TN)[:, 0:192]
    more = dot(x[:, 768:896], y[:, 1920:2688], TN)
    for r in range(2):
        at = slice(r * QR, (r + 1) * QR)
        for c in range(2):
            cols = slice(c * QC, (c + 1) * QC)
            g_up[0, at, cols] = ffn[4 + 2 * r + c] + more[at, cols]
    tall = jnp.concatenate([ffn[0], ffn[1], ffn[2], ffn[3]], axis=0)
    g_down[0] = jnp.transpose(tall) + dot(x[:, 896:1280], y[:, 2688:2944], TN)[:, 0:192]
    left = jnp.concatenate([att[i] for i in range(6)], axis=0)
    right = jnp.concatenate([att[6 + i] for i in range(6)], axis=0)
    mid, last = right[:, 128:256], right[:, 256:384]
    slabs = jnp.concatenate([left, right[:, 0:128]], axis=1)

    @pl.when(lax.rem(doc, 2) == 0)
    def _():
        g_qkv[0, :, 0:512] = slabs
        g_qkv[0, :, 512:576] = mid[:, 0:64]
        g_out[0, :, 0:128] = last
        g_out[0, :, 128:192] = mid[:, 64:128]

    @pl.when(lax.rem(doc, 2) == 1)
    def _():
        g_qkv[0] = jnp.concatenate([mid[:, 64:128], slabs], axis=1)
        g_out[0] = jnp.concatenate([mid[:, 0:64], last], axis=1)

    if stride > 1:
        for layer in range(2):
            g_vec[layer] = sums[16 * layer : 16 * layer + 8, 0:96]
            g_bias[layer] = sums[16 * layer + 8 : 16 * layer + 12, 0:96]
    else:
        for layer in range(2):
            g_vec[layer] = sums[pl.ds(16 * layer + 2 * doc, 2), 0:96]
            for i in range(4):
                at = 16 * layer + 8 + i
                g_bias[layer : layer + 1, i * 96 : i * 96 + 96] = sums[at : at + 1, 0:96]
    g_pos[...] = sums[32:, 0:96]


def run_assemble(stride, ffn, att, rows_x, rows_y, sums, output, grad_tok):
    shape = jax.ShapeDtypeStruct
    return pl.pallas_call(
        functools.partial(assemble, stride),
        out_shape=(
            shape((2, 96, 576), F32),
            shape((2, 96, 192), F32),
            shape((2, 96, 768), F32),
            shape((2, 384, 192), F32),
            shape((2, 2, 96) if stride == 1 else (2, 8, 96), F32),
            shape((2, 384) if stride == 1 else (2, 4, 96), F32),
            shape((sums.shape[0] - 32, 96), F32),
            shape(output.shape, BF16),
            shape(grad_tok.shape, F32),
        ),
        in_specs=[VM] * 7,
        out_specs=(VM,) * 9,
        compiler_params=pltpu.CompilerParams(vmem_limit_bytes=LIMIT),
        name="assemble",
    )(ffn, att, rows_x, rows_y, sums, output, grad_tok)


def shards(
    tokens,
    token_mask,
    doc_counts,
    w_qkv,
    w_out,
    w_up,
    w_down,
    vectors,
    ffn_bias,
    pos_embed,
    cotangent,
):
    docs, slots, width = tokens.shape
    seg_dev = slots // SEG
    groups = docs * seg_dev
    count = lax.axis_size("seg")
    stride = count // 8
    rest = lax.rem(lax.axis_index("seg"), stride)
    tok = tokens.reshape(groups * SEG, width)
    cot = cotangent.reshape(groups * SEG, width)
    weights = (w_qkv, w_out, w_up, w_down)
    run = run_whole if groups * count <= 16 else run_halves
    output, grad_tok, ffn, att, rows_x, rows_y, _, sums = run(
        stride, count, doc_counts, tok, token_mask.reshape(groups, SEG), cot, pos_embed, vectors, ffn_bias, weights
    )
    g_qkv, g_out, g_up, g_down, g_vec, g_bias, g_pos, output, grad_tok = run_assemble(
        stride, ffn, att, rows_x, rows_y, sums, output, grad_tok
    )
    if stride > 1:
        lanes = [[i * stride + j for j in range(stride)] for i in range(8)]

        def own(arr, dim):
            low = lax.psum_scatter(arr[0:1], "seg", scatter_dimension=dim, axis_index_groups=lanes, tiled=True)
            size = arr.shape[dim] // stride
            return jnp.concatenate([low, lax.dynamic_slice_in_dim(arr[1:2], rest * size, size, dim)], axis=0)

        g_qkv, g_out, g_up, g_down = own(g_qkv, 1), own(g_out, 1), own(g_up, 1), own(g_down, 1)
        each = 96 // stride
        g_vec = lax.dynamic_slice(g_vec, (0, lax.axis_index("doc") * 2, rest * each), (2, 2, each))
        g_bias = lax.dynamic_slice_in_dim(g_bias.reshape(2, 384), rest * (384 // stride), 384 // stride, 1)
        g_pos = lax.dynamic_slice_in_dim(g_pos, rest * each, each, 1)
    return (
        output.reshape(tokens.shape),
        grad_tok.reshape(tokens.shape),
        g_qkv,
        g_out,
        g_up,
        g_down,
        g_vec,
        g_bias,
        g_pos,
    )


def solution(mesh):
    return jax.shard_map(
        shards,
        mesh=mesh,
        in_specs=(
            P("doc", "seg", None),
            P("doc", "seg"),
            P("doc"),
            P(),
            P(),
            P(),
            P(),
            P(),
            P(),
            P(),
            P("doc", "seg", None),
        ),
        out_specs=(
            P("doc", "seg", None),
            P("doc", "seg", None),
            P(None, "seg", "doc"),
            P(None, "seg", "doc"),
            P(None, "seg", "doc"),
            P(None, "seg", "doc"),
            P(None, "doc", "seg"),
            P(None, "seg"),
            P(None, "seg"),
        ),
        check_vma=False,
    )
```

```python
import functools
from types import SimpleNamespace

import jax
import jax.numpy as jnp
from jax import lax
from jax.experimental import pallas as pl
from jax.experimental.pallas import tpu as pltpu
from jax.sharding import PartitionSpec as P

MESH = pl.DeviceIdType.MESH
HEAD = 64
SEG = 128
NEG = -1e30
EPS = 1e-05
ROOT_HALF = 0.7071067811865476
INV_ROOT_TWO_PI = 0.3989422804014327
SCALE = HEAD ** (-0.5)
F32 = jnp.float32
BF16 = jnp.bfloat16
VM = pl.BlockSpec(memory_space=pltpu.VMEM)
SM = pl.BlockSpec(memory_space=pltpu.SMEM)
ANY = pl.BlockSpec(memory_space=pl.ANY)
LIMIT = 62 << 20
QR, QC = 48, 384
NN = (((1,), (0,)), ((), ()))
NT = (((1,), (1,)), ((), ()))
TN = (((0,), (0,)), ((), ()))


def dot(a, b, dims):
    return lax.dot_general(a, b, dims, preferred_element_type=F32)


def norm_forward(resid):
    cent = resid - jnp.mean(resid, axis=-1, keepdims=True)
    inv = lax.rsqrt(jnp.mean(cent * cent, axis=-1, keepdims=True) + EPS)
    return cent * inv, inv


def norm_backward(scaled, normed, inv):
    inner = jnp.mean(scaled * normed, axis=-1, keepdims=True)
    return inv * (scaled - jnp.mean(scaled, axis=-1, keepdims=True) - normed * inner)


def gelu_pair(pre):
    half_cdf = 0.5 * (1.0 + lax.erf(pre * ROOT_HALF))
    slope = half_cdf + pre * jnp.exp(-0.5 * pre * pre) * INV_ROOT_TWO_PI
    return pre * half_cdf, slope


def col_sum(arr):
    return jnp.sum(arr.astype(F32), axis=0, keepdims=True)


def softmax_rows(scores):
    expo = jnp.exp(scores - jnp.max(scores, axis=-1, keepdims=True))
    return expo / jnp.sum(expo, axis=-1, keepdims=True)


def lane_halves(rows):
    lane = lax.broadcasted_iota(jnp.int32, (rows, 128), 1)
    return lane < HEAD


def two_heads(slab):
    low = lane_halves(slab.shape[0])
    zero = jnp.zeros_like(slab)
    return jnp.concatenate([jnp.where(low, slab, zero), jnp.where(low, zero, slab)], axis=0)


def fetch(pairs, sem):
    copies = [pltpu.make_async_copy(src, dst, sem.at[i]) for i, (src, dst) in enumerate(pairs)]
    for copy in copies:
        copy.start()
    return copies


def xor_bit(a, b):
    return a + b - 2 * a * b


FFN_ORDERS = (
    "xyab", "axyb", "yabx", "xyab", "yabx", "xayb", "yxab", "abyx",
)
ATT_ORDERS = (
    "xayb", "axby", "yaxb", "xyab", "yxab", "xyab", "xayb", "yxab", "yxab", "xayb", "xaby", "xaby",
)


def relative(b, d, me, doc):
    return {
        "c": xor_bit(lax.rem(me, 2), b % 2),
        "x": xor_bit(lax.rem(doc, 2), d % 2),
        "y": xor_bit(doc // 2, d // 2),
        "a": xor_bit(lax.rem(me // 2, 2), (b // 2) % 2),
        "b": xor_bit(me // 4, b // 4),
    }


def slot_of(order, bits):
    return sum(bits[name] * (16 >> i) for i, name in enumerate("c" + order))


def first_rows(rows, width):
    return lax.rem(lax.broadcasted_iota(jnp.int32, (rows, width), 0), SEG) == 0


def put_bias_sums(pack_v, dpre):
    for b in range(8):
        for i in range(4):
            at = b * 384 + i * 96
            pack_v[b, 8 + i : 9 + i, 0:96] = col_sum(dpre[:, at : at + 96])


def put_sums(pack_v, sums):
    for b in range(8):
        for i, value in sums.items():
            pack_v[b, i : i + 1, 0:96] = value[:, b * 96 : (b + 1) * 96]


def head_rows(arr, heads):
    rows, width = arr.shape
    lane = lax.broadcasted_iota(jnp.int32, (rows, width), 1)
    zero = jnp.zeros_like(arr)
    parts = [jnp.where(lane // HEAD == h, arr, zero) for h in range(heads)]
    return jnp.concatenate(parts, axis=0)


def head_join(arr, heads):
    rows = arr.shape[0] // heads
    lane = lax.broadcasted_iota(jnp.int32, (rows, arr.shape[1]), 1)
    out = jnp.zeros((rows, arr.shape[1]), F32)
    for h in range(heads):
        out = jnp.where(lane // HEAD == h, arr[h * rows : (h + 1) * rows], out)
    return out


class Halving:
    def __init__(self, orders, kept, got, shares, partners, send_sem, recv_sem, staged=None):
        self.orders, self.kept, self.got, self.shares, self.staged = orders, kept, got, shares, staged
        self.partners, self.send_sem, self.recv_sem = partners, send_sem, recv_sem
        self.sends = {}
        self.loads = []

    def send(self, stage, chunk, src):
        copy = pltpu.make_async_remote_copy(
            src_ref=src,
            dst_ref=self.got[stage].at[chunk],
            send_sem=self.send_sem.at[stage, chunk],
            recv_sem=self.recv_sem.at[stage, chunk],
            device_id=self.partners[("c" + self.orders[chunk])[stage]],
            device_id_type=MESH,
        )
        copy.start()
        self.sends[stage, chunk] = copy

    def load(self, chunk, source, sem):
        copy = pltpu.make_async_copy(source.at[chunk, pl.ds(0, 16)], self.staged.at[chunk % 2], sem.at[chunk])
        copy.start()
        self.loads.append(copy)

    def add(self, stage, chunk, first, last):
        kept = self.kept
        more = self.got[stage].at[chunk]
        if stage == 0 and self.staged is not None:
            more = self.staged.at[chunk % 2]

        kept[chunk, first:last] = kept[chunk, first:last] + more[first:last]

    def step(self, stage, chunk):
        if stage == 0 and self.staged is not None:
            self.loads[chunk].wait()
        self.sends[stage, chunk].wait_recv()
        half = (16 >> stage) // 2
        if stage < 4:
            self.add(stage, chunk, half, 2 * half)
            self.send(stage + 1, chunk, self.kept.at[chunk, pl.ds(half, half)])
            if stage > 0:
                self.sends.pop((stage - 1, chunk)).wait_send()
            self.add(stage, chunk, 0, half)
        else:
            self.shares[chunk] = self.kept[chunk, 0].astype(F32) + self.got[4][chunk, 0].astype(F32)

    def finish(self):
        for copy in self.sends.values():
            copy.wait_send()


STEPS = (
    0, 1, 2, 3, 4, 5, 6, 7, 100, 101, 102, 103, 107, 104, 202, 105, 201, 106, 204, 1009, 1010, 207, 1011, 200,
    302, 205, 203, 1000, 1003, 206, 1006, 1001, 1002, 1004, 1005, 1007, 1008, 300, 1109, 304, 303, 1110, 301,
    306, 307, 1111, 402, 1101, 305, 1209, 1100, 400, 1102, 1210, 403, 1103, 1104, 401, 1106, 1107, 1211, 406,
    1105, 1108, 1200, 404, 405, 1309, 407, 1202, 1203, 1201, 1205, 1310, 1206, 1300, 1204, 1207, 1311, 1303,
    1409, 1410, 1208, 1306, 1305, 1302, 1301, 1304, 1411, 1400, 1307, 1308, 1403, 1401, 1406, 1405, 1402, 1404,
    1407, 1408,
)
PUMPS = (
    0, 0, 0, 1, 1, 2, 2, 2, 0, 1, 1, 1, 0, 2, 1, 1, 1, 0, 2, 3, 2, 1, 0, 1, 8,
)
LATE = 16


def weight_copy(r, layer, i):
    src = (r.w_qkv, r.w_out, r.w_up, r.w_down)[i]
    dst = (r.b_qkv, r.b_out, r.b_up, r.b_down)[i]
    return pltpu.make_async_copy(src.at[layer], dst, r.w_sem.at[i])


def position(r):
    r.seg = lax.axis_index("seg")
    r.doc = lax.axis_index("doc")
    r.me = r.seg // r.stride


def forward_phase(r):
    tok, vec, qkv = r.tok, r.vec, r.qkv
    rows, width = tok.shape
    groups = rows // SEG
    pairs = width // 128
    hidden = r.act.shape[1]
    thirds = []
    for part in range(3):
        cols = slice(part * width, (part + 1) * width)
        thirds.append(
            pltpu.make_async_copy(r.w_qkv.at[0, :, cols], r.b_qkv.at[:, cols], r.third_sem.at[part])
        )
        thirds[part].start()
    for i in range(1, 4):
        weight_copy(r, 0, i).start()
    for part in range(3):
        cols = slice(part * width, (part + 1) * width)
        thirds[part].wait()
        out = dot(tok[...], r.b_qkv[:, cols], NN)
        if part != 1:
            out = out + vec[0, part // 2 : part // 2 + 1, :]
        qkv[:, cols] = out.astype(BF16)
    r.leave("qkv")
    for g in range(groups):
        here = slice(g * SEG, (g + 1) * SEG)
        keep = r.mask[g : g + 1, :] > 0
        for pair in range(pairs):
            at = pair * 128
            query = two_heads(qkv[here, at : at + 128])
            scores = dot(query, qkv[here, width + at : width + at + 128], NT) * SCALE
            prob = softmax_rows(jnp.where(keep, scores, NEG))
            r.probs[g * pairs + pair] = prob
            low = prob.astype(BF16)
            side = jnp.concatenate([low[:SEG], low[SEG:]], axis=1)
            value = two_heads(qkv[here, 2 * width + at : 2 * width + at + 128])
            r.ctx[here, at : at + 128] = dot(side, value, NN).astype(BF16)
    r.leave("probs")
    r.leave("ctx")
    weight_copy(r, 0, 1).wait()
    resid = tok[...].astype(F32) + (dot(r.ctx[...], r.b_out[...], NN) + vec[0, 2:3, :])
    normed, inv = norm_forward(resid)
    r.n1[...] = normed
    r.inv1[...] = jnp.broadcast_to(inv, r.inv1.shape)
    r.leave("n1")
    r.leave("inv1")
    r.h1[...] = (normed * vec[0, 3:4, :] + vec[0, 4:5, :]).astype(BF16)
    weight_copy(r, 0, 2).wait()
    for part in range(hidden // width):
        cols = slice(part * width, (part + 1) * width)
        value, grad = gelu_pair(dot(r.h1[...], r.b_up[:, cols], NN) + r.fbias[0:1, cols])
        r.act[:, cols] = value.astype(BF16)
        r.slope[:, cols] = grad.astype(BF16)
    weight_copy(r, 0, 3).wait()
    r.used(0)
    r.used(1)
    first = r.n1[...] * vec[0, 3:4, :] + vec[0, 4:5, :]
    normed, inv = norm_forward(first + (dot(r.act[...], r.b_down[...], NN) + vec[0, 5:6, :]))
    r.first[...] = (normed * vec[0, 6:7, :] + vec[0, 7:8, :]).astype(BF16)
    r.leave("first")
    r.rows_zero[...] = jnp.zeros_like(r.rows_zero)
    starts = [g * SEG for g in range(groups)]
    tops = [r.first[at : at + 16, :].astype(F32)[0:1] for at in starts]
    tops += [r.cot[at : at + 16, :].astype(F32)[0:1] for at in starts]
    tops += [r.h1[at : at + 16, :].astype(F32)[0:1] for at in starts]
    tops += [normed[at : at + 1] for at in starts]
    r.heads[...] = jnp.concatenate(tops, axis=0).astype(BF16)
    for g, at in enumerate(starts):
        r.rows_zero[g : g + 1, :] = jnp.broadcast_to(inv[at : at + 1], (1, 128))
    r.heads_ready()
    grad = jnp.where(first_rows(rows, width), 0.0, r.cot[...].astype(F32))
    sums = {6: col_sum(grad * normed), 7: col_sum(grad)}
    dr2 = norm_backward(grad * vec[0, 6:7, :], normed, inv)
    r.dffn[...] = dr2.astype(BF16)
    r.dh1[...] = dr2
    sums[5] = col_sum(r.dffn[...])
    r.pack_v[...] = jnp.zeros_like(r.pack_v)
    put_sums(r.pack_v, sums)

    def place(chunk, b, d, value):
        slot = slot_of(FFN_ORDERS[chunk], relative(b, d, r.me, r.doc))
        r.parts[chunk, slot] = value.astype(BF16)

    for b in range(8):
        tile = dot(r.dffn[...], r.act[:, b * QC : (b + 1) * QC], TN)
        for d in range(4):
            for j in range(4):
                at = d * 192 + j * QR
                place(j, b, d, tile[at : at + QR])
    r.parts_ready(0, 4)
    for part in range(hidden // width):
        cols = slice(part * width, (part + 1) * width)
        r.dpre[:, cols] = (dot(r.dffn[...], r.b_down[cols, :], NT) * r.slope[:, cols].astype(F32)).astype(BF16)
        if part > 0:
            r.pump(part - 1)
    r.used(3)
    for d in range(4):
        for half in range(2):
            at = d * 768 + half * QC
            tile = dot(r.h1[...], r.dpre[:, at : at + QC], TN)
            for b in range(8):
                for top_half in range(2):
                    row = b * 96 + top_half * QR
                    place(4 + 2 * top_half + half, b, d, tile[row : row + QR])
        if d == 1:
            r.pump(3)
    r.parts_ready(4, 8)
    r.pump(4)
    put_bias_sums(r.pack_v, r.dpre)
    r.dh1[...] = r.dh1[...] + dot(r.dpre[...], r.b_up[...], NT)
    r.used(2)
    r.pump(5)
    r.leave("dh1")


def connect(r):
    count, stride = r.count, r.stride
    position(r)
    seg, doc, me = r.seg, r.doc, r.me
    rest = lax.rem(seg, stride)
    core = lax.rem(me, 2)
    z = me // 2
    near = z + 1 - 2 * lax.rem(z, 2)
    far = lax.rem(z + 2, 4)
    r.partners = {
        "c": (doc, (me + 1 - 2 * core) * stride + rest),
        "x": (doc + 1 - 2 * lax.rem(doc, 2), seg),
        "y": (lax.rem(doc + 2, 4), seg),
        "a": (doc, (near * 2 + core) * stride + rest),
        "b": (doc, (far * 2 + core) * stride + rest),
    }
    r.seg_peer = lambda step: (doc, lax.rem(seg + step, count))
    r.doc_peer = lambda step: (lax.rem(doc + step, 4), seg)
    barrier = pltpu.get_barrier_semaphore()

    def greet(step, carry):
        pl.semaphore_signal(barrier, inc=1, device_id=r.seg_peer(step), device_id_type=MESH)
        return carry

    lax.fori_loop(1, count, greet, 0)
    for step in range(1, 4):
        pl.semaphore_signal(barrier, inc=1, device_id=r.doc_peer(step), device_id_type=MESH)
    ffn_got = [r.f_got0, r.f_got1, r.f_got2, r.f_got3, r.f_got4]
    att_got = [r.a_got0, r.a_got1, r.a_got2, r.a_got3, r.a_got4]
    staged = getattr(r, "f_staged", None)
    kept = r.parts if staged is None else r.f_got0
    r.ffn = Halving(FFN_ORDERS, kept, ffn_got, r.ffn_shares, r.partners, r.f_send, r.f_recv, staged)
    r.att = Halving(ATT_ORDERS, r.a_parts, att_got, r.att_shares, r.partners, r.a_send, r.a_recv)
    todo = list(STEPS)

    def run(n):
        for _ in range(min(n, len(todo))):
            code = todo.pop(0)
            stage, chunk = code % 1000 // 100, code % 100
            if code >= 1000:
                r.att.step(stage, chunk)
                continue
            r.ffn.step(stage, chunk)
            if stage == 0 and staged is not None and chunk + 2 < 8:
                r.ffn.load(chunk + 2, r.i_parts, r.load_sem)

    r.run = run
    r.pump = lambda i: run(PUMPS[i])
    return lambda: pl.semaphore_wait(barrier, count + 2)


def spread(r, src, dst, send_sem, recv_sem):
    def copy(step):
        return pltpu.make_async_remote_copy(
            src_ref=src,
            dst_ref=dst.at[r.seg],
            send_sem=send_sem.at[step],
            recv_sem=recv_sem.at[step],
            device_id=r.seg_peer(step),
            device_id_type=MESH,
        )

    def begin(step, carry):
        copy(step).start()
        return carry

    def end(step, carry):
        copy(step).wait()
        return carry

    lax.fori_loop(1, r.count, begin, 0)
    return lambda: lax.fori_loop(1, r.count, end, 0)


def share_rows(r):
    r.end_heads = spread(r, r.heads, r.every, r.h_send, r.h_recv)
    r.local = fetch([(r.heads, r.every.at[r.seg]), (r.rows_zero, r.every_zero.at[r.seg])], r.local_sem)
    r.end_zero = spread(r, r.rows_zero, r.every_zero, r.z_send, r.z_recv)


def rest_phase(r):
    tok, vec, fbias = r.tok, r.vec, r.fbias
    rows, width = tok.shape
    groups = rows // SEG
    hidden = r.c_act.shape[1]
    docs = groups
    segs = r.count
    c_rows = docs * segs
    heads_n = width // HEAD
    for copy in r.local:
        copy.wait()
    r.end_heads()
    for s in range(segs):
        row = r.every[s].astype(F32)
        for d in range(docs):
            at = d * segs + s
            r.c_in[at : at + 1, :] = row[d : d + 1] + r.pos[s : s + 1, :]
            r.c_cot[at : at + 1, :] = row[docs + d : docs + d + 1]
            r.zeros[0, at : at + 1, :] = row[2 * docs + d : 2 * docs + d + 1]
            r.zeros[1, at : at + 1, :] = row[3 * docs + d : 3 * docs + d + 1]
    base = r.c_in[...]
    base_low = base.astype(BF16)
    weight_copy(r, 1, 0).wait()
    for part in range(3):
        cols = slice(part * width, (part + 1) * width)
        out = dot(base_low, r.b_qkv[:, cols], NN)
        if part != 1:
            out = out + vec[1, part // 2 : part // 2 + 1, :]
        r.c_qkv[:, cols] = out.astype(BF16)
    r.pump(6)
    blocks = [(0, c_rows)] if c_rows <= 16 else [(d * segs, segs) for d in range(docs)]
    context = []
    attention = []
    for at, n in blocks:
        here = slice(at, at + n)
        query = head_rows(r.c_qkv[here, 0:width], heads_n)
        row_doc = (at + lax.rem(lax.broadcasted_iota(jnp.int32, (heads_n * n, n), 0), n)) // segs
        key = at + lax.broadcasted_iota(jnp.int32, (heads_n * n, n), 1)
        limit = jnp.zeros((heads_n * n, n), jnp.int32)
        for d in range(docs):
            limit = jnp.where(key // segs == d, r.counts[d], limit)
        keep = jnp.logical_and(row_doc == key // segs, lax.rem(key, segs) * SEG < limit)
        scores = dot(query, r.c_qkv[here, width : 2 * width], NT) * SCALE
        prob = softmax_rows(jnp.where(keep, scores, NEG))
        prob_low = prob.astype(BF16)
        context.append(head_join(dot(prob_low, r.c_qkv[here, 2 * width : 3 * width], NN), heads_n).astype(BF16))
        attention.append((query, prob, prob_low))
    context = context[0] if len(context) == 1 else jnp.concatenate(context, axis=0)
    weight_copy(r, 1, 1).wait()
    c_n1, c_inv1 = norm_forward(base + (dot(context, r.b_out[...], NN) + vec[1, 2:3, :]))
    c_first = c_n1 * vec[1, 3:4, :] + vec[1, 4:5, :]
    c_low = c_first.astype(BF16)
    r.pump(7)
    weight_copy(r, 1, 2).wait()
    for part in range(hidden // width):
        cols = slice(part * width, (part + 1) * width)
        value, grad = gelu_pair(dot(c_low, r.b_up[:, cols], NN) + fbias[1:2, cols])
        r.c_act[:, cols] = value.astype(BF16)
        r.c_slope[:, cols] = grad.astype(r.c_slope.dtype)
    r.pump(8)
    weight_copy(r, 1, 3).wait()
    c_n2, c_inv2 = norm_forward(c_first + (dot(r.c_act[...], r.b_down[...], NN) + vec[1, 5:6, :]))
    r.mixed[...] = c_n2 * vec[1, 6:7, :] + vec[1, 7:8, :]
    r.pump(9)
    g = r.c_cot[...]
    sums = {6: col_sum(g * c_n2), 7: col_sum(g)}
    dr2 = norm_backward(g * vec[1, 6:7, :], c_n2, c_inv2)
    dffn = dr2.astype(BF16)
    for part in range(hidden // width):
        cols = slice(part * width, (part + 1) * width)
        r.c_dpre[:, cols] = (dot(dffn, r.b_down[cols, :], NT) * r.c_slope[:, cols].astype(F32)).astype(BF16)
    weight_copy(r, 0, 3).start()
    r.pump(10)
    c_grad = dr2 + dot(r.c_dpre[...], r.b_up[...], NT)
    weight_copy(r, 0, 2).start()
    r.pump(11)
    sums[3] = col_sum(c_grad * c_n1)
    sums[4] = col_sum(c_grad)
    sums[5] = col_sum(dffn)
    dr1 = norm_backward(c_grad * vec[1, 3:4, :], c_n1, c_inv1)
    dattn = dr1.astype(BF16)
    d_context = dot(dattn, r.b_out[...], NT).astype(BF16)
    weight_copy(r, 0, 1).start()
    d_parts = []
    for (at, n), (query, prob, prob_low) in zip(blocks, attention):
        here = slice(at, at + n)
        down = head_rows(d_context[here], heads_n)
        dp = dot(down, r.c_qkv[here, 2 * width : 3 * width], NT)
        ds = (prob * (dp - jnp.sum(prob * dp, axis=-1, keepdims=True))).astype(BF16)
        dv = dot(prob_low, down, TN).astype(BF16)
        dq = (head_join(dot(ds, r.c_qkv[here, width : 2 * width], NN), heads_n) * SCALE).astype(BF16)
        dk = (dot(ds, query, TN) * SCALE).astype(BF16)
        d_parts.append(jnp.concatenate([dq, dk, dv], axis=1))
    c_dqkv = d_parts[0] if len(d_parts) == 1 else jnp.concatenate(d_parts, axis=0)
    sums[0] = col_sum(c_dqkv[:, 0:width])
    sums[1] = col_sum(c_dqkv[:, 2 * width : 3 * width])
    sums[2] = col_sum(dattn)
    r.pump(12)
    dh = dr1 + dot(c_dqkv, r.b_qkv[...], NT)
    weight_copy(r, 0, 0).start()
    r.pump(13)
    r.end_zero()
    for s in range(segs):
        for d in range(docs):
            at = d * segs + s
            r.z_inv[at : at + 1, :] = r.every_zero[s, d : d + 1, :]
    z_n2, z_inv2 = r.zeros[1], r.z_inv[:, 0:1]
    z_sums = {6: col_sum(dh * z_n2), 7: col_sum(dh)}
    z_dr2 = norm_backward(dh * vec[0, 6:7, :], z_n2, z_inv2)
    z_dffn = z_dr2.astype(BF16)
    z_sums[5] = col_sum(z_dffn)
    z_low = r.zeros[0].astype(BF16)
    r.pack_x[...] = jnp.zeros_like(r.pack_x)
    r.pack_y[...] = jnp.zeros_like(r.pack_y)
    r.pack_c[...] = jnp.zeros_like(r.pack_c)
    total = dh[0:segs]
    for d in range(1, docs):
        total = total + dh[d * segs : (d + 1) * segs]
    for b in range(8):
        cols = slice(b * 96, (b + 1) * 96)
        r.pack_x[b, :, 0:96] = base_low[:, cols]
        r.pack_x[b, :, 128:224] = context[:, cols]
        r.pack_x[b, :, 256:352] = c_low[:, cols]
        r.pack_x[b, :, 384:768] = r.c_act[:, b * 384 : (b + 1) * 384]
        r.pack_x[b, :, 768:864] = z_low[:, cols]
        r.pack_p[b] = jnp.zeros_like(r.pack_p[b])
        r.pack_p[b, :, 0:96] = total[:, cols]
    put_sums(r.pack_c.at[:, 0:16], sums)
    put_bias_sums(r.pack_c.at[:, 0:16], r.c_dpre)
    for b in range(4):
        r.pack_y[b, :, 0:576] = c_dqkv[:, b * 576 : (b + 1) * 576]
        r.pack_y[b, :, 640:832] = dattn[:, b * 192 : (b + 1) * 192]
        r.pack_y[b, :, 896:1664] = r.c_dpre[:, b * 768 : (b + 1) * 768]
        r.pack_y[b, :, 1664:1856] = dffn[:, b * 192 : (b + 1) * 192]
        r.pack_y[b, :, 2688:2880] = z_dffn[:, b * 192 : (b + 1) * 192]
    weight_copy(r, 0, 2).wait()
    for part in range(hidden // width):
        cols = slice(part * width, (part + 1) * width)
        value, grad = gelu_pair(dot(z_low, r.b_up[:, cols], NN) + fbias[0:1, cols])
        r.c_act[:, cols] = value.astype(BF16)
        r.c_slope[:, cols] = grad.astype(r.c_slope.dtype)
    for b in range(8):
        r.pack_x[b, :, 896:1280] = r.c_act[:, b * 384 : (b + 1) * 384]
    r.pump(14)
    weight_copy(r, 0, 3).wait()
    for part in range(hidden // width):
        cols = slice(part * width, (part + 1) * width)
        r.c_dpre[:, cols] = (dot(z_dffn, r.b_down[cols, :], NT) * r.c_slope[:, cols].astype(F32)).astype(BF16)
        r.pack_y[part, :, 1920:2688] = r.c_dpre[:, cols]
    put_sums(r.pack_c.at[:, 16:32], z_sums)
    put_bias_sums(r.pack_c.at[:, 16:32], r.c_dpre)
    r.pump(15)
    r.c_in[...] = z_dr2 + dot(r.c_dpre[...], r.b_up[...], NT)
    r.pump(16)
    exchange = []
    half_y = pl.ds(pl.multiple_of(lax.rem(r.me, 2) * 1536, 128), 1536)
    local = fetch([(r.pack_x.at[r.me], r.rows_x.at[r.doc]), (r.pack_y.at[r.doc], r.rows_y.at[r.doc])], r.local_sem)
    for step in range(1, 4):
        there = r.doc_peer(step)
        pair = [
            (r.pack_x.at[r.me], r.rows_x.at[r.doc]),
            (r.pack_y.at[there[0], :, half_y], r.rows_y.at[r.doc, :, half_y]),
        ]
        for i, (src, dst) in enumerate(pair):
            copy = pltpu.make_async_remote_copy(
                src_ref=src,
                dst_ref=dst,
                send_sem=r.x_send.at[step, i],
                recv_sem=r.x_recv.at[step, i],
                device_id=there,
                device_id_type=MESH,
            )
            copy.start()
            exchange.append(copy)
    r.inputs_ready()
    top = lax.broadcasted_iota(jnp.int32, (SEG, width), 0) == 0
    top_low = lax.broadcasted_iota(jnp.int32, (16, width), 0) == 0
    grads = []
    for g in range(groups):
        here = slice(g * SEG, (g + 1) * SEG)
        own = pl.ds(g * segs + r.seg, 1)
        tile = slice(g * SEG, g * SEG + 16)
        r.output[tile, :] = jnp.where(top_low, r.mixed[own, :], r.output[tile, :].astype(F32)).astype(BF16)
        grads.append(jnp.where(top, r.c_in[own, :], r.dh1[here, :]))
    grad = jnp.concatenate(grads, axis=0)
    normed = r.n1[...]
    sums = {3: col_sum(grad * normed), 4: col_sum(grad)}
    dr1 = norm_backward(grad * vec[0, 3:4, :], normed, r.inv1[:, 0:1])
    dattn = dr1.astype(BF16)
    sums[2] = col_sum(dattn)
    r.grad_tok[...] = dr1
    low = lane_halves(rows)
    for d in range(4):
        mid = dattn[:, (3 * (d // 2) + 1) * 128 : (3 * (d // 2) + 2) * 128]
        whole = 3 * (d // 2) + 2 * (d % 2)
        fill = jnp.zeros_like(mid)
        r.y_out[:, d * 256 : d * 256 + 128] = dattn[:, whole * 128 : (whole + 1) * 128]
        r.y_out[:, d * 256 + 128 : d * 256 + 256] = (
            jnp.where(low, mid, fill) if d % 2 == 0 else jnp.where(low, fill, mid)
        )
    weight_copy(r, 0, 1).wait()
    r.dctx[...] = dot(dattn, r.b_out[...], NT).astype(BF16)

    def put(chunk, b, d, at, value):
        slot = slot_of(ATT_ORDERS[chunk], relative(b, d, r.me, r.doc))
        r.a_parts[chunk, slot, :, at : at + value.shape[1]] = value.astype(BF16)

    def begin(*chunks):
        for chunk in chunks:
            r.att.send(0, chunk, r.a_parts.at[chunk, pl.ds(16, 16)])

    def strips(tile, b, i):
        at = b * 96 + i * 32
        return tile[at : at + 16], tile[at + 16 : at + 32]

    def side_by_side(d, upper, lower):
        if d % 2 == 0:
            return upper + pltpu.roll(lower, HEAD, 1)
        return pltpu.roll(upper, HEAD, 1) + lower

    for d in range(4):
        tile = dot(r.ctx[...], r.y_out[:, d * 256 : d * 256 + 256], TN)
        for b in range(8):
            for i in range(3):
                upper, lower = strips(tile, b, i)
                put(9 + i, b, d, 0, upper[:, 0:128])
                put(9 + i, b, d, 128, lower[:, 0:128])
                put(9 + i, b, d, 256, side_by_side(d, upper[:, 128:256], lower[:, 128:256]))
    begin(9, 10, 11)
    r.pump(17)
    pairs = width // 128
    half = lane_halves(SEG)
    for g in range(groups):
        here = slice(g * SEG, (g + 1) * SEG)
        for pair in range(pairs):
            at = pair * 128
            prob = r.probs[g * pairs + pair]
            down = two_heads(r.dctx[here, at : at + 128])
            query = two_heads(r.qkv[here, at : at + 128])
            key = two_heads(r.qkv[here, width + at : width + at + 128])
            dp = dot(down, r.qkv[here, 2 * width + at : 2 * width + at + 128], NT)
            dv = dot(prob.astype(BF16), down, TN)
            ds = (prob * (dp - jnp.sum(prob * dp, axis=-1, keepdims=True))).astype(BF16)
            dq = dot(jnp.concatenate([ds[:SEG], ds[SEG:]], axis=1), key, NN) * SCALE
            dk = dot(ds, query, TN) * SCALE
            for kind, value in enumerate((dq, dk, dv)):
                value = value.astype(BF16)
                r.dqkv[here, kind * width + at : kind * width + at + 128] = value
                slab = kind * pairs + pair
                d, tile = slab // 9 * 2, slab % 9
                if tile < 4:
                    r.y_qkv[here, d * 640 + tile * 128 : d * 640 + tile * 128 + 128] = value
                elif tile > 4:
                    r.y_qkv[here, d * 640 + tile * 128 : d * 640 + tile * 128 + 128] = value
                else:
                    zero = jnp.zeros_like(value)
                    r.y_qkv[here, d * 640 + 512 : d * 640 + 640] = jnp.where(half, value, zero)
                    r.y_qkv[here, d * 640 + 1152 : d * 640 + 1280] = jnp.where(half, zero, value)
            if pair % 3 == 2:
                r.pump(18 + 2 * g + pair // 3)
    for d in range(4):
        tile = dot(tok[...], r.y_qkv[:, d * 640 : d * 640 + QC], TN)
        for b in range(8):
            for i in range(3):
                upper, lower = strips(tile, b, i)
                put(3 * i, b, d, 0, upper)
                put(3 * i + 1, b, d, 128, lower[:, 0:256])
                put(3 * i + 2, b, d, 0, lower[:, 256:QC])
    begin(0, 3, 6)
    r.pump(22)
    for d in range(4):
        tile = dot(tok[...], r.y_qkv[:, d * 640 + QC : d * 640 + 640], TN)
        for b in range(8):
            for i in range(3):
                upper, lower = strips(tile, b, i)
                put(3 * i + 1, b, d, 0, upper[:, 0:128])
                put(3 * i + 2, b, d, 128, lower[:, 0:128])
                put(3 * i + 2, b, d, 256, side_by_side(d, upper[:, 128:256], lower[:, 128:256]))
    begin(1, 2, 4, 5, 7, 8)
    r.pump(23)
    sums[0] = col_sum(r.dqkv[:, 0:width])
    sums[1] = col_sum(r.dqkv[:, 2 * width : 3 * width])
    put_sums(r.pack_v, sums)

    def vec_copy(step):
        there = r.seg_peer(step)
        return pltpu.make_async_remote_copy(
            src_ref=r.pack_v.at[there[1] // r.stride],
            dst_ref=r.vec_got.at[r.seg],
            send_sem=r.v_send.at[step],
            recv_sem=r.v_recv.at[step],
            device_id=there,
            device_id_type=MESH,
        )

    def vec_begin(step, carry):
        vec_copy(step).start()
        return carry

    def vec_finish(step, carry):
        vec_copy(step).wait()
        return carry

    lax.fori_loop(1, r.count, vec_begin, 0)
    own_vec = pltpu.make_async_copy(r.pack_v.at[r.me], r.vec_got.at[r.seg], r.local_sem.at[2])
    own_vec.start()
    weight_copy(r, 0, 0).wait()
    r.grad_tok[...] = r.grad_tok[...] + dot(r.dqkv[:, 0 : 3 * width], r.b_qkv[...], NT)
    r.pump(24)
    r.run(LATE)
    for copy in exchange:
        copy.wait()
    exchange = []
    for step in range(1, 4):
        there = r.doc_peer(step)[0]
        copy = pltpu.make_async_remote_copy(
            src_ref=r.rows_y.at[there, :, half_y],
            dst_ref=r.rows_y.at[there, :, half_y],
            send_sem=r.y_send.at[step],
            recv_sem=r.y_recv.at[step],
            device_id=r.partners["c"],
            device_id_type=MESH,
        )
        copy.start()
        exchange.append(copy)
    own_vec.wait()
    lax.fori_loop(1, r.count, vec_finish, 0)
    r.vec_one[0:16, :] = lax.fori_loop(
        0, r.count, lambda i, total: total + r.vec_got[i], r.pack_c[r.me, 16:32, :]
    )
    r.vec_one[16:32, :] = r.pack_c[r.me, 0:16, :]
    r.vec_one[32:, :] = r.pack_p[r.me]
    own_vec = pltpu.make_async_copy(r.vec_one, r.vec_all.at[r.doc], r.local_sem.at[3])
    own_vec.start()
    for step in range(1, 4):
        copy = pltpu.make_async_remote_copy(
            src_ref=r.vec_one,
            dst_ref=r.vec_all.at[r.doc],
            send_sem=r.s_send.at[step],
            recv_sem=r.s_recv.at[step],
            device_id=r.doc_peer(step),
            device_id_type=MESH,
        )
        copy.start()
        exchange.append(copy)
    r.run(len(STEPS))
    for copy in exchange + local:
        copy.wait()
    own_vec.wait()
    r.vec_sum[...] = r.vec_all[0] + r.vec_all[1] + r.vec_all[2] + r.vec_all[3]
    r.ffn.finish()
    r.att.finish()


def refs_of(r, names, refs):
    for name, ref in zip(names, refs, strict=True):
        setattr(r, name, ref)


WEIGHTS = ("b_qkv", "b_out", "b_up", "b_down")
SAVED = ("qkv", "probs", "ctx", "n1", "inv1", "dh1", "first")
ACTS = ("h1", "act", "slope", "dffn", "dpre")


def sizes(rows, width, hidden, segs):
    groups = rows // SEG
    c_rows = groups * segs
    dma = pltpu.SemaphoreType.DMA
    table = {
        "b_qkv": ((width, 3 * width), BF16),
        "b_out": ((width, width), BF16),
        "b_up": ((width, hidden), BF16),
        "b_down": ((hidden, width), BF16),
        "qkv": ((rows, 3 * width), BF16),
        "probs": ((groups * width // 128, 2 * SEG, SEG), F32),
        "ctx": ((rows, width), BF16),
        "n1": ((rows, width), F32),
        "inv1": ((rows, 128), F32),
        "dh1": ((rows, width), F32),
        "first": ((rows, width), BF16),
        "h1": ((rows, width), BF16),
        "act": ((rows, hidden), BF16),
        "slope": ((rows, hidden), BF16),
        "dffn": ((rows, width), BF16),
        "dpre": ((rows, hidden), BF16),
        "parts": ((8, 32, QR, QC), BF16),
        "heads": ((4 * groups, width), BF16),
        "rows_zero": ((8, 128), F32),
        "pack_v": ((8, 16, 128), F32),
        "output": ((rows, width), BF16),
        "grad_tok": ((rows, width), F32),
        "ffn_shares": ((8, QR, QC), F32),
        "att_shares": ((12, 16, QC), F32),
        "rows_x": ((4, c_rows, 1280), BF16),
        "rows_y": ((4, c_rows, 3072), BF16),
        "vec_all": ((4, 32 + segs, 128), F32),
        "vec_sum": ((32 + segs, 128), F32),
        "every": ((segs, 4 * groups, width), BF16),
        "every_zero": ((segs, 8, 128), F32),
        "c_qkv": ((c_rows, 3 * width), BF16),
        "c_in": ((c_rows, width), F32),
        "c_cot": ((c_rows, width), F32),
        "c_act": ((c_rows, hidden), BF16),
        "c_slope": ((c_rows, hidden), F32 if c_rows <= 16 else BF16),
        "c_dpre": ((c_rows, hidden), BF16),
        "mixed": ((c_rows, width), F32),
        "zeros": ((2, c_rows, width), F32),
        "z_inv": ((c_rows, 128), F32),
        "pack_x": ((8, c_rows, 1280), BF16),
        "pack_y": ((4, c_rows, 3072), BF16),
        "pack_c": ((8, 32, 128), F32),
        "pack_p": ((8, segs, 128), F32),
        "dctx": ((rows, width), BF16),
        "vec_got": ((segs, 16, 128), F32),
        "vec_one": ((32 + segs, 128), F32),
        "a_parts": ((12, 32, 16, QC), BF16),
        "f_staged": ((2, 16, QR, QC), BF16),
        "y_qkv": ((rows, 2560), BF16),
        "y_out": ((rows, 1024), BF16),
        "dqkv": ((rows, 3 * width), BF16),
    }
    for i in range(5):
        table[f"f_got{i}"] = ((8, 16 >> i, QR, QC), BF16)
        table[f"a_got{i}"] = ((12, 16 >> i, 16, QC), BF16)
    sems = {
        "w_sem": (4,), "third_sem": (3,), "in_sem": (7,), "load_sem": (8,), "out_sem": (9,), "h_send": (segs,), "h_recv": (segs,),
        "z_send": (segs,), "z_recv": (segs,), "f_send": (5, 8), "f_recv": (5, 8), "a_send": (5, 12),
        "a_recv": (5, 12), "x_send": (4, 2), "x_recv": (4, 2), "v_send": (segs,), "v_recv": (segs,),
        "s_send": (4,), "s_recv": (4,), "y_send": (4,), "y_recv": (4,), "local_sem": (4,),
    }
    return table, {name: dma(shape) for name, shape in sems.items()}


REST_OUT = ("output", "grad_tok", "ffn_shares", "att_shares", "rows_x", "rows_y", "vec_all", "vec_sum")
REST_SCRATCH = (
    ("every", "every_zero", "c_qkv", "c_in", "c_cot", "c_act", "c_slope", "c_dpre", "mixed", "zeros", "z_inv")
    + ("pack_x", "pack_y", "pack_c", "pack_p", "dctx", "vec_got", "vec_one", "a_parts")
    + tuple(f"f_got{i}" for i in range(5))
    + tuple(f"a_got{i}" for i in range(5))
)
REST_SEMS = (
    ("w_sem", "in_sem", "load_sem", "h_send", "h_recv", "z_send", "z_recv", "f_send", "f_recv", "a_send", "a_recv")
    + ("x_send", "x_recv", "v_send", "v_recv", "s_send", "s_recv", "y_send", "y_recv", "local_sem")
)
W_NAMES = ("w_qkv", "w_out", "w_up", "w_down")


def call(body, name, ins, in_specs, outs, out_specs, scratch, table, sems, collective, args):
    shape = jax.ShapeDtypeStruct
    return pl.pallas_call(
        body,
        out_shape=tuple(shape(*table[n]) for n in outs),
        in_specs=in_specs,
        out_specs=out_specs,
        scratch_shapes=[sems[n] if n in sems else pltpu.VMEM(*table[n]) for n in scratch],
        compiler_params=pltpu.CompilerParams(
            vmem_limit_bytes=LIMIT,
            **(dict(collective_id=0, has_side_effects=True) if collective else {}),
        ),
        name=name,
    )(*args)


def run_whole(stride, segs, counts, tok, mask, cot, pos, vec, fbias, weights):
    rows, width = tok.shape
    table, sems = sizes(rows, width, weights[2].shape[2], segs)
    ins = ("counts", "tok", "mask", "cot", "pos", "vec", "fbias") + W_NAMES
    kept = SAVED[:-1] + ACTS + ("parts", "heads", "rows_zero", "pack_v")
    scratch = WEIGHTS + kept + REST_SCRATCH + REST_SEMS + ("third_sem",)

    def body(*refs):
        r = SimpleNamespace(stride=stride, count=segs)
        refs_of(r, ins + REST_OUT + scratch, refs)
        r.first = r.output
        r.y_qkv, r.y_out, r.dqkv = r.dpre, r.act, r.slope
        enter = connect(r)
        r.leave = lambda name: None
        r.used = lambda i: weight_copy(r, 1, i).start()
        r.inputs_ready = lambda: None

        def heads_ready():
            enter()
            share_rows(r)

        def parts_ready(first, last):
            for chunk in range(first, last):
                r.ffn.send(0, chunk, r.parts.at[chunk, pl.ds(16, 16)])

        r.heads_ready = heads_ready
        r.parts_ready = parts_ready
        forward_phase(r)
        rest_phase(r)

    return call(
        body, "whole_step", ins, [SM] + [VM] * 6 + [ANY] * 4, REST_OUT, (VM,) * 8, scratch, table, sems, True,
        (counts, tok, mask, cot, pos, vec, fbias) + weights,
    )


def run_halves(stride, segs, counts, tok, mask, cot, pos, vec, fbias, weights):
    rows, width = tok.shape
    table, sems = sizes(rows, width, weights[2].shape[2], segs)
    ins = ("tok", "mask", "cot", "vec", "fbias") + W_NAMES
    outs = tuple("o_" + n for n in SAVED) + ("o_parts", "heads", "rows_zero", "pack_v")
    for n in SAVED + ("parts",):
        table["o_" + n] = table[n]
    scratch = WEIGHTS + SAVED + ACTS + ("parts", "w_sem", "third_sem", "out_sem")

    def first_body(*refs):
        r = SimpleNamespace(stride=stride, count=segs)
        refs_of(r, ins + outs + scratch, refs)
        position(r)
        leaving = []

        def go(src, dst):
            copy = pltpu.make_async_copy(src, dst, r.out_sem.at[len(leaving)])
            copy.start()
            leaving.append(copy)

        r.leave = lambda name: go(getattr(r, name), getattr(r, "o_" + name))
        r.parts_ready = lambda a, b: go(r.parts.at[a:b], r.o_parts.at[a:b])
        r.used = lambda i: None
        r.pump = lambda i: None
        r.heads_ready = lambda: None
        forward_phase(r)
        for copy in leaving:
            copy.wait()

    *saved, parts, heads, rows_zero, pack_v = call(
        first_body, "segment_forward", ins, [VM] * 5 + [ANY] * 4, outs, (ANY,) * 8 + (VM,) * 3, scratch, table, sems,
        False, (tok, mask, cot, vec, fbias) + weights,
    )
    ins_b = ("counts", "heads", "rows_zero", "tok", "pack_v", "pos", "vec", "fbias", "i_parts")
    ins_b = ins_b + tuple("i_" + n for n in SAVED) + W_NAMES
    scratch_b = WEIGHTS + SAVED[:-1] + REST_SCRATCH + ("f_staged", "y_qkv", "y_out", "dqkv") + REST_SEMS

    def second_body(*refs):
        r = SimpleNamespace(stride=stride, count=segs)
        refs_of(r, ins_b + REST_OUT + scratch_b, refs)
        for i in range(4):
            weight_copy(r, 1, i).start()
        enter = connect(r)
        enter()
        share_rows(r)
        for chunk in range(8):
            r.ffn.send(0, chunk, r.i_parts.at[chunk, pl.ds(16, 16)])
        for chunk in range(2):
            r.ffn.load(chunk, r.i_parts, r.load_sem)
        r.first = r.output
        inputs = fetch([(getattr(r, "i_" + n), getattr(r, n)) for n in SAVED], r.in_sem)

        def inputs_ready():
            for copy in inputs:
                copy.wait()

        r.inputs_ready = inputs_ready
        rest_phase(r)

    return call(
        second_body, "the_rest", ins_b, [SM] + [VM] * 7 + [ANY] * 12, REST_OUT, (VM,) * 4 + (ANY,) * 2 + (VM,) * 2,
        scratch_b, table, sems, True,
        (counts, heads, rows_zero, tok, pack_v, pos, vec, fbias, parts, *saved) + weights,
    )


def assemble(
    stride, ffn, att, rows_x, rows_y, sums, i_output, i_grad, g_qkv, g_out, g_up, g_down, g_vec, g_bias, g_pos,
    output, grad_tok,
):
    output[...] = i_output[...]
    grad_tok[...] = i_grad[...]
    rows = rows_x.shape[0] * rows_x.shape[1]
    doc = lax.axis_index("doc")
    x = rows_x[...].reshape(rows, rows_x.shape[2])
    y = rows_y[...].reshape(rows, rows_y.shape[2])
    g_qkv[1] = dot(x[:, 0:128], y[:, 0:640], TN)[0:96, 0:576]
    g_out[1] = dot(x[:, 128:256], y[:, 640:896], TN)[0:96, 0:192]
    g_up[1] = dot(x[:, 256:384], y[:, 896:1664], TN)[0:96, :]
    g_down[1] = dot(y[:, 1664:1920], x[:, 384:768], TN)[0:192]
    more = dot(x[:, 768:896], y[:, 1920:2688], TN)
    for r in range(2):
        at = slice(r * QR, (r + 1) * QR)
        for c in range(2):
            cols = slice(c * QC, (c + 1) * QC)
            g_up[0, at, cols] = ffn[4 + 2 * r + c] + more[at, cols]
    tall = jnp.concatenate([ffn[0], ffn[1], ffn[2], ffn[3]], axis=0)
    g_down[0] = tall + dot(y[:, 2688:2944], x[:, 896:1280], TN)[0:192]
    even = lax.rem(doc, 2) == 0
    for i in range(3):
        one, two, three, out = att[3 * i], att[3 * i + 1], att[3 * i + 2], att[9 + i]
        slabs = (
            jnp.concatenate([one, two[:, 0:128]], axis=1),
            jnp.concatenate([two[:, 128:384], three[:, 0:256]], axis=1),
        )
        for k in range(2):
            at = slice(32 * i + 16 * k, 32 * i + 16 * k + 16)
            side = slice(256 + 64 * k, 320 + 64 * k)
            whole = out[:, 128 * k : 128 * k + 128]

            @pl.when(even)
            def _():
                g_qkv[0, at, 0:512] = slabs[k]
                g_qkv[0, at, 512:576] = three[:, side]
                g_out[0, at, 0:128] = whole
                g_out[0, at, 128:192] = out[:, side]

            @pl.when(jnp.logical_not(even))
            def _():
                g_qkv[0, at, :] = jnp.concatenate([three[:, side], slabs[k]], axis=1)
                g_out[0, at, :] = jnp.concatenate([out[:, side], whole], axis=1)

    if stride > 1:
        for layer in range(2):
            g_vec[layer] = sums[16 * layer : 16 * layer + 8, 0:96]
            g_bias[layer] = sums[16 * layer + 8 : 16 * layer + 12, 0:96]
    else:
        for layer in range(2):
            g_vec[layer] = sums[pl.ds(16 * layer + 2 * doc, 2), 0:96]
            for i in range(4):
                at = 16 * layer + 8 + i
                g_bias[layer : layer + 1, i * 96 : i * 96 + 96] = sums[at : at + 1, 0:96]
    g_pos[...] = sums[32:, 0:96]


def run_assemble(stride, ffn, att, rows_x, rows_y, sums, output, grad_tok):
    shape = jax.ShapeDtypeStruct
    return pl.pallas_call(
        functools.partial(assemble, stride),
        out_shape=(
            shape((2, 96, 576), F32),
            shape((2, 96, 192), F32),
            shape((2, 96, 768), F32),
            shape((2, 192, 384), F32),
            shape((2, 2, 96) if stride == 1 else (2, 8, 96), F32),
            shape((2, 384) if stride == 1 else (2, 4, 96), F32),
            shape((sums.shape[0] - 32, 96), F32),
            shape(output.shape, BF16),
            shape(grad_tok.shape, F32),
        ),
        in_specs=[VM] * 7,
        out_specs=(VM,) * 9,
        compiler_params=pltpu.CompilerParams(vmem_limit_bytes=LIMIT),
        name="assemble",
    )(ffn, att, rows_x, rows_y, sums, output, grad_tok)


def shards(
    tokens,
    token_mask,
    doc_counts,
    w_qkv,
    w_out,
    w_up,
    w_down,
    vectors,
    ffn_bias,
    pos_embed,
    cotangent,
):
    docs, slots, width = tokens.shape
    seg_dev = slots // SEG
    groups = docs * seg_dev
    count = lax.axis_size("seg")
    stride = count // 8
    rest = lax.rem(lax.axis_index("seg"), stride)
    tok = tokens.reshape(groups * SEG, width)
    cot = cotangent.reshape(groups * SEG, width)
    weights = (w_qkv, w_out, w_up, w_down)
    run = run_whole if groups * count <= 16 else run_halves
    output, grad_tok, ffn, att, rows_x, rows_y, _, sums = run(
        stride, count, doc_counts, tok, token_mask.reshape(groups, SEG), cot, pos_embed, vectors, ffn_bias, weights
    )
    g_qkv, g_out, g_up, g_down, g_vec, g_bias, g_pos, output, grad_tok = run_assemble(
        stride, ffn, att, rows_x, rows_y, sums, output, grad_tok
    )
    g_down = jnp.transpose(g_down, (0, 2, 1))
    if stride > 1:
        lanes = [[i * stride + j for j in range(stride)] for i in range(8)]

        def own(arr, dim):
            low = lax.psum_scatter(arr[0:1], "seg", scatter_dimension=dim, axis_index_groups=lanes, tiled=True)
            size = arr.shape[dim] // stride
            return jnp.concatenate([low, lax.dynamic_slice_in_dim(arr[1:2], rest * size, size, dim)], axis=0)

        g_qkv, g_out, g_up, g_down = own(g_qkv, 1), own(g_out, 1), own(g_up, 1), own(g_down, 1)
        each = 96 // stride
        g_vec = lax.dynamic_slice(g_vec, (0, lax.axis_index("doc") * 2, rest * each), (2, 2, each))
        g_bias = lax.dynamic_slice_in_dim(g_bias.reshape(2, 384), rest * (384 // stride), 384 // stride, 1)
        g_pos = lax.dynamic_slice_in_dim(g_pos, rest * each, each, 1)
    return (
        output.reshape(tokens.shape),
        grad_tok.reshape(tokens.shape),
        g_qkv,
        g_out,
        g_up,
        g_down,
        g_vec,
        g_bias,
        g_pos,
    )


def solution(mesh):
    return jax.shard_map(
        shards,
        mesh=mesh,
        in_specs=(
            P("doc", "seg", None),
            P("doc", "seg"),
            P("doc"),
            P(),
            P(),
            P(),
            P(),
            P(),
            P(),
            P(),
            P("doc", "seg", None),
        ),
        out_specs=(
            P("doc", "seg", None),
            P("doc", "seg", None),
            P(None, "seg", "doc"),
            P(None, "seg", "doc"),
            P(None, "seg", "doc"),
            P(None, "seg", "doc"),
            P(None, "doc", "seg"),
            P(None, "seg"),
            P(None, "seg"),
        ),
        check_vma=False,
    )
```

```python
import functools
from types import SimpleNamespace

import jax
import jax.numpy as jnp
from jax import lax
from jax.experimental import pallas as pl
from jax.experimental.pallas import tpu as pltpu
from jax.sharding import PartitionSpec as P

MESH = pl.DeviceIdType.MESH
HEAD = 64
SEG = 128
NEG = -1e30
EPS = 1e-05
ROOT_HALF = 0.7071067811865476
INV_ROOT_TWO_PI = 0.3989422804014327
SCALE = HEAD ** (-0.5)
F32 = jnp.float32
BF16 = jnp.bfloat16
VM = pl.BlockSpec(memory_space=pltpu.VMEM)
SM = pl.BlockSpec(memory_space=pltpu.SMEM)
ANY = pl.BlockSpec(memory_space=pl.ANY)
LIMIT = 62 << 20
QR, QC = 48, 384
NN = (((1,), (0,)), ((), ()))
NT = (((1,), (1,)), ((), ()))
TN = (((0,), (0,)), ((), ()))


def dot(a, b, dims):
    return lax.dot_general(a, b, dims, preferred_element_type=F32)


def norm_forward(resid):
    cent = resid - jnp.mean(resid, axis=-1, keepdims=True)
    inv = lax.rsqrt(jnp.mean(cent * cent, axis=-1, keepdims=True) + EPS)
    return cent * inv, inv


def norm_backward(scaled, normed, inv):
    inner = jnp.mean(scaled * normed, axis=-1, keepdims=True)
    return inv * (scaled - jnp.mean(scaled, axis=-1, keepdims=True) - normed * inner)


def gelu_pair(pre):
    half_cdf = 0.5 * (1.0 + lax.erf(pre * ROOT_HALF))
    slope = half_cdf + pre * jnp.exp(-0.5 * pre * pre) * INV_ROOT_TWO_PI
    return pre * half_cdf, slope


def col_sum(arr):
    return jnp.sum(arr.astype(F32), axis=0, keepdims=True)


def softmax_rows(scores):
    expo = jnp.exp(scores - jnp.max(scores, axis=-1, keepdims=True))
    return expo / jnp.sum(expo, axis=-1, keepdims=True)


def lane_halves(rows):
    lane = lax.broadcasted_iota(jnp.int32, (rows, 128), 1)
    return lane < HEAD


def two_heads(slab):
    low = lane_halves(slab.shape[0])
    zero = jnp.zeros_like(slab)
    return jnp.concatenate([jnp.where(low, slab, zero), jnp.where(low, zero, slab)], axis=0)


def fetch(pairs, sem):
    copies = [pltpu.make_async_copy(src, dst, sem.at[i]) for i, (src, dst) in enumerate(pairs)]
    for copy in copies:
        copy.start()
    return copies


def xor_bit(a, b):
    return a + b - 2 * a * b


FFN_ORDERS = (
    "xyab", "yaxb", "abxy", "xyab", "axyb", "yabx", "xayb", "yxab",
)
ATT_ORDERS = (
    "yabx", "xyab", "xyab", "xyab", "xyab", "xyab", "xayb", "abxy", "yaxb", "yxab", "yabx", "xayb",
)


def relative(b, d, me, doc):
    return {
        "c": xor_bit(lax.rem(me, 2), b % 2),
        "x": xor_bit(lax.rem(doc, 2), d % 2),
        "y": xor_bit(doc // 2, d // 2),
        "a": xor_bit(lax.rem(me // 2, 2), (b // 2) % 2),
        "b": xor_bit(me // 4, b // 4),
    }


def slot_of(order, bits):
    return sum(bits[name] * (16 >> i) for i, name in enumerate("c" + order))


def first_rows(rows, width):
    return lax.rem(lax.broadcasted_iota(jnp.int32, (rows, width), 0), SEG) == 0


def put_bias_sums(pack_v, dpre):
    for b in range(8):
        for i in range(4):
            at = b * 384 + i * 96
            pack_v[b, 8 + i : 9 + i, 0:96] = col_sum(dpre[:, at : at + 96])


def put_sums(pack_v, sums):
    for b in range(8):
        for i, value in sums.items():
            pack_v[b, i : i + 1, 0:96] = value[:, b * 96 : (b + 1) * 96]


def head_rows(arr, heads):
    rows, width = arr.shape
    lane = lax.broadcasted_iota(jnp.int32, (rows, width), 1)
    zero = jnp.zeros_like(arr)
    parts = [jnp.where(lane // HEAD == h, arr, zero) for h in range(heads)]
    return jnp.concatenate(parts, axis=0)


def head_join(arr, heads):
    rows = arr.shape[0] // heads
    lane = lax.broadcasted_iota(jnp.int32, (rows, arr.shape[1]), 1)
    out = jnp.zeros((rows, arr.shape[1]), F32)
    for h in range(heads):
        out = jnp.where(lane // HEAD == h, arr[h * rows : (h + 1) * rows], out)
    return out


class Halving:
    def __init__(self, orders, kept, got, shares, partners, send_sem, recv_sem, staged=None):
        self.orders, self.kept, self.got, self.shares, self.staged = orders, kept, got, shares, staged
        self.partners, self.send_sem, self.recv_sem = partners, send_sem, recv_sem
        self.sends = {}
        self.loads = []

    def send(self, stage, chunk, src):
        copy = pltpu.make_async_remote_copy(
            src_ref=src,
            dst_ref=self.got[stage].at[chunk],
            send_sem=self.send_sem.at[stage, chunk],
            recv_sem=self.recv_sem.at[stage, chunk],
            device_id=self.partners[("c" + self.orders[chunk])[stage]],
            device_id_type=MESH,
        )
        copy.start()
        self.sends[stage, chunk] = copy

    def load(self, chunk, source, sem):
        copy = pltpu.make_async_copy(source.at[chunk, pl.ds(0, 16)], self.staged.at[chunk % 2], sem.at[chunk])
        copy.start()
        self.loads.append(copy)

    def add(self, stage, chunk, first, last):
        kept = self.kept
        more = self.got[stage].at[chunk]
        if stage == 0 and self.staged is not None:
            more = self.staged.at[chunk % 2]

        kept[chunk, first:last] = kept[chunk, first:last] + more[first:last]

    def step(self, stage, chunk):
        if stage == 0 and self.staged is not None:
            self.loads[chunk].wait()
        self.sends[stage, chunk].wait_recv()
        half = (16 >> stage) // 2
        if stage < 4:
            self.add(stage, chunk, half, 2 * half)
            self.send(stage + 1, chunk, self.kept.at[chunk, pl.ds(half, half)])
            if stage > 0:
                self.sends.pop((stage - 1, chunk)).wait_send()
            self.add(stage, chunk, 0, half)
        else:
            self.shares[chunk] = self.kept[chunk, 0].astype(F32) + self.got[4][chunk, 0].astype(F32)

    def finish(self):
        for copy in self.sends.values():
            copy.wait_send()


STEPS = (
    0, 1, 2, 3, 4, 6, 5, 7, 100, 101, 102, 103, 105, 104, 201, 106, 107, 204, 301, 200, 205, 1009, 1010, 202,
    1011, 203, 206, 401, 300, 1000, 207, 1003, 1006, 1001, 1002, 1004, 1005, 302, 304, 1007, 1008, 303, 305,
    1111, 1109, 400, 307, 1103, 1110, 404, 306, 1106, 1107, 1100, 1211, 1101, 403, 402, 1210, 407, 1102, 1108,
    1203, 1206, 406, 1311, 1104, 1201, 1200, 1202, 1207, 1105, 1306, 405, 1310, 1208, 1204, 1303, 1209, 1301,
    1307, 1411, 1205, 1410, 1302, 1308, 1300, 1304, 1406, 1407, 1309, 1403, 1305, 1401, 1400, 1402, 1408, 1404,
    1409, 1405,
)
PUMPS = (
    0, 1, 0, 1, 1, 2, 2, 1, 1, 1, 1, 0, 1, 2, 0, 2, 1, 1, 2, 5, 0, 1, 1, 0, 8,
)
LATE = 36


def weight_copy(r, layer, i):
    src = (r.w_qkv, r.w_out, r.w_up, r.w_down)[i]
    dst = (r.b_qkv, r.b_out, r.b_up, r.b_down)[i]
    return pltpu.make_async_copy(src.at[layer], dst, r.w_sem.at[i])


def position(r):
    r.seg = lax.axis_index("seg")
    r.doc = lax.axis_index("doc")
    r.me = r.seg // r.stride


def forward_phase(r):
    tok, vec, qkv = r.tok, r.vec, r.qkv
    rows, width = tok.shape
    groups = rows // SEG
    pairs = width // 128
    hidden = r.act.shape[1]
    thirds = []
    for part in range(3):
        cols = slice(part * width, (part + 1) * width)
        thirds.append(
            pltpu.make_async_copy(r.w_qkv.at[0, :, cols], r.b_qkv.at[:, cols], r.third_sem.at[part])
        )
        thirds[part].start()
    for i in range(1, 4):
        weight_copy(r, 0, i).start()
    for part in range(3):
        cols = slice(part * width, (part + 1) * width)
        thirds[part].wait()
        out = dot(tok[...], r.b_qkv[:, cols], NN)
        if part != 1:
            out = out + vec[0, part // 2 : part // 2 + 1, :]
        qkv[:, cols] = out.astype(BF16)
    r.leave("qkv")
    for g in range(groups):
        here = slice(g * SEG, (g + 1) * SEG)
        keep = r.mask[g : g + 1, :] > 0
        for pair in range(pairs):
            at = pair * 128
            query = two_heads(qkv[here, at : at + 128])
            scores = dot(query, qkv[here, width + at : width + at + 128], NT) * SCALE
            prob = softmax_rows(jnp.where(keep, scores, NEG))
            r.probs[g * pairs + pair] = prob
            low = prob.astype(BF16)
            side = jnp.concatenate([low[:SEG], low[SEG:]], axis=1)
            value = two_heads(qkv[here, 2 * width + at : 2 * width + at + 128])
            r.ctx[here, at : at + 128] = dot(side, value, NN).astype(BF16)
    r.leave("probs")
    r.leave("ctx")
    weight_copy(r, 0, 1).wait()
    resid = tok[...].astype(F32) + (dot(r.ctx[...], r.b_out[...], NN) + vec[0, 2:3, :])
    normed, inv = norm_forward(resid)
    r.n1[...] = normed
    r.inv1[...] = jnp.broadcast_to(inv, r.inv1.shape)
    r.leave("n1")
    r.leave("inv1")
    r.h1[...] = (normed * vec[0, 3:4, :] + vec[0, 4:5, :]).astype(BF16)
    weight_copy(r, 0, 2).wait()
    for part in range(hidden // width):
        cols = slice(part * width, (part + 1) * width)
        value, grad = gelu_pair(dot(r.h1[...], r.b_up[:, cols], NN) + r.fbias[0:1, cols])
        r.act[:, cols] = value.astype(BF16)
        r.slope[:, cols] = grad.astype(BF16)
    weight_copy(r, 0, 3).wait()
    r.used(0)
    r.used(1)
    first = r.n1[...] * vec[0, 3:4, :] + vec[0, 4:5, :]
    normed, inv = norm_forward(first + (dot(r.act[...], r.b_down[...], NN) + vec[0, 5:6, :]))
    r.first[...] = (normed * vec[0, 6:7, :] + vec[0, 7:8, :]).astype(BF16)
    r.leave("first")
    r.rows_zero[...] = jnp.zeros_like(r.rows_zero)
    starts = [g * SEG for g in range(groups)]
    tops = [r.first[at : at + 16, :].astype(F32)[0:1] for at in starts]
    tops += [r.cot[at : at + 16, :].astype(F32)[0:1] for at in starts]
    tops += [r.h1[at : at + 16, :].astype(F32)[0:1] for at in starts]
    tops += [normed[at : at + 1] for at in starts]
    r.heads[...] = jnp.concatenate(tops, axis=0).astype(BF16)
    for g, at in enumerate(starts):
        r.rows_zero[g : g + 1, :] = jnp.broadcast_to(inv[at : at + 1], (1, 128))
    r.heads_ready()
    grad = jnp.where(first_rows(rows, width), 0.0, r.cot[...].astype(F32))
    sums = {6: col_sum(grad * normed), 7: col_sum(grad)}
    dr2 = norm_backward(grad * vec[0, 6:7, :], normed, inv)
    r.dffn[...] = dr2.astype(BF16)
    r.dh1[...] = dr2
    sums[5] = col_sum(r.dffn[...])
    r.pack_v[...] = jnp.zeros_like(r.pack_v)
    put_sums(r.pack_v, sums)

    def place(chunk, b, d, value):
        slot = slot_of(FFN_ORDERS[chunk], relative(b, d, r.me, r.doc))
        r.parts[chunk, slot] = value.astype(BF16)

    for j in range(4):
        pieces = [dr2[:, d * 192 + j * QR : d * 192 + (j + 1) * QR] for d in range(4)]
        tile = dot(jnp.concatenate(pieces, axis=1).astype(BF16), r.act[...], TN)
        for d in range(4):
            for b in range(8):
                place(j, b, d, tile[d * QR : (d + 1) * QR, b * QC : (b + 1) * QC])
        r.parts_ready(j)
    for part in range(hidden // width):
        cols = slice(part * width, (part + 1) * width)
        r.dpre[:, cols] = (dot(r.dffn[...], r.b_down[cols, :], NT) * r.slope[:, cols].astype(F32)).astype(BF16)
        if part > 0:
            r.pump(part - 1)
    r.used(3)
    for half in range(2):
        for d in range(4):
            at = d * 768 + half * QC
            tile = dot(r.h1[...], r.dpre[:, at : at + QC], TN)
            for b in range(8):
                for top_half in range(2):
                    row = b * 96 + top_half * QR
                    place(4 + 2 * top_half + half, b, d, tile[row : row + QR])
        r.parts_ready(4 + half, 6 + half)
        if half == 0:
            r.pump(3)
    r.pump(4)
    put_bias_sums(r.pack_v, r.dpre)
    r.dh1[...] = r.dh1[...] + dot(r.dpre[...], r.b_up[...], NT)
    r.used(2)
    r.pump(5)
    r.leave("dh1")


def connect(r):
    count, stride = r.count, r.stride
    position(r)
    seg, doc, me = r.seg, r.doc, r.me
    rest = lax.rem(seg, stride)
    core = lax.rem(me, 2)
    z = me // 2
    near = z + 1 - 2 * lax.rem(z, 2)
    far = lax.rem(z + 2, 4)
    r.partners = {
        "c": (doc, (me + 1 - 2 * core) * stride + rest),
        "x": (doc + 1 - 2 * lax.rem(doc, 2), seg),
        "y": (lax.rem(doc + 2, 4), seg),
        "a": (doc, (near * 2 + core) * stride + rest),
        "b": (doc, (far * 2 + core) * stride + rest),
    }
    r.seg_peer = lambda step: (doc, lax.rem(seg + step, count))
    r.doc_peer = lambda step: (lax.rem(doc + step, 4), seg)
    barrier = pltpu.get_barrier_semaphore()

    def greet(step, carry):
        pl.semaphore_signal(barrier, inc=1, device_id=r.seg_peer(step), device_id_type=MESH)
        return carry

    lax.fori_loop(1, count, greet, 0)
    for step in range(1, 4):
        pl.semaphore_signal(barrier, inc=1, device_id=r.doc_peer(step), device_id_type=MESH)
    ffn_got = [r.f_got0, r.f_got1, r.f_got2, r.f_got3, r.f_got4]
    att_got = [r.a_got0, r.a_got1, r.a_got2, r.a_got3, r.a_got4]
    staged = getattr(r, "f_staged", None)
    kept = r.parts if staged is None else r.f_got0
    r.ffn = Halving(FFN_ORDERS, kept, ffn_got, r.ffn_shares, r.partners, r.f_send, r.f_recv, staged)
    r.att = Halving(ATT_ORDERS, r.a_parts, att_got, r.att_shares, r.partners, r.a_send, r.a_recv)
    todo = list(STEPS)

    def run(n):
        for _ in range(min(n, len(todo))):
            code = todo.pop(0)
            stage, chunk = code % 1000 // 100, code % 100
            if code >= 1000:
                r.att.step(stage, chunk)
                continue
            r.ffn.step(stage, chunk)
            if stage == 0 and staged is not None and chunk + 2 < 8:
                r.ffn.load(chunk + 2, r.i_parts, r.load_sem)

    r.run = run
    r.pump = lambda i: run(PUMPS[i])
    return lambda: pl.semaphore_wait(barrier, count + 2)


def spread(r, src, dst, send_sem, recv_sem):
    def copy(step):
        return pltpu.make_async_remote_copy(
            src_ref=src,
            dst_ref=dst.at[r.seg],
            send_sem=send_sem.at[step],
            recv_sem=recv_sem.at[step],
            device_id=r.seg_peer(step),
            device_id_type=MESH,
        )

    def begin(step, carry):
        copy(step).start()
        return carry

    def end(step, carry):
        copy(step).wait()
        return carry

    lax.fori_loop(1, r.count, begin, 0)
    return lambda: lax.fori_loop(1, r.count, end, 0)


def share_rows(r):
    r.end_heads = spread(r, r.heads, r.every, r.h_send, r.h_recv)
    r.local = fetch([(r.heads, r.every.at[r.seg]), (r.rows_zero, r.every_zero.at[r.seg])], r.local_sem)
    r.end_zero = spread(r, r.rows_zero, r.every_zero, r.z_send, r.z_recv)


def rest_phase(r):
    tok, vec, fbias = r.tok, r.vec, r.fbias
    rows, width = tok.shape
    groups = rows // SEG
    hidden = r.c_act.shape[1]
    docs = groups
    segs = r.count
    c_rows = docs * segs
    heads_n = width // HEAD
    for copy in r.local:
        copy.wait()
    r.end_heads()
    for s in range(segs):
        row = r.every[s].astype(F32)
        for d in range(docs):
            at = d * segs + s
            r.c_in[at : at + 1, :] = row[d : d + 1] + r.pos[s : s + 1, :]
            r.c_cot[at : at + 1, :] = row[docs + d : docs + d + 1]
            r.zeros[0, at : at + 1, :] = row[2 * docs + d : 2 * docs + d + 1]
            r.zeros[1, at : at + 1, :] = row[3 * docs + d : 3 * docs + d + 1]
    base = r.c_in[...]
    base_low = base.astype(BF16)
    weight_copy(r, 1, 0).wait()
    for part in range(3):
        cols = slice(part * width, (part + 1) * width)
        out = dot(base_low, r.b_qkv[:, cols], NN)
        if part != 1:
            out = out + vec[1, part // 2 : part // 2 + 1, :]
        r.c_qkv[:, cols] = out.astype(BF16)
    r.pump(6)
    blocks = [(0, c_rows)] if c_rows <= 16 else [(d * segs, segs) for d in range(docs)]
    context = []
    attention = []
    for at, n in blocks:
        here = slice(at, at + n)
        query = head_rows(r.c_qkv[here, 0:width], heads_n)
        row_doc = (at + lax.rem(lax.broadcasted_iota(jnp.int32, (heads_n * n, n), 0), n)) // segs
        key = at + lax.broadcasted_iota(jnp.int32, (heads_n * n, n), 1)
        limit = jnp.zeros((heads_n * n, n), jnp.int32)
        for d in range(docs):
            limit = jnp.where(key // segs == d, r.counts[d], limit)
        keep = jnp.logical_and(row_doc == key // segs, lax.rem(key, segs) * SEG < limit)
        scores = dot(query, r.c_qkv[here, width : 2 * width], NT) * SCALE
        prob = softmax_rows(jnp.where(keep, scores, NEG))
        prob_low = prob.astype(BF16)
        context.append(head_join(dot(prob_low, r.c_qkv[here, 2 * width : 3 * width], NN), heads_n).astype(BF16))
        attention.append((query, prob, prob_low))
    context = context[0] if len(context) == 1 else jnp.concatenate(context, axis=0)
    weight_copy(r, 1, 1).wait()
    c_n1, c_inv1 = norm_forward(base + (dot(context, r.b_out[...], NN) + vec[1, 2:3, :]))
    c_first = c_n1 * vec[1, 3:4, :] + vec[1, 4:5, :]
    c_low = c_first.astype(BF16)
    r.pump(7)
    weight_copy(r, 1, 2).wait()
    for part in range(hidden // width):
        cols = slice(part * width, (part + 1) * width)
        value, grad = gelu_pair(dot(c_low, r.b_up[:, cols], NN) + fbias[1:2, cols])
        r.c_act[:, cols] = value.astype(BF16)
        r.c_slope[:, cols] = grad.astype(r.c_slope.dtype)
    r.pump(8)
    weight_copy(r, 1, 3).wait()
    c_n2, c_inv2 = norm_forward(c_first + (dot(r.c_act[...], r.b_down[...], NN) + vec[1, 5:6, :]))
    r.mixed[...] = c_n2 * vec[1, 6:7, :] + vec[1, 7:8, :]
    r.pump(9)
    g = r.c_cot[...]
    sums = {6: col_sum(g * c_n2), 7: col_sum(g)}
    dr2 = norm_backward(g * vec[1, 6:7, :], c_n2, c_inv2)
    dffn = dr2.astype(BF16)
    for part in range(hidden // width):
        cols = slice(part * width, (part + 1) * width)
        r.c_dpre[:, cols] = (dot(dffn, r.b_down[cols, :], NT) * r.c_slope[:, cols].astype(F32)).astype(BF16)
    weight_copy(r, 0, 3).start()
    r.pump(10)
    c_grad = dr2 + dot(r.c_dpre[...], r.b_up[...], NT)
    weight_copy(r, 0, 2).start()
    r.pump(11)
    sums[3] = col_sum(c_grad * c_n1)
    sums[4] = col_sum(c_grad)
    sums[5] = col_sum(dffn)
    dr1 = norm_backward(c_grad * vec[1, 3:4, :], c_n1, c_inv1)
    dattn = dr1.astype(BF16)
    d_context = dot(dattn, r.b_out[...], NT).astype(BF16)
    weight_copy(r, 0, 1).start()
    d_parts = []
    for (at, n), (query, prob, prob_low) in zip(blocks, attention):
        here = slice(at, at + n)
        down = head_rows(d_context[here], heads_n)
        dp = dot(down, r.c_qkv[here, 2 * width : 3 * width], NT)
        ds = (prob * (dp - jnp.sum(prob * dp, axis=-1, keepdims=True))).astype(BF16)
        dv = dot(prob_low, down, TN).astype(BF16)
        dq = (head_join(dot(ds, r.c_qkv[here, width : 2 * width], NN), heads_n) * SCALE).astype(BF16)
        dk = (dot(ds, query, TN) * SCALE).astype(BF16)
        d_parts.append(jnp.concatenate([dq, dk, dv], axis=1))
    c_dqkv = d_parts[0] if len(d_parts) == 1 else jnp.concatenate(d_parts, axis=0)
    sums[0] = col_sum(c_dqkv[:, 0:width])
    sums[1] = col_sum(c_dqkv[:, 2 * width : 3 * width])
    sums[2] = col_sum(dattn)
    r.pump(12)
    dh = dr1 + dot(c_dqkv, r.b_qkv[...], NT)
    weight_copy(r, 0, 0).start()
    r.pump(13)
    r.end_zero()
    for s in range(segs):
        for d in range(docs):
            at = d * segs + s
            r.z_inv[at : at + 1, :] = r.every_zero[s, d : d + 1, :]
    z_n2, z_inv2 = r.zeros[1], r.z_inv[:, 0:1]
    z_sums = {6: col_sum(dh * z_n2), 7: col_sum(dh)}
    z_dr2 = norm_backward(dh * vec[0, 6:7, :], z_n2, z_inv2)
    z_dffn = z_dr2.astype(BF16)
    z_sums[5] = col_sum(z_dffn)
    z_low = r.zeros[0].astype(BF16)
    r.pack_x[...] = jnp.zeros_like(r.pack_x)
    r.pack_y[...] = jnp.zeros_like(r.pack_y)
    r.pack_c[...] = jnp.zeros_like(r.pack_c)
    total = dh[0:segs]
    for d in range(1, docs):
        total = total + dh[d * segs : (d + 1) * segs]
    for b in range(8):
        cols = slice(b * 96, (b + 1) * 96)
        r.pack_x[b, :, 0:96] = base_low[:, cols]
        r.pack_x[b, :, 128:224] = context[:, cols]
        r.pack_x[b, :, 256:352] = c_low[:, cols]
        r.pack_x[b, :, 384:768] = r.c_act[:, b * 384 : (b + 1) * 384]
        r.pack_x[b, :, 768:864] = z_low[:, cols]
        r.pack_p[b] = jnp.zeros_like(r.pack_p[b])
        r.pack_p[b, :, 0:96] = total[:, cols]
    put_sums(r.pack_c.at[:, 0:16], sums)
    put_bias_sums(r.pack_c.at[:, 0:16], r.c_dpre)
    for b in range(4):
        r.pack_y[b, :, 0:576] = c_dqkv[:, b * 576 : (b + 1) * 576]
        r.pack_y[b, :, 640:832] = dattn[:, b * 192 : (b + 1) * 192]
        r.pack_y[b, :, 896:1664] = r.c_dpre[:, b * 768 : (b + 1) * 768]
        r.pack_y[b, :, 1664:1856] = dffn[:, b * 192 : (b + 1) * 192]
        r.pack_y[b, :, 2688:2880] = z_dffn[:, b * 192 : (b + 1) * 192]
    weight_copy(r, 0, 2).wait()
    for part in range(hidden // width):
        cols = slice(part * width, (part + 1) * width)
        value, grad = gelu_pair(dot(z_low, r.b_up[:, cols], NN) + fbias[0:1, cols])
        r.c_act[:, cols] = value.astype(BF16)
        r.c_slope[:, cols] = grad.astype(r.c_slope.dtype)
    for b in range(8):
        r.pack_x[b, :, 896:1280] = r.c_act[:, b * 384 : (b + 1) * 384]
    r.pump(14)
    weight_copy(r, 0, 3).wait()
    for part in range(hidden // width):
        cols = slice(part * width, (part + 1) * width)
        r.c_dpre[:, cols] = (dot(z_dffn, r.b_down[cols, :], NT) * r.c_slope[:, cols].astype(F32)).astype(BF16)
        r.pack_y[part, :, 1920:2688] = r.c_dpre[:, cols]
    put_sums(r.pack_c.at[:, 16:32], z_sums)
    put_bias_sums(r.pack_c.at[:, 16:32], r.c_dpre)
    r.pump(15)
    r.c_in[...] = z_dr2 + dot(r.c_dpre[...], r.b_up[...], NT)
    r.pump(16)
    exchange = []
    half_y = pl.ds(pl.multiple_of(lax.rem(r.me, 2) * 1536, 128), 1536)
    local = fetch([(r.pack_x.at[r.me], r.rows_x.at[r.doc]), (r.pack_y.at[r.doc], r.rows_y.at[r.doc])], r.local_sem)
    for step in range(1, 4):
        there = r.doc_peer(step)
        pair = [
            (r.pack_x.at[r.me], r.rows_x.at[r.doc]),
            (r.pack_y.at[there[0], :, half_y], r.rows_y.at[r.doc, :, half_y]),
        ]
        for i, (src, dst) in enumerate(pair):
            copy = pltpu.make_async_remote_copy(
                src_ref=src,
                dst_ref=dst,
                send_sem=r.x_send.at[step, i],
                recv_sem=r.x_recv.at[step, i],
                device_id=there,
                device_id_type=MESH,
            )
            copy.start()
            exchange.append(copy)
    r.inputs_ready()
    top = lax.broadcasted_iota(jnp.int32, (SEG, width), 0) == 0
    top_low = lax.broadcasted_iota(jnp.int32, (16, width), 0) == 0
    grads = []
    for g in range(groups):
        here = slice(g * SEG, (g + 1) * SEG)
        own = pl.ds(g * segs + r.seg, 1)
        tile = slice(g * SEG, g * SEG + 16)
        r.output[tile, :] = jnp.where(top_low, r.mixed[own, :], r.output[tile, :].astype(F32)).astype(BF16)
        grads.append(jnp.where(top, r.c_in[own, :], r.dh1[here, :]))
    grad = jnp.concatenate(grads, axis=0)
    normed = r.n1[...]
    sums = {3: col_sum(grad * normed), 4: col_sum(grad)}
    dr1 = norm_backward(grad * vec[0, 3:4, :], normed, r.inv1[:, 0:1])
    dattn = dr1.astype(BF16)
    sums[2] = col_sum(dattn)
    r.grad_tok[...] = dr1
    low = lane_halves(rows)
    for d in range(4):
        mid = dattn[:, (3 * (d // 2) + 1) * 128 : (3 * (d // 2) + 2) * 128]
        whole = 3 * (d // 2) + 2 * (d % 2)
        fill = jnp.zeros_like(mid)
        r.y_out[:, d * 256 : d * 256 + 128] = dattn[:, whole * 128 : (whole + 1) * 128]
        r.y_out[:, d * 256 + 128 : d * 256 + 256] = (
            jnp.where(low, mid, fill) if d % 2 == 0 else jnp.where(low, fill, mid)
        )
    weight_copy(r, 0, 1).wait()
    r.dctx[...] = dot(dattn, r.b_out[...], NT).astype(BF16)

    def put(chunk, b, d, at, value):
        slot = slot_of(ATT_ORDERS[chunk], relative(b, d, r.me, r.doc))
        r.a_parts[chunk, slot, :, at : at + value.shape[1]] = value.astype(BF16)

    def begin(*chunks):
        for chunk in chunks:
            r.att.send(0, chunk, r.a_parts.at[chunk, pl.ds(16, 16)])

    def strips(tile, b, i):
        at = b * 96 + i * 32
        return tile[at : at + 16], tile[at + 16 : at + 32]

    def side_by_side(d, upper, lower):
        if d % 2 == 0:
            return upper + pltpu.roll(lower, HEAD, 1)
        return pltpu.roll(upper, HEAD, 1) + lower

    for d in range(4):
        tile = dot(r.ctx[...], r.y_out[:, d * 256 : d * 256 + 256], TN)
        for b in range(8):
            for i in range(3):
                upper, lower = strips(tile, b, i)
                put(9 + i, b, d, 0, upper[:, 0:128])
                put(9 + i, b, d, 128, lower[:, 0:128])
                put(9 + i, b, d, 256, side_by_side(d, upper[:, 128:256], lower[:, 128:256]))
    begin(9, 10, 11)
    r.pump(17)
    pairs = width // 128
    half = lane_halves(SEG)
    for g in range(groups):
        here = slice(g * SEG, (g + 1) * SEG)
        for pair in range(pairs):
            at = pair * 128
            prob = r.probs[g * pairs + pair]
            down = two_heads(r.dctx[here, at : at + 128])
            query = two_heads(r.qkv[here, at : at + 128])
            key = two_heads(r.qkv[here, width + at : width + at + 128])
            dp = dot(down, r.qkv[here, 2 * width + at : 2 * width + at + 128], NT)
            dv = dot(prob.astype(BF16), down, TN)
            ds = (prob * (dp - jnp.sum(prob * dp, axis=-1, keepdims=True))).astype(BF16)
            dq = dot(jnp.concatenate([ds[:SEG], ds[SEG:]], axis=1), key, NN) * SCALE
            dk = dot(ds, query, TN) * SCALE
            for kind, value in enumerate((dq, dk, dv)):
                value = value.astype(BF16)
                r.dqkv[here, kind * width + at : kind * width + at + 128] = value
                slab = kind * pairs + pair
                d, tile = slab // 9 * 2, slab % 9
                if tile < 4:
                    r.y_qkv[here, d * 640 + tile * 128 : d * 640 + tile * 128 + 128] = value
                elif tile > 4:
                    r.y_qkv[here, d * 640 + tile * 128 : d * 640 + tile * 128 + 128] = value
                else:
                    zero = jnp.zeros_like(value)
                    r.y_qkv[here, d * 640 + 512 : d * 640 + 640] = jnp.where(half, value, zero)
                    r.y_qkv[here, d * 640 + 1152 : d * 640 + 1280] = jnp.where(half, zero, value)
            if pair % 3 == 2:
                r.pump(18 + 2 * g + pair // 3)
    for d in range(4):
        tile = dot(tok[...], r.y_qkv[:, d * 640 : d * 640 + QC], TN)
        for b in range(8):
            for i in range(3):
                upper, lower = strips(tile, b, i)
                put(3 * i, b, d, 0, upper)
                put(3 * i + 1, b, d, 128, lower[:, 0:256])
                put(3 * i + 2, b, d, 0, lower[:, 256:QC])
    begin(0, 3, 6)
    r.pump(22)
    for d in range(4):
        tile = dot(tok[...], r.y_qkv[:, d * 640 + QC : d * 640 + 640], TN)
        for b in range(8):
            for i in range(3):
                upper, lower = strips(tile, b, i)
                put(3 * i + 1, b, d, 0, upper[:, 0:128])
                put(3 * i + 2, b, d, 128, lower[:, 0:128])
                put(3 * i + 2, b, d, 256, side_by_side(d, upper[:, 128:256], lower[:, 128:256]))
    begin(1, 2, 4, 5, 7, 8)
    r.pump(23)
    sums[0] = col_sum(r.dqkv[:, 0:width])
    sums[1] = col_sum(r.dqkv[:, 2 * width : 3 * width])
    put_sums(r.pack_v, sums)

    def vec_copy(step):
        there = r.seg_peer(step)
        return pltpu.make_async_remote_copy(
            src_ref=r.pack_v.at[there[1] // r.stride],
            dst_ref=r.vec_got.at[r.seg],
            send_sem=r.v_send.at[step],
            recv_sem=r.v_recv.at[step],
            device_id=there,
            device_id_type=MESH,
        )

    def vec_begin(step, carry):
        vec_copy(step).start()
        return carry

    def vec_finish(step, carry):
        vec_copy(step).wait()
        return carry

    lax.fori_loop(1, r.count, vec_begin, 0)
    own_vec = pltpu.make_async_copy(r.pack_v.at[r.me], r.vec_got.at[r.seg], r.local_sem.at[2])
    own_vec.start()
    weight_copy(r, 0, 0).wait()
    r.grad_tok[...] = r.grad_tok[...] + dot(r.dqkv[:, 0 : 3 * width], r.b_qkv[...], NT)
    r.pump(24)
    r.run(LATE)
    for copy in exchange:
        copy.wait()
    exchange = []
    for step in range(1, 4):
        there = r.doc_peer(step)[0]
        copy = pltpu.make_async_remote_copy(
            src_ref=r.rows_y.at[there, :, half_y],
            dst_ref=r.rows_y.at[there, :, half_y],
            send_sem=r.y_send.at[step],
            recv_sem=r.y_recv.at[step],
            device_id=r.partners["c"],
            device_id_type=MESH,
        )
        copy.start()
        exchange.append(copy)
    own_vec.wait()
    lax.fori_loop(1, r.count, vec_finish, 0)
    r.vec_one[0:16, :] = lax.fori_loop(
        0, r.count, lambda i, total: total + r.vec_got[i], r.pack_c[r.me, 16:32, :]
    )
    r.vec_one[16:32, :] = r.pack_c[r.me, 0:16, :]
    r.vec_one[32:, :] = r.pack_p[r.me]
    own_vec = pltpu.make_async_copy(r.vec_one, r.vec_all.at[r.doc], r.local_sem.at[3])
    own_vec.start()
    for step in range(1, 4):
        copy = pltpu.make_async_remote_copy(
            src_ref=r.vec_one,
            dst_ref=r.vec_all.at[r.doc],
            send_sem=r.s_send.at[step],
            recv_sem=r.s_recv.at[step],
            device_id=r.doc_peer(step),
            device_id_type=MESH,
        )
        copy.start()
        exchange.append(copy)
    r.run(len(STEPS))
    for copy in exchange + local:
        copy.wait()
    own_vec.wait()
    r.vec_sum[...] = r.vec_all[0] + r.vec_all[1] + r.vec_all[2] + r.vec_all[3]
    r.ffn.finish()
    r.att.finish()


def refs_of(r, names, refs):
    for name, ref in zip(names, refs, strict=True):
        setattr(r, name, ref)


WEIGHTS = ("b_qkv", "b_out", "b_up", "b_down")
SAVED = ("qkv", "probs", "ctx", "n1", "inv1", "dh1", "first")
ACTS = ("h1", "act", "slope", "dffn", "dpre")


def sizes(rows, width, hidden, segs):
    groups = rows // SEG
    c_rows = groups * segs
    dma = pltpu.SemaphoreType.DMA
    table = {
        "b_qkv": ((width, 3 * width), BF16),
        "b_out": ((width, width), BF16),
        "b_up": ((width, hidden), BF16),
        "b_down": ((hidden, width), BF16),
        "qkv": ((rows, 3 * width), BF16),
        "probs": ((groups * width // 128, 2 * SEG, SEG), F32),
        "ctx": ((rows, width), BF16),
        "n1": ((rows, width), F32),
        "inv1": ((rows, 128), F32),
        "dh1": ((rows, width), F32),
        "first": ((rows, width), BF16),
        "h1": ((rows, width), BF16),
        "act": ((rows, hidden), BF16),
        "slope": ((rows, hidden), BF16),
        "dffn": ((rows, width), BF16),
        "dpre": ((rows, hidden), BF16),
        "parts": ((8, 32, QR, QC), BF16),
        "heads": ((4 * groups, width), BF16),
        "rows_zero": ((8, 128), F32),
        "pack_v": ((8, 16, 128), F32),
        "output": ((rows, width), BF16),
        "grad_tok": ((rows, width), F32),
        "ffn_shares": ((8, QR, QC), F32),
        "att_shares": ((12, 16, QC), F32),
        "rows_x": ((4, c_rows, 1280), BF16),
        "rows_y": ((4, c_rows, 3072), BF16),
        "vec_all": ((4, 32 + segs, 128), F32),
        "vec_sum": ((32 + segs, 128), F32),
        "every": ((segs, 4 * groups, width), BF16),
        "every_zero": ((segs, 8, 128), F32),
        "c_qkv": ((c_rows, 3 * width), BF16),
        "c_in": ((c_rows, width), F32),
        "c_cot": ((c_rows, width), F32),
        "c_act": ((c_rows, hidden), BF16),
        "c_slope": ((c_rows, hidden), F32 if c_rows <= 16 else BF16),
        "c_dpre": ((c_rows, hidden), BF16),
        "mixed": ((c_rows, width), F32),
        "zeros": ((2, c_rows, width), F32),
        "z_inv": ((c_rows, 128), F32),
        "pack_x": ((8, c_rows, 1280), BF16),
        "pack_y": ((4, c_rows, 3072), BF16),
        "pack_c": ((8, 32, 128), F32),
        "pack_p": ((8, segs, 128), F32),
        "dctx": ((rows, width), BF16),
        "vec_got": ((segs, 16, 128), F32),
        "vec_one": ((32 + segs, 128), F32),
        "a_parts": ((12, 32, 16, QC), BF16),
        "f_staged": ((2, 16, QR, QC), BF16),
        "y_qkv": ((rows, 2560), BF16),
        "y_out": ((rows, 1024), BF16),
        "dqkv": ((rows, 3 * width), BF16),
    }
    for i in range(5):
        table[f"f_got{i}"] = ((8, 16 >> i, QR, QC), BF16)
        table[f"a_got{i}"] = ((12, 16 >> i, 16, QC), BF16)
    sems = {
        "w_sem": (4,), "third_sem": (3,), "in_sem": (7,), "load_sem": (8,), "out_sem": (15,), "h_send": (segs,), "h_recv": (segs,),
        "z_send": (segs,), "z_recv": (segs,), "f_send": (5, 8), "f_recv": (5, 8), "a_send": (5, 12),
        "a_recv": (5, 12), "x_send": (4, 2), "x_recv": (4, 2), "v_send": (segs,), "v_recv": (segs,),
        "s_send": (4,), "s_recv": (4,), "y_send": (4,), "y_recv": (4,), "local_sem": (4,),
    }
    return table, {name: dma(shape) for name, shape in sems.items()}


REST_OUT = ("output", "grad_tok", "ffn_shares", "att_shares", "rows_x", "rows_y", "vec_all", "vec_sum")
REST_SCRATCH = (
    ("every", "every_zero", "c_qkv", "c_in", "c_cot", "c_act", "c_slope", "c_dpre", "mixed", "zeros", "z_inv")
    + ("pack_x", "pack_y", "pack_c", "pack_p", "dctx", "vec_got", "vec_one", "a_parts")
    + tuple(f"f_got{i}" for i in range(5))
    + tuple(f"a_got{i}" for i in range(5))
)
REST_SEMS = (
    ("w_sem", "in_sem", "load_sem", "h_send", "h_recv", "z_send", "z_recv", "f_send", "f_recv", "a_send", "a_recv")
    + ("x_send", "x_recv", "v_send", "v_recv", "s_send", "s_recv", "y_send", "y_recv", "local_sem")
)
W_NAMES = ("w_qkv", "w_out", "w_up", "w_down")


def call(body, name, ins, in_specs, outs, out_specs, scratch, table, sems, collective, args):
    shape = jax.ShapeDtypeStruct
    return pl.pallas_call(
        body,
        out_shape=tuple(shape(*table[n]) for n in outs),
        in_specs=in_specs,
        out_specs=out_specs,
        scratch_shapes=[sems[n] if n in sems else pltpu.VMEM(*table[n]) for n in scratch],
        compiler_params=pltpu.CompilerParams(
            vmem_limit_bytes=LIMIT,
            **(dict(collective_id=0, has_side_effects=True) if collective else {}),
        ),
        name=name,
    )(*args)


def run_whole(stride, segs, counts, tok, mask, cot, pos, vec, fbias, weights):
    rows, width = tok.shape
    table, sems = sizes(rows, width, weights[2].shape[2], segs)
    ins = ("counts", "tok", "mask", "cot", "pos", "vec", "fbias") + W_NAMES
    kept = SAVED[:-1] + ACTS + ("parts", "heads", "rows_zero", "pack_v")
    scratch = WEIGHTS + kept + REST_SCRATCH + REST_SEMS + ("third_sem",)

    def body(*refs):
        r = SimpleNamespace(stride=stride, count=segs)
        refs_of(r, ins + REST_OUT + scratch, refs)
        r.first = r.output
        r.y_qkv, r.y_out, r.dqkv = r.dpre, r.act, r.slope
        enter = connect(r)
        r.leave = lambda name: None
        r.used = lambda i: weight_copy(r, 1, i).start()
        r.inputs_ready = lambda: None

        def heads_ready():
            enter()
            share_rows(r)

        def parts_ready(*chunks):
            for chunk in chunks:
                r.ffn.send(0, chunk, r.parts.at[chunk, pl.ds(16, 16)])

        r.heads_ready = heads_ready
        r.parts_ready = parts_ready
        forward_phase(r)
        rest_phase(r)

    return call(
        body, "whole_step", ins, [SM] + [VM] * 6 + [ANY] * 4, REST_OUT, (VM,) * 8, scratch, table, sems, True,
        (counts, tok, mask, cot, pos, vec, fbias) + weights,
    )


def run_halves(stride, segs, counts, tok, mask, cot, pos, vec, fbias, weights):
    rows, width = tok.shape
    table, sems = sizes(rows, width, weights[2].shape[2], segs)
    ins = ("tok", "mask", "cot", "vec", "fbias") + W_NAMES
    outs = tuple("o_" + n for n in SAVED) + ("o_parts", "heads", "rows_zero", "pack_v")
    for n in SAVED + ("parts",):
        table["o_" + n] = table[n]
    scratch = WEIGHTS + SAVED + ACTS + ("parts", "w_sem", "third_sem", "out_sem")

    def first_body(*refs):
        r = SimpleNamespace(stride=stride, count=segs)
        refs_of(r, ins + outs + scratch, refs)
        position(r)
        leaving = []

        def go(src, dst):
            copy = pltpu.make_async_copy(src, dst, r.out_sem.at[len(leaving)])
            copy.start()
            leaving.append(copy)

        r.leave = lambda name: go(getattr(r, name), getattr(r, "o_" + name))
        r.parts_ready = lambda *chunks: [go(r.parts.at[c], r.o_parts.at[c]) for c in chunks]
        r.used = lambda i: None
        r.pump = lambda i: None
        r.heads_ready = lambda: None
        forward_phase(r)
        for copy in leaving:
            copy.wait()

    *saved, parts, heads, rows_zero, pack_v = call(
        first_body, "segment_forward", ins, [VM] * 5 + [ANY] * 4, outs, (ANY,) * 8 + (VM,) * 3, scratch, table, sems,
        False, (tok, mask, cot, vec, fbias) + weights,
    )
    ins_b = ("counts", "heads", "rows_zero", "tok", "pack_v", "pos", "vec", "fbias", "i_parts")
    ins_b = ins_b + tuple("i_" + n for n in SAVED) + W_NAMES
    scratch_b = WEIGHTS + SAVED[:-1] + REST_SCRATCH + ("f_staged", "y_qkv", "y_out", "dqkv") + REST_SEMS

    def second_body(*refs):
        r = SimpleNamespace(stride=stride, count=segs)
        refs_of(r, ins_b + REST_OUT + scratch_b, refs)
        for i in range(4):
            weight_copy(r, 1, i).start()
        enter = connect(r)
        enter()
        share_rows(r)
        for chunk in range(8):
            r.ffn.send(0, chunk, r.i_parts.at[chunk, pl.ds(16, 16)])
        for chunk in range(2):
            r.ffn.load(chunk, r.i_parts, r.load_sem)
        r.first = r.output
        inputs = fetch([(getattr(r, "i_" + n), getattr(r, n)) for n in SAVED], r.in_sem)

        def inputs_ready():
            for copy in inputs:
                copy.wait()

        r.inputs_ready = inputs_ready
        rest_phase(r)

    return call(
        second_body, "the_rest", ins_b, [SM] + [VM] * 7 + [ANY] * 12, REST_OUT, (VM,) * 4 + (ANY,) * 2 + (VM,) * 2,
        scratch_b, table, sems, True,
        (counts, heads, rows_zero, tok, pack_v, pos, vec, fbias, parts, *saved) + weights,
    )


def assemble(
    stride, ffn, att, rows_x, rows_y, sums, i_output, i_grad, g_qkv, g_out, g_up, g_down, g_vec, g_bias, g_pos,
    output, grad_tok,
):
    output[...] = i_output[...]
    grad_tok[...] = i_grad[...]
    rows = rows_x.shape[0] * rows_x.shape[1]
    doc = lax.axis_index("doc")
    x = rows_x[...].reshape(rows, rows_x.shape[2])
    y = rows_y[...].reshape(rows, rows_y.shape[2])
    g_qkv[1] = dot(x[:, 0:128], y[:, 0:640], TN)[0:96, 0:576]
    g_out[1] = dot(x[:, 128:256], y[:, 640:896], TN)[0:96, 0:192]
    g_up[1] = dot(x[:, 256:384], y[:, 896:1664], TN)[0:96, :]
    g_down[1] = dot(y[:, 1664:1920], x[:, 384:768], TN)[0:192]
    more = dot(x[:, 768:896], y[:, 1920:2688], TN)
    for r in range(2):
        at = slice(r * QR, (r + 1) * QR)
        for c in range(2):
            cols = slice(c * QC, (c + 1) * QC)
            g_up[0, at, cols] = ffn[4 + 2 * r + c] + more[at, cols]
    tall = jnp.concatenate([ffn[0], ffn[1], ffn[2], ffn[3]], axis=0)
    g_down[0] = tall + dot(y[:, 2688:2944], x[:, 896:1280], TN)[0:192]
    even = lax.rem(doc, 2) == 0
    for i in range(3):
        one, two, three, out = att[3 * i], att[3 * i + 1], att[3 * i + 2], att[9 + i]
        slabs = (
            jnp.concatenate([one, two[:, 0:128]], axis=1),
            jnp.concatenate([two[:, 128:384], three[:, 0:256]], axis=1),
        )
        for k in range(2):
            at = slice(32 * i + 16 * k, 32 * i + 16 * k + 16)
            side = slice(256 + 64 * k, 320 + 64 * k)
            whole = out[:, 128 * k : 128 * k + 128]

            @pl.when(even)
            def _():
                g_qkv[0, at, 0:512] = slabs[k]
                g_qkv[0, at, 512:576] = three[:, side]
                g_out[0, at, 0:128] = whole
                g_out[0, at, 128:192] = out[:, side]

            @pl.when(jnp.logical_not(even))
            def _():
                g_qkv[0, at, :] = jnp.concatenate([three[:, side], slabs[k]], axis=1)
                g_out[0, at, :] = jnp.concatenate([out[:, side], whole], axis=1)

    if stride > 1:
        for layer in range(2):
            g_vec[layer] = sums[16 * layer : 16 * layer + 8, 0:96]
            g_bias[layer] = sums[16 * layer + 8 : 16 * layer + 12, 0:96]
    else:
        for layer in range(2):
            g_vec[layer] = sums[pl.ds(16 * layer + 2 * doc, 2), 0:96]
            for i in range(4):
                at = 16 * layer + 8 + i
                g_bias[layer : layer + 1, i * 96 : i * 96 + 96] = sums[at : at + 1, 0:96]
    g_pos[...] = sums[32:, 0:96]


def run_assemble(stride, ffn, att, rows_x, rows_y, sums, output, grad_tok):
    shape = jax.ShapeDtypeStruct
    return pl.pallas_call(
        functools.partial(assemble, stride),
        out_shape=(
            shape((2, 96, 576), F32),
            shape((2, 96, 192), F32),
            shape((2, 96, 768), F32),
            shape((2, 192, 384), F32),
            shape((2, 2, 96) if stride == 1 else (2, 8, 96), F32),
            shape((2, 384) if stride == 1 else (2, 4, 96), F32),
            shape((sums.shape[0] - 32, 96), F32),
            shape(output.shape, BF16),
            shape(grad_tok.shape, F32),
        ),
        in_specs=[VM] * 7,
        out_specs=(VM,) * 9,
        compiler_params=pltpu.CompilerParams(vmem_limit_bytes=LIMIT),
        name="assemble",
    )(ffn, att, rows_x, rows_y, sums, output, grad_tok)


def shards(
    tokens,
    token_mask,
    doc_counts,
    w_qkv,
    w_out,
    w_up,
    w_down,
    vectors,
    ffn_bias,
    pos_embed,
    cotangent,
):
    docs, slots, width = tokens.shape
    seg_dev = slots // SEG
    groups = docs * seg_dev
    count = lax.axis_size("seg")
    stride = count // 8
    rest = lax.rem(lax.axis_index("seg"), stride)
    tok = tokens.reshape(groups * SEG, width)
    cot = cotangent.reshape(groups * SEG, width)
    weights = (w_qkv, w_out, w_up, w_down)
    run = run_whole if groups * count <= 16 else run_halves
    output, grad_tok, ffn, att, rows_x, rows_y, _, sums = run(
        stride, count, doc_counts, tok, token_mask.reshape(groups, SEG), cot, pos_embed, vectors, ffn_bias, weights
    )
    g_qkv, g_out, g_up, g_down, g_vec, g_bias, g_pos, output, grad_tok = run_assemble(
        stride, ffn, att, rows_x, rows_y, sums, output, grad_tok
    )
    g_down = jnp.transpose(g_down, (0, 2, 1))
    if stride > 1:
        lanes = [[i * stride + j for j in range(stride)] for i in range(8)]

        def own(arr, dim):
            low = lax.psum_scatter(arr[0:1], "seg", scatter_dimension=dim, axis_index_groups=lanes, tiled=True)
            size = arr.shape[dim] // stride
            return jnp.concatenate([low, lax.dynamic_slice_in_dim(arr[1:2], rest * size, size, dim)], axis=0)

        g_qkv, g_out, g_up, g_down = own(g_qkv, 1), own(g_out, 1), own(g_up, 1), own(g_down, 1)
        each = 96 // stride
        g_vec = lax.dynamic_slice(g_vec, (0, lax.axis_index("doc") * 2, rest * each), (2, 2, each))
        g_bias = lax.dynamic_slice_in_dim(g_bias.reshape(2, 384), rest * (384 // stride), 384 // stride, 1)
        g_pos = lax.dynamic_slice_in_dim(g_pos, rest * each, each, 1)
    return (
        output.reshape(tokens.shape),
        grad_tok.reshape(tokens.shape),
        g_qkv,
        g_out,
        g_up,
        g_down,
        g_vec,
        g_bias,
        g_pos,
    )


def solution(mesh):
    return jax.shard_map(
        shards,
        mesh=mesh,
        in_specs=(
            P("doc", "seg", None),
            P("doc", "seg"),
            P("doc"),
            P(),
            P(),
            P(),
            P(),
            P(),
            P(),
            P(),
            P("doc", "seg", None),
        ),
        out_specs=(
            P("doc", "seg", None),
            P("doc", "seg", None),
            P(None, "seg", "doc"),
            P(None, "seg", "doc"),
            P(None, "seg", "doc"),
            P(None, "seg", "doc"),
            P(None, "doc", "seg"),
            P(None, "seg"),
            P(None, "seg"),
        ),
        check_vma=False,
    )
```

```python
import functools
from types import SimpleNamespace

import jax
import jax.numpy as jnp
from jax import lax
from jax.experimental import pallas as pl
from jax.experimental.pallas import tpu as pltpu
from jax.sharding import PartitionSpec as P

MESH = pl.DeviceIdType.MESH
HEAD = 64
SEG = 128
NEG = -1e30
EPS = 1e-05
ROOT_HALF = 0.7071067811865476
INV_ROOT_TWO_PI = 0.3989422804014327
SCALE = HEAD ** (-0.5)
F32 = jnp.float32
BF16 = jnp.bfloat16
VM = pl.BlockSpec(memory_space=pltpu.VMEM)
SM = pl.BlockSpec(memory_space=pltpu.SMEM)
ANY = pl.BlockSpec(memory_space=pl.ANY)
LIMIT = 62 << 20
QR, QC = 48, 384
NN = (((1,), (0,)), ((), ()))
NT = (((1,), (1,)), ((), ()))
TN = (((0,), (0,)), ((), ()))


def dot(a, b, dims):
    return lax.dot_general(a, b, dims, preferred_element_type=F32)


def norm_forward(resid):
    cent = resid - jnp.mean(resid, axis=-1, keepdims=True)
    inv = lax.rsqrt(jnp.mean(cent * cent, axis=-1, keepdims=True) + EPS)
    return cent * inv, inv


def norm_backward(scaled, normed, inv):
    inner = jnp.mean(scaled * normed, axis=-1, keepdims=True)
    return inv * (scaled - jnp.mean(scaled, axis=-1, keepdims=True) - normed * inner)


def gelu_pair(pre):
    half_cdf = 0.5 * (1.0 + lax.erf(pre * ROOT_HALF))
    slope = half_cdf + pre * jnp.exp(-0.5 * pre * pre) * INV_ROOT_TWO_PI
    return pre * half_cdf, slope


def col_sum(arr):
    return jnp.sum(arr.astype(F32), axis=0, keepdims=True)


def softmax_rows(scores):
    expo = jnp.exp(scores - jnp.max(scores, axis=-1, keepdims=True))
    return expo / jnp.sum(expo, axis=-1, keepdims=True)


def lane_halves(rows):
    lane = lax.broadcasted_iota(jnp.int32, (rows, 128), 1)
    return lane < HEAD


def two_heads(slab):
    low = lane_halves(slab.shape[0])
    zero = jnp.zeros_like(slab)
    return jnp.concatenate([jnp.where(low, slab, zero), jnp.where(low, zero, slab)], axis=0)


def fetch(pairs, sem):
    copies = [pltpu.make_async_copy(src, dst, sem.at[i]) for i, (src, dst) in enumerate(pairs)]
    for copy in copies:
        copy.start()
    return copies


def xor_bit(a, b):
    return a + b - 2 * a * b


FFN_ORDERS = (
    "xyab", "yaxb", "abxy", "axyb", "xyab", "yabx", "xayb", "yxab",
)
ATT_ORDERS = (
    "xaby", "yxab", "yxab", "xaby", "xaby", "yxab", "yxab", "xyab", "ayxb", "yabx", "yxab", "xyab",
)


def relative(b, d, me, doc):
    return {
        "c": xor_bit(lax.rem(me, 2), b % 2),
        "x": xor_bit(lax.rem(doc, 2), d % 2),
        "y": xor_bit(doc // 2, d // 2),
        "a": xor_bit(lax.rem(me // 2, 2), (b // 2) % 2),
        "b": xor_bit(me // 4, b // 4),
    }


def slot_of(order, bits):
    return sum(bits[name] * (16 >> i) for i, name in enumerate("c" + order))


def first_rows(rows, width):
    return lax.rem(lax.broadcasted_iota(jnp.int32, (rows, width), 0), SEG) == 0


def put_bias_sums(pack_v, dpre):
    for b in range(8):
        for i in range(4):
            at = b * 384 + i * 96
            pack_v[b, 8 + i : 9 + i, 0:96] = col_sum(dpre[:, at : at + 96])


def put_sums(pack_v, sums):
    for b in range(8):
        for i, value in sums.items():
            pack_v[b, i : i + 1, 0:96] = value[:, b * 96 : (b + 1) * 96]


def head_rows(arr, heads):
    rows, width = arr.shape
    lane = lax.broadcasted_iota(jnp.int32, (rows, width), 1)
    zero = jnp.zeros_like(arr)
    parts = [jnp.where(lane // HEAD == h, arr, zero) for h in range(heads)]
    return jnp.concatenate(parts, axis=0)


def head_join(arr, heads):
    rows = arr.shape[0] // heads
    lane = lax.broadcasted_iota(jnp.int32, (rows, arr.shape[1]), 1)
    out = jnp.zeros((rows, arr.shape[1]), F32)
    for h in range(heads):
        out = jnp.where(lane // HEAD == h, arr[h * rows : (h + 1) * rows], out)
    return out


class Halving:
    def __init__(self, orders, kept, got, shares, partners, send_sem, recv_sem, staged=None):
        self.orders, self.kept, self.got, self.shares, self.staged = orders, kept, got, shares, staged
        self.partners, self.send_sem, self.recv_sem = partners, send_sem, recv_sem
        self.sends = {}
        self.loads = []

    def send(self, stage, chunk, src):
        copy = pltpu.make_async_remote_copy(
            src_ref=src,
            dst_ref=self.got[stage].at[chunk],
            send_sem=self.send_sem.at[stage, chunk],
            recv_sem=self.recv_sem.at[stage, chunk],
            device_id=self.partners[("c" + self.orders[chunk])[stage]],
            device_id_type=MESH,
        )
        copy.start()
        self.sends[stage, chunk] = copy

    def load(self, chunk, source, sem):
        copy = pltpu.make_async_copy(source.at[chunk, pl.ds(0, 16)], self.staged.at[chunk % 2], sem.at[chunk])
        copy.start()
        self.loads.append(copy)

    def add(self, stage, chunk, first, last):
        kept = self.kept
        more = self.got[stage].at[chunk]
        if stage == 0 and self.staged is not None:
            more = self.staged.at[chunk % 2]

        kept[chunk, first:last] = kept[chunk, first:last] + more[first:last]

    def step(self, stage, chunk):
        if stage == 0 and self.staged is not None:
            self.loads[chunk].wait()
        self.sends[stage, chunk].wait_recv()
        half = (16 >> stage) // 2
        if stage < 4:
            self.add(stage, chunk, half, 2 * half)
            self.send(stage + 1, chunk, self.kept.at[chunk, pl.ds(half, half)])
            if stage > 0:
                self.sends.pop((stage - 1, chunk)).wait_send()
            self.add(stage, chunk, 0, half)
        else:
            self.shares[chunk] = self.kept[chunk, 0].astype(F32) + self.got[4][chunk, 0].astype(F32)

    def finish(self):
        for copy in self.sends.values():
            copy.wait_send()


STEPS = (
    0, 1, 2, 3, 4, 6, 5, 7, 100, 101, 102, 104, 105, 103, 201, 106, 107, 203, 200, 301, 205, 202, 1009, 1010,
    1011, 204, 206, 300, 1000, 1003, 1006, 1001, 401, 207, 1002, 1004, 1005, 303, 1007, 1008, 302, 304, 1109,
    305, 1111, 400, 1110, 307, 1100, 306, 403, 1108, 1103, 1106, 1209, 404, 1104, 1101, 1200, 407, 1107, 1102,
    405, 1203, 406, 1210, 1105, 1309, 1204, 1206, 402, 1201, 1300, 1211, 1310, 1202, 1303, 1208, 1306, 1205,
    1409, 1304, 1301, 1207, 1400, 1311, 1403, 1302, 1410, 1308, 1404, 1305, 1406, 1307, 1401, 1411, 1402, 1408,
    1405, 1407,
)
PUMPS = (
    0, 1, 1, 1, 1, 1, 2, 1, 2, 1, 0, 0, 2, 1, 0, 1, 2, 1, 3, 4, 0, 1, 1, 0, 5,
)
LATE = 36


def weight_copy(r, layer, i):
    src = (r.w_qkv, r.w_out, r.w_up, r.w_down)[i]
    dst = (r.b_qkv, r.b_out, r.b_up, r.b_down)[i]
    return pltpu.make_async_copy(src.at[layer], dst, r.w_sem.at[i])


def position(r):
    r.seg = lax.axis_index("seg")
    r.doc = lax.axis_index("doc")
    r.me = r.seg // r.stride


def forward_phase(r):
    tok, vec, qkv = r.tok, r.vec, r.qkv
    rows, width = tok.shape
    groups = rows // SEG
    pairs = width // 128
    hidden = r.act.shape[1]
    thirds = []
    for part in range(3):
        cols = slice(part * width, (part + 1) * width)
        thirds.append(
            pltpu.make_async_copy(r.w_qkv.at[0, :, cols], r.b_qkv.at[:, cols], r.third_sem.at[part])
        )
        thirds[part].start()
    for i in range(1, 4):
        weight_copy(r, 0, i).start()
    for part in range(3):
        cols = slice(part * width, (part + 1) * width)
        thirds[part].wait()
        out = dot(tok[...], r.b_qkv[:, cols], NN)
        if part != 1:
            out = out + vec[0, part // 2 : part // 2 + 1, :]
        qkv[:, cols] = out.astype(BF16)
    r.leave("qkv")
    for g in range(groups):
        here = slice(g * SEG, (g + 1) * SEG)
        keep = r.mask[g : g + 1, :] > 0
        for pair in range(pairs):
            at = pair * 128
            query = two_heads(qkv[here, at : at + 128])
            scores = dot(query, qkv[here, width + at : width + at + 128], NT) * SCALE
            prob = softmax_rows(jnp.where(keep, scores, NEG))
            r.probs[g * pairs + pair] = prob
            low = prob.astype(BF16)
            side = jnp.concatenate([low[:SEG], low[SEG:]], axis=1)
            value = two_heads(qkv[here, 2 * width + at : 2 * width + at + 128])
            r.ctx[here, at : at + 128] = dot(side, value, NN).astype(BF16)
    r.leave("probs")
    r.leave("ctx")
    weight_copy(r, 0, 1).wait()
    resid = tok[...].astype(F32) + (dot(r.ctx[...], r.b_out[...], NN) + vec[0, 2:3, :])
    normed, inv = norm_forward(resid)
    r.n1[...] = normed
    r.inv1[...] = jnp.broadcast_to(inv, r.inv1.shape)
    r.leave("n1")
    r.leave("inv1")
    r.h1[...] = (normed * vec[0, 3:4, :] + vec[0, 4:5, :]).astype(BF16)
    weight_copy(r, 0, 2).wait()
    for part in range(hidden // width):
        cols = slice(part * width, (part + 1) * width)
        value, grad = gelu_pair(dot(r.h1[...], r.b_up[:, cols], NN) + r.fbias[0:1, cols])
        r.act[:, cols] = value.astype(BF16)
        r.slope[:, cols] = grad.astype(BF16)
    weight_copy(r, 0, 3).wait()
    r.used(0)
    r.used(1)
    first = r.n1[...] * vec[0, 3:4, :] + vec[0, 4:5, :]
    normed, inv = norm_forward(first + (dot(r.act[...], r.b_down[...], NN) + vec[0, 5:6, :]))
    r.first[...] = (normed * vec[0, 6:7, :] + vec[0, 7:8, :]).astype(BF16)
    r.leave("first")
    r.rows_zero[...] = jnp.zeros_like(r.rows_zero)
    starts = [g * SEG for g in range(groups)]
    tops = [r.first[at : at + 16, :].astype(F32)[0:1] for at in starts]
    tops += [r.cot[at : at + 16, :].astype(F32)[0:1] for at in starts]
    tops += [r.h1[at : at + 16, :].astype(F32)[0:1] for at in starts]
    tops += [normed[at : at + 1] for at in starts]
    r.heads[...] = jnp.concatenate(tops, axis=0).astype(BF16)
    for g, at in enumerate(starts):
        r.rows_zero[g : g + 1, :] = jnp.broadcast_to(inv[at : at + 1], (1, 128))
    r.heads_ready()
    grad = jnp.where(first_rows(rows, width), 0.0, r.cot[...].astype(F32))
    sums = {6: col_sum(grad * normed), 7: col_sum(grad)}
    dr2 = norm_backward(grad * vec[0, 6:7, :], normed, inv)
    r.dffn[...] = dr2.astype(BF16)
    r.dh1[...] = dr2
    sums[5] = col_sum(r.dffn[...])
    r.pack_v[...] = jnp.zeros_like(r.pack_v)
    put_sums(r.pack_v, sums)

    def place(chunk, b, d, value):
        slot = slot_of(FFN_ORDERS[chunk], relative(b, d, r.me, r.doc))
        r.parts[chunk, slot] = value.astype(BF16)

    for j in range(4):
        pieces = [dr2[:, d * 192 + j * QR : d * 192 + (j + 1) * QR] for d in range(4)]
        tile = dot(jnp.concatenate(pieces, axis=1).astype(BF16), r.act[...], TN)
        for d in range(4):
            for b in range(8):
                place(j, b, d, tile[d * QR : (d + 1) * QR, b * QC : (b + 1) * QC])
        r.parts_ready(j)
    for part in range(hidden // width):
        cols = slice(part * width, (part + 1) * width)
        r.dpre[:, cols] = (dot(r.dffn[...], r.b_down[cols, :], NT) * r.slope[:, cols].astype(F32)).astype(BF16)
        if part > 0:
            r.pump(part - 1)
    r.used(3)
    for half in range(2):
        for d in range(4):
            at = d * 768 + half * QC
            tile = dot(r.h1[...], r.dpre[:, at : at + QC], TN)
            for b in range(8):
                for top_half in range(2):
                    row = b * 96 + top_half * QR
                    place(4 + 2 * top_half + half, b, d, tile[row : row + QR])
        r.parts_ready(4 + half, 6 + half)
        if half == 0:
            r.pump(3)
    r.pump(4)
    put_bias_sums(r.pack_v, r.dpre)
    r.dh1[...] = r.dh1[...] + dot(r.dpre[...], r.b_up[...], NT)
    r.used(2)
    r.pump(5)
    r.leave("dh1")


def connect(r):
    count, stride = r.count, r.stride
    position(r)
    seg, doc, me = r.seg, r.doc, r.me
    rest = lax.rem(seg, stride)
    core = lax.rem(me, 2)
    z = me // 2
    near = z + 1 - 2 * lax.rem(z, 2)
    far = lax.rem(z + 2, 4)
    r.partners = {
        "c": (doc, (me + 1 - 2 * core) * stride + rest),
        "x": (doc + 1 - 2 * lax.rem(doc, 2), seg),
        "y": (lax.rem(doc + 2, 4), seg),
        "a": (doc, (near * 2 + core) * stride + rest),
        "b": (doc, (far * 2 + core) * stride + rest),
    }
    r.seg_peer = lambda step: (doc, lax.rem(seg + step, count))
    r.doc_peer = lambda step: (lax.rem(doc + step, 4), seg)
    barrier = pltpu.get_barrier_semaphore()

    def greet(step, carry):
        pl.semaphore_signal(barrier, inc=1, device_id=r.seg_peer(step), device_id_type=MESH)
        return carry

    lax.fori_loop(1, count, greet, 0)
    for step in range(1, 4):
        pl.semaphore_signal(barrier, inc=1, device_id=r.doc_peer(step), device_id_type=MESH)
    ffn_got = [r.f_got0, r.f_got1, r.f_got2, r.f_got3, r.f_got4]
    att_got = [r.a_got0, r.a_got1, r.a_got2, r.a_got3, r.a_got4]
    staged = getattr(r, "f_staged", None)
    kept = r.parts if staged is None else r.f_got0
    r.ffn = Halving(FFN_ORDERS, kept, ffn_got, r.ffn_shares, r.partners, r.f_send, r.f_recv, staged)
    r.att = Halving(ATT_ORDERS, r.a_parts, att_got, r.att_shares, r.partners, r.a_send, r.a_recv)
    todo = list(STEPS)

    def run(n):
        for _ in range(min(n, len(todo))):
            code = todo.pop(0)
            stage, chunk = code % 1000 // 100, code % 100
            if code >= 1000:
                r.att.step(stage, chunk)
                continue
            r.ffn.step(stage, chunk)
            if stage == 0 and staged is not None and chunk + 2 < 8:
                r.ffn.load(chunk + 2, r.i_parts, r.load_sem)

    r.run = run
    r.pump = lambda i: run(PUMPS[i])
    return lambda: pl.semaphore_wait(barrier, count + 2)


def spread(r, src, dst, send_sem, recv_sem):
    def copy(step):
        return pltpu.make_async_remote_copy(
            src_ref=src,
            dst_ref=dst.at[r.seg],
            send_sem=send_sem.at[step],
            recv_sem=recv_sem.at[step],
            device_id=r.seg_peer(step),
            device_id_type=MESH,
        )

    def begin(step, carry):
        copy(step).start()
        return carry

    def end(step, carry):
        copy(step).wait()
        return carry

    lax.fori_loop(1, r.count, begin, 0)
    return lambda: lax.fori_loop(1, r.count, end, 0)


def share_rows(r):
    r.end_heads = spread(r, r.heads, r.every, r.h_send, r.h_recv)
    r.local = fetch([(r.heads, r.every.at[r.seg]), (r.rows_zero, r.every_zero.at[r.seg])], r.local_sem)
    r.end_zero = spread(r, r.rows_zero, r.every_zero, r.z_send, r.z_recv)


def rest_phase(r):
    tok, vec, fbias = r.tok, r.vec, r.fbias
    rows, width = tok.shape
    groups = rows // SEG
    hidden = r.c_act.shape[1]
    docs = groups
    segs = r.count
    c_rows = docs * segs
    heads_n = width // HEAD
    for copy in r.local:
        copy.wait()
    r.end_heads()
    for s in range(segs):
        row = r.every[s].astype(F32)
        for d in range(docs):
            at = d * segs + s
            r.c_in[at : at + 1, :] = row[d : d + 1] + r.pos[s : s + 1, :]
            r.c_cot[at : at + 1, :] = row[docs + d : docs + d + 1]
            r.zeros[0, at : at + 1, :] = row[2 * docs + d : 2 * docs + d + 1]
            r.zeros[1, at : at + 1, :] = row[3 * docs + d : 3 * docs + d + 1]
    base = r.c_in[...]
    base_low = base.astype(BF16)
    weight_copy(r, 1, 0).wait()
    for part in range(3):
        cols = slice(part * width, (part + 1) * width)
        out = dot(base_low, r.b_qkv[:, cols], NN)
        if part != 1:
            out = out + vec[1, part // 2 : part // 2 + 1, :]
        r.c_qkv[:, cols] = out.astype(BF16)
    r.pump(6)
    blocks = [(0, c_rows)] if c_rows <= 16 else [(d * segs, segs) for d in range(docs)]
    context = []
    attention = []
    for at, n in blocks:
        here = slice(at, at + n)
        query = head_rows(r.c_qkv[here, 0:width], heads_n)
        row_doc = (at + lax.rem(lax.broadcasted_iota(jnp.int32, (heads_n * n, n), 0), n)) // segs
        key = at + lax.broadcasted_iota(jnp.int32, (heads_n * n, n), 1)
        limit = jnp.zeros((heads_n * n, n), jnp.int32)
        for d in range(docs):
            limit = jnp.where(key // segs == d, r.counts[d], limit)
        keep = jnp.logical_and(row_doc == key // segs, lax.rem(key, segs) * SEG < limit)
        scores = dot(query, r.c_qkv[here, width : 2 * width], NT) * SCALE
        prob = softmax_rows(jnp.where(keep, scores, NEG))
        prob_low = prob.astype(BF16)
        context.append(head_join(dot(prob_low, r.c_qkv[here, 2 * width : 3 * width], NN), heads_n).astype(BF16))
        attention.append((query, prob, prob_low))
    context = context[0] if len(context) == 1 else jnp.concatenate(context, axis=0)
    weight_copy(r, 1, 1).wait()
    c_n1, c_inv1 = norm_forward(base + (dot(context, r.b_out[...], NN) + vec[1, 2:3, :]))
    c_first = c_n1 * vec[1, 3:4, :] + vec[1, 4:5, :]
    c_low = c_first.astype(BF16)
    r.pump(7)
    weight_copy(r, 1, 2).wait()
    for part in range(hidden // width):
        cols = slice(part * width, (part + 1) * width)
        value, grad = gelu_pair(dot(c_low, r.b_up[:, cols], NN) + fbias[1:2, cols])
        r.c_act[:, cols] = value.astype(BF16)
        r.c_slope[:, cols] = grad.astype(r.c_slope.dtype)
    r.pump(8)
    weight_copy(r, 1, 3).wait()
    c_n2, c_inv2 = norm_forward(c_first + (dot(r.c_act[...], r.b_down[...], NN) + vec[1, 5:6, :]))
    r.mixed[...] = c_n2 * vec[1, 6:7, :] + vec[1, 7:8, :]
    r.pump(9)
    g = r.c_cot[...]
    sums = {6: col_sum(g * c_n2), 7: col_sum(g)}
    dr2 = norm_backward(g * vec[1, 6:7, :], c_n2, c_inv2)
    dffn = dr2.astype(BF16)
    for part in range(hidden // width):
        cols = slice(part * width, (part + 1) * width)
        r.c_dpre[:, cols] = (dot(dffn, r.b_down[cols, :], NT) * r.c_slope[:, cols].astype(F32)).astype(BF16)
    weight_copy(r, 0, 3).start()
    r.pump(10)
    c_grad = dr2 + dot(r.c_dpre[...], r.b_up[...], NT)
    weight_copy(r, 0, 2).start()
    r.pump(11)
    sums[3] = col_sum(c_grad * c_n1)
    sums[4] = col_sum(c_grad)
    sums[5] = col_sum(dffn)
    dr1 = norm_backward(c_grad * vec[1, 3:4, :], c_n1, c_inv1)
    dattn = dr1.astype(BF16)
    d_context = dot(dattn, r.b_out[...], NT).astype(BF16)
    weight_copy(r, 0, 1).start()
    d_parts = []
    for (at, n), (query, prob, prob_low) in zip(blocks, attention):
        here = slice(at, at + n)
        down = head_rows(d_context[here], heads_n)
        dp = dot(down, r.c_qkv[here, 2 * width : 3 * width], NT)
        ds = (prob * (dp - jnp.sum(prob * dp, axis=-1, keepdims=True))).astype(BF16)
        dv = dot(prob_low, down, TN).astype(BF16)
        dq = (head_join(dot(ds, r.c_qkv[here, width : 2 * width], NN), heads_n) * SCALE).astype(BF16)
        dk = (dot(ds, query, TN) * SCALE).astype(BF16)
        d_parts.append(jnp.concatenate([dq, dk, dv], axis=1))
    c_dqkv = d_parts[0] if len(d_parts) == 1 else jnp.concatenate(d_parts, axis=0)
    sums[0] = col_sum(c_dqkv[:, 0:width])
    sums[1] = col_sum(c_dqkv[:, 2 * width : 3 * width])
    sums[2] = col_sum(dattn)
    r.pump(12)
    dh = dr1 + dot(c_dqkv, r.b_qkv[...], NT)
    weight_copy(r, 0, 0).start()
    r.pump(13)
    r.end_zero()
    for s in range(segs):
        for d in range(docs):
            at = d * segs + s
            r.z_inv[at : at + 1, :] = r.every_zero[s, d : d + 1, :]
    z_n2, z_inv2 = r.zeros[1], r.z_inv[:, 0:1]
    z_sums = {6: col_sum(dh * z_n2), 7: col_sum(dh)}
    z_dr2 = norm_backward(dh * vec[0, 6:7, :], z_n2, z_inv2)
    z_dffn = z_dr2.astype(BF16)
    z_sums[5] = col_sum(z_dffn)
    z_low = r.zeros[0].astype(BF16)
    r.pack_x[...] = jnp.zeros_like(r.pack_x)
    r.pack_y[...] = jnp.zeros_like(r.pack_y)
    r.pack_c[...] = jnp.zeros_like(r.pack_c)
    total = dh[0:segs]
    for d in range(1, docs):
        total = total + dh[d * segs : (d + 1) * segs]
    for b in range(8):
        cols = slice(b * 96, (b + 1) * 96)
        r.pack_x[b, :, 0:96] = base_low[:, cols]
        r.pack_x[b, :, 128:224] = context[:, cols]
        r.pack_x[b, :, 256:352] = c_low[:, cols]
        r.pack_x[b, :, 384:768] = r.c_act[:, b * 384 : (b + 1) * 384]
        r.pack_x[b, :, 768:864] = z_low[:, cols]
        r.pack_p[b] = jnp.zeros_like(r.pack_p[b])
        r.pack_p[b, :, 0:96] = total[:, cols]
    put_sums(r.pack_c.at[:, 0:16], sums)
    put_bias_sums(r.pack_c.at[:, 0:16], r.c_dpre)
    for b in range(4):
        r.pack_y[b, :, 0:576] = c_dqkv[:, b * 576 : (b + 1) * 576]
        r.pack_y[b, :, 640:832] = dattn[:, b * 192 : (b + 1) * 192]
        r.pack_y[b, :, 896:1664] = r.c_dpre[:, b * 768 : (b + 1) * 768]
        r.pack_y[b, :, 1664:1856] = dffn[:, b * 192 : (b + 1) * 192]
        r.pack_y[b, :, 2688:2880] = z_dffn[:, b * 192 : (b + 1) * 192]
    weight_copy(r, 0, 2).wait()
    for part in range(hidden // width):
        cols = slice(part * width, (part + 1) * width)
        value, grad = gelu_pair(dot(z_low, r.b_up[:, cols], NN) + fbias[0:1, cols])
        r.c_act[:, cols] = value.astype(BF16)
        r.c_slope[:, cols] = grad.astype(r.c_slope.dtype)
    for b in range(8):
        r.pack_x[b, :, 896:1280] = r.c_act[:, b * 384 : (b + 1) * 384]
    r.pump(14)
    weight_copy(r, 0, 3).wait()
    for part in range(hidden // width):
        cols = slice(part * width, (part + 1) * width)
        r.c_dpre[:, cols] = (dot(z_dffn, r.b_down[cols, :], NT) * r.c_slope[:, cols].astype(F32)).astype(BF16)
        r.pack_y[part, :, 1920:2688] = r.c_dpre[:, cols]
    put_sums(r.pack_c.at[:, 16:32], z_sums)
    put_bias_sums(r.pack_c.at[:, 16:32], r.c_dpre)
    r.pump(15)
    r.c_in[...] = z_dr2 + dot(r.c_dpre[...], r.b_up[...], NT)
    r.pump(16)
    exchange = []
    half_y = pl.ds(pl.multiple_of(lax.rem(r.me, 2) * 1536, 128), 1536)
    local = fetch([(r.pack_x.at[r.me], r.rows_x.at[r.doc]), (r.pack_y.at[r.doc], r.rows_y.at[r.doc])], r.local_sem)
    for step in range(1, 4):
        there = r.doc_peer(step)
        pair = [
            (r.pack_x.at[r.me], r.rows_x.at[r.doc]),
            (r.pack_y.at[there[0], :, half_y], r.rows_y.at[r.doc, :, half_y]),
        ]
        for i, (src, dst) in enumerate(pair):
            copy = pltpu.make_async_remote_copy(
                src_ref=src,
                dst_ref=dst,
                send_sem=r.x_send.at[step, i],
                recv_sem=r.x_recv.at[step, i],
                device_id=there,
                device_id_type=MESH,
            )
            copy.start()
            exchange.append(copy)
    r.inputs_ready()
    top = lax.broadcasted_iota(jnp.int32, (SEG, width), 0) == 0
    top_low = lax.broadcasted_iota(jnp.int32, (16, width), 0) == 0
    grads = []
    for g in range(groups):
        here = slice(g * SEG, (g + 1) * SEG)
        own = pl.ds(g * segs + r.seg, 1)
        tile = slice(g * SEG, g * SEG + 16)
        r.output[tile, :] = jnp.where(top_low, r.mixed[own, :], r.output[tile, :].astype(F32)).astype(BF16)
        grads.append(jnp.where(top, r.c_in[own, :], r.dh1[here, :]))
    grad = jnp.concatenate(grads, axis=0)
    normed = r.n1[...]
    sums = {3: col_sum(grad * normed), 4: col_sum(grad)}
    dr1 = norm_backward(grad * vec[0, 3:4, :], normed, r.inv1[:, 0:1])
    dattn = dr1.astype(BF16)
    sums[2] = col_sum(dattn)
    r.grad_tok[...] = dr1
    low = lane_halves(rows)
    for d in range(4):
        mid = dattn[:, (3 * (d // 2) + 1) * 128 : (3 * (d // 2) + 2) * 128]
        whole = 3 * (d // 2) + 2 * (d % 2)
        fill = jnp.zeros_like(mid)
        r.y_out[:, d * 256 : d * 256 + 128] = dattn[:, whole * 128 : (whole + 1) * 128]
        r.y_out[:, d * 256 + 128 : d * 256 + 256] = (
            jnp.where(low, mid, fill) if d % 2 == 0 else jnp.where(low, fill, mid)
        )
    weight_copy(r, 0, 1).wait()
    r.dctx[...] = dot(dattn, r.b_out[...], NT).astype(BF16)

    def put(chunk, b, d, at, value):
        slot = slot_of(ATT_ORDERS[chunk], relative(b, d, r.me, r.doc))
        r.a_parts[chunk, slot, :, at : at + value.shape[1]] = value.astype(BF16)

    def begin(*chunks):
        for chunk in chunks:
            r.att.send(0, chunk, r.a_parts.at[chunk, pl.ds(16, 16)])

    def strips(tile, b, i):
        at = b * 96 + i * 32
        return tile[at : at + 16], tile[at + 16 : at + 32]

    def side_by_side(d, upper, lower):
        if d % 2 == 0:
            return upper + pltpu.roll(lower, HEAD, 1)
        return pltpu.roll(upper, HEAD, 1) + lower

    for d in range(4):
        tile = dot(r.ctx[...], r.y_out[:, d * 256 : d * 256 + 256], TN)
        for b in range(8):
            for i in range(3):
                upper, lower = strips(tile, b, i)
                put(9 + i, b, d, 0, upper[:, 0:128])
                put(9 + i, b, d, 128, lower[:, 0:128])
                put(9 + i, b, d, 256, side_by_side(d, upper[:, 128:256], lower[:, 128:256]))
    begin(9, 10, 11)
    r.pump(17)
    pairs = width // 128
    half = lane_halves(SEG)
    for g in range(groups):
        here = slice(g * SEG, (g + 1) * SEG)
        for pair in range(pairs):
            at = pair * 128
            prob = r.probs[g * pairs + pair]
            down = two_heads(r.dctx[here, at : at + 128])
            query = two_heads(r.qkv[here, at : at + 128])
            key = two_heads(r.qkv[here, width + at : width + at + 128])
            dp = dot(down, r.qkv[here, 2 * width + at : 2 * width + at + 128], NT)
            dv = dot(prob.astype(BF16), down, TN)
            ds = (prob * (dp - jnp.sum(prob * dp, axis=-1, keepdims=True))).astype(BF16)
            dq = dot(jnp.concatenate([ds[:SEG], ds[SEG:]], axis=1), key, NN) * SCALE
            dk = dot(ds, query, TN) * SCALE
            for kind, value in enumerate((dq, dk, dv)):
                value = value.astype(BF16)
                r.dqkv[here, kind * width + at : kind * width + at + 128] = value
                slab = kind * pairs + pair
                d, tile = slab // 9 * 2, slab % 9
                if tile < 4:
                    r.y_qkv[here, d * 640 + tile * 128 : d * 640 + tile * 128 + 128] = value
                elif tile > 4:
                    r.y_qkv[here, d * 640 + tile * 128 : d * 640 + tile * 128 + 128] = value
                else:
                    zero = jnp.zeros_like(value)
                    r.y_qkv[here, d * 640 + 512 : d * 640 + 640] = jnp.where(half, value, zero)
                    r.y_qkv[here, d * 640 + 1152 : d * 640 + 1280] = jnp.where(half, zero, value)
            if pair % 3 == 2:
                r.pump(18 + 2 * g + pair // 3)
    for d in range(4):
        tile = dot(tok[...], r.y_qkv[:, d * 640 : d * 640 + QC], TN)
        for b in range(8):
            for i in range(3):
                upper, lower = strips(tile, b, i)
                put(3 * i, b, d, 0, upper)
                put(3 * i + 1, b, d, 128, lower[:, 0:256])
                put(3 * i + 2, b, d, 0, lower[:, 256:QC])
    begin(0, 3, 6)
    r.pump(22)
    for d in range(4):
        tile = dot(tok[...], r.y_qkv[:, d * 640 + QC : d * 640 + 640], TN)
        for b in range(8):
            for i in range(3):
                upper, lower = strips(tile, b, i)
                put(3 * i + 1, b, d, 0, upper[:, 0:128])
                put(3 * i + 2, b, d, 128, lower[:, 0:128])
                put(3 * i + 2, b, d, 256, side_by_side(d, upper[:, 128:256], lower[:, 128:256]))
    begin(1, 2, 4, 5, 7, 8)
    r.pump(23)
    sums[0] = col_sum(r.dqkv[:, 0:width])
    sums[1] = col_sum(r.dqkv[:, 2 * width : 3 * width])
    put_sums(r.pack_v, sums)

    def vec_copy(step):
        there = r.seg_peer(step)
        return pltpu.make_async_remote_copy(
            src_ref=r.pack_v.at[there[1] // r.stride],
            dst_ref=r.vec_got.at[r.seg],
            send_sem=r.v_send.at[step],
            recv_sem=r.v_recv.at[step],
            device_id=there,
            device_id_type=MESH,
        )

    def vec_begin(step, carry):
        vec_copy(step).start()
        return carry

    def vec_finish(step, carry):
        vec_copy(step).wait()
        return carry

    lax.fori_loop(1, r.count, vec_begin, 0)
    own_vec = pltpu.make_async_copy(r.pack_v.at[r.me], r.vec_got.at[r.seg], r.local_sem.at[2])
    own_vec.start()
    weight_copy(r, 0, 0).wait()
    r.grad_tok[...] = r.grad_tok[...] + dot(r.dqkv[:, 0 : 3 * width], r.b_qkv[...], NT)
    r.pump(24)
    r.run(LATE)
    for copy in exchange:
        copy.wait()
    exchange = []
    for step in range(1, 4):
        there = r.doc_peer(step)[0]
        copy = pltpu.make_async_remote_copy(
            src_ref=r.rows_y.at[there, :, half_y],
            dst_ref=r.rows_y.at[there, :, half_y],
            send_sem=r.y_send.at[step],
            recv_sem=r.y_recv.at[step],
            device_id=r.partners["c"],
            device_id_type=MESH,
        )
        copy.start()
        exchange.append(copy)
    own_vec.wait()
    lax.fori_loop(1, r.count, vec_finish, 0)
    r.vec_one[0:16, :] = lax.fori_loop(
        0, r.count, lambda i, total: total + r.vec_got[i], r.pack_c[r.me, 16:32, :]
    )
    r.vec_one[16:32, :] = r.pack_c[r.me, 0:16, :]
    r.vec_one[32:, :] = r.pack_p[r.me]
    own_vec = pltpu.make_async_copy(r.vec_one, r.vec_all.at[r.doc], r.local_sem.at[3])
    own_vec.start()
    for step in range(1, 4):
        copy = pltpu.make_async_remote_copy(
            src_ref=r.vec_one,
            dst_ref=r.vec_all.at[r.doc],
            send_sem=r.s_send.at[step],
            recv_sem=r.s_recv.at[step],
            device_id=r.doc_peer(step),
            device_id_type=MESH,
        )
        copy.start()
        exchange.append(copy)
    r.run(len(STEPS))
    for copy in exchange + local:
        copy.wait()
    own_vec.wait()
    r.vec_sum[...] = r.vec_all[0] + r.vec_all[1] + r.vec_all[2] + r.vec_all[3]
    r.ffn.finish()
    r.att.finish()


def refs_of(r, names, refs):
    for name, ref in zip(names, refs, strict=True):
        setattr(r, name, ref)


WEIGHTS = ("b_qkv", "b_out", "b_up", "b_down")
SAVED = ("qkv", "probs", "ctx", "n1", "inv1", "dh1", "first")
ACTS = ("h1", "act", "slope", "dffn", "dpre")


def sizes(rows, width, hidden, segs):
    groups = rows // SEG
    c_rows = groups * segs
    dma = pltpu.SemaphoreType.DMA
    table = {
        "b_qkv": ((width, 3 * width), BF16),
        "b_out": ((width, width), BF16),
        "b_up": ((width, hidden), BF16),
        "b_down": ((hidden, width), BF16),
        "qkv": ((rows, 3 * width), BF16),
        "probs": ((groups * width // 128, 2 * SEG, SEG), F32),
        "ctx": ((rows, width), BF16),
        "n1": ((rows, width), F32),
        "inv1": ((rows, 128), F32),
        "dh1": ((rows, width), F32),
        "first": ((rows, width), BF16),
        "h1": ((rows, width), BF16),
        "act": ((rows, hidden), BF16),
        "slope": ((rows, hidden), BF16),
        "dffn": ((rows, width), BF16),
        "dpre": ((rows, hidden), BF16),
        "parts": ((8, 32, QR, QC), BF16),
        "heads": ((4 * groups, width), BF16),
        "rows_zero": ((8, 128), F32),
        "pack_v": ((8, 16, 128), F32),
        "output": ((rows, width), BF16),
        "grad_tok": ((rows, width), F32),
        "ffn_shares": ((8, QR, QC), F32),
        "att_shares": ((12, 16, QC), F32),
        "rows_x": ((4, c_rows, 1280), BF16),
        "rows_y": ((4, c_rows, 3072), BF16),
        "vec_all": ((4, 32 + segs, 128), F32),
        "vec_sum": ((32 + segs, 128), F32),
        "every": ((segs, 4 * groups, width), BF16),
        "every_zero": ((segs, 8, 128), F32),
        "c_qkv": ((c_rows, 3 * width), BF16),
        "c_in": ((c_rows, width), F32),
        "c_cot": ((c_rows, width), F32),
        "c_act": ((c_rows, hidden), BF16),
        "c_slope": ((c_rows, hidden), F32 if c_rows <= 16 else BF16),
        "c_dpre": ((c_rows, hidden), BF16),
        "mixed": ((c_rows, width), F32),
        "zeros": ((2, c_rows, width), F32),
        "z_inv": ((c_rows, 128), F32),
        "pack_x": ((8, c_rows, 1280), BF16),
        "pack_y": ((4, c_rows, 3072), BF16),
        "pack_c": ((8, 32, 128), F32),
        "pack_p": ((8, segs, 128), F32),
        "dctx": ((rows, width), BF16),
        "vec_got": ((segs, 16, 128), F32),
        "vec_one": ((32 + segs, 128), F32),
        "a_parts": ((12, 32, 16, QC), BF16),
        "f_staged": ((2, 16, QR, QC), BF16),
        "y_qkv": ((rows, 2560), BF16),
        "y_out": ((rows, 1024), BF16),
        "dqkv": ((rows, 3 * width), BF16),
    }
    for i in range(5):
        table[f"f_got{i}"] = ((8, 16 >> i, QR, QC), BF16)
        table[f"a_got{i}"] = ((12, 16 >> i, 16, QC), BF16)
    sems = {
        "w_sem": (4,), "third_sem": (3,), "in_sem": (7,), "load_sem": (8,), "out_sem": (15,), "h_send": (segs,), "h_recv": (segs,),
        "z_send": (segs,), "z_recv": (segs,), "f_send": (5, 8), "f_recv": (5, 8), "a_send": (5, 12),
        "a_recv": (5, 12), "x_send": (4, 2), "x_recv": (4, 2), "v_send": (segs,), "v_recv": (segs,),
        "s_send": (4,), "s_recv": (4,), "y_send": (4,), "y_recv": (4,), "local_sem": (4,),
    }
    return table, {name: dma(shape) for name, shape in sems.items()}


REST_OUT = ("output", "grad_tok", "ffn_shares", "att_shares", "rows_x", "rows_y", "vec_all", "vec_sum")
REST_SCRATCH = (
    ("every", "every_zero", "c_qkv", "c_in", "c_cot", "c_act", "c_slope", "c_dpre", "mixed", "zeros", "z_inv")
    + ("pack_x", "pack_y", "pack_c", "pack_p", "dctx", "vec_got", "vec_one", "a_parts")
    + tuple(f"f_got{i}" for i in range(5))
    + tuple(f"a_got{i}" for i in range(5))
)
REST_SEMS = (
    ("w_sem", "in_sem", "load_sem", "h_send", "h_recv", "z_send", "z_recv", "f_send", "f_recv", "a_send", "a_recv")
    + ("x_send", "x_recv", "v_send", "v_recv", "s_send", "s_recv", "y_send", "y_recv", "local_sem")
)
W_NAMES = ("w_qkv", "w_out", "w_up", "w_down")


def call(body, name, ins, in_specs, outs, out_specs, scratch, table, sems, collective, args):
    shape = jax.ShapeDtypeStruct
    return pl.pallas_call(
        body,
        out_shape=tuple(shape(*table[n]) for n in outs),
        in_specs=in_specs,
        out_specs=out_specs,
        scratch_shapes=[sems[n] if n in sems else pltpu.VMEM(*table[n]) for n in scratch],
        compiler_params=pltpu.CompilerParams(
            vmem_limit_bytes=LIMIT,
            **(dict(collective_id=0, has_side_effects=True) if collective else {}),
        ),
        name=name,
    )(*args)


def run_whole(stride, segs, counts, tok, mask, cot, pos, vec, fbias, weights):
    rows, width = tok.shape
    table, sems = sizes(rows, width, weights[2].shape[2], segs)
    ins = ("counts", "tok", "mask", "cot", "pos", "vec", "fbias") + W_NAMES
    kept = SAVED[:-1] + ACTS + ("parts", "heads", "rows_zero", "pack_v")
    scratch = WEIGHTS + kept + REST_SCRATCH + REST_SEMS + ("third_sem",)

    def body(*refs):
        r = SimpleNamespace(stride=stride, count=segs)
        refs_of(r, ins + REST_OUT + scratch, refs)
        r.first = r.output
        r.y_qkv, r.y_out, r.dqkv = r.dpre, r.act, r.slope
        enter = connect(r)
        r.leave = lambda name: None
        r.used = lambda i: weight_copy(r, 1, i).start()
        r.inputs_ready = lambda: None

        def heads_ready():
            enter()
            share_rows(r)

        def parts_ready(*chunks):
            for chunk in chunks:
                r.ffn.send(0, chunk, r.parts.at[chunk, pl.ds(16, 16)])

        r.heads_ready = heads_ready
        r.parts_ready = parts_ready
        forward_phase(r)
        rest_phase(r)

    return call(
        body, "whole_step", ins, [SM] + [VM] * 6 + [ANY] * 4, REST_OUT, (VM,) * 8, scratch, table, sems, True,
        (counts, tok, mask, cot, pos, vec, fbias) + weights,
    )


def run_halves(stride, segs, counts, tok, mask, cot, pos, vec, fbias, weights):
    rows, width = tok.shape
    table, sems = sizes(rows, width, weights[2].shape[2], segs)
    ins = ("tok", "mask", "cot", "vec", "fbias") + W_NAMES
    outs = tuple("o_" + n for n in SAVED) + ("o_parts", "heads", "rows_zero", "pack_v")
    for n in SAVED + ("parts",):
        table["o_" + n] = table[n]
    scratch = WEIGHTS + SAVED + ACTS + ("parts", "w_sem", "third_sem", "out_sem")

    def first_body(*refs):
        r = SimpleNamespace(stride=stride, count=segs)
        refs_of(r, ins + outs + scratch, refs)
        position(r)
        leaving = []

        def go(src, dst):
            copy = pltpu.make_async_copy(src, dst, r.out_sem.at[len(leaving)])
            copy.start()
            leaving.append(copy)

        r.leave = lambda name: go(getattr(r, name), getattr(r, "o_" + name))
        r.parts_ready = lambda *chunks: [go(r.parts.at[c], r.o_parts.at[c]) for c in chunks]
        r.used = lambda i: None
        r.pump = lambda i: None
        r.heads_ready = lambda: None
        forward_phase(r)
        for copy in leaving:
            copy.wait()

    *saved, parts, heads, rows_zero, pack_v = call(
        first_body, "segment_forward", ins, [VM] * 5 + [ANY] * 4, outs, (ANY,) * 8 + (VM,) * 3, scratch, table, sems,
        False, (tok, mask, cot, vec, fbias) + weights,
    )
    ins_b = ("counts", "heads", "rows_zero", "tok", "pack_v", "pos", "vec", "fbias", "i_parts")
    ins_b = ins_b + tuple("i_" + n for n in SAVED) + W_NAMES
    scratch_b = WEIGHTS + SAVED[:-1] + REST_SCRATCH + ("f_staged", "y_qkv", "y_out", "dqkv") + REST_SEMS

    def second_body(*refs):
        r = SimpleNamespace(stride=stride, count=segs)
        refs_of(r, ins_b + REST_OUT + scratch_b, refs)
        for i in range(4):
            weight_copy(r, 1, i).start()
        enter = connect(r)
        enter()
        share_rows(r)
        for chunk in range(8):
            r.ffn.send(0, chunk, r.i_parts.at[chunk, pl.ds(16, 16)])
        for chunk in range(2):
            r.ffn.load(chunk, r.i_parts, r.load_sem)
        r.first = r.output
        inputs = fetch([(getattr(r, "i_" + n), getattr(r, n)) for n in SAVED], r.in_sem)

        def inputs_ready():
            for copy in inputs:
                copy.wait()

        r.inputs_ready = inputs_ready
        rest_phase(r)

    return call(
        second_body, "the_rest", ins_b, [SM] + [VM] * 7 + [ANY] * 12, REST_OUT, (VM,) * 4 + (ANY,) * 2 + (VM,) * 2,
        scratch_b, table, sems, True,
        (counts, heads, rows_zero, tok, pack_v, pos, vec, fbias, parts, *saved) + weights,
    )


def assemble(
    stride, ffn, att, rows_x, rows_y, sums, i_output, i_grad, g_qkv, g_out, g_up, g_down, g_vec, g_bias, g_pos,
    output, grad_tok,
):
    output[...] = i_output[...]
    grad_tok[...] = i_grad[...]
    rows = rows_x.shape[0] * rows_x.shape[1]
    doc = lax.axis_index("doc")
    x = rows_x[...].reshape(rows, rows_x.shape[2])
    y = rows_y[...].reshape(rows, rows_y.shape[2])
    g_qkv[1] = dot(x[:, 0:128], y[:, 0:640], TN)[0:96, 0:576]
    g_out[1] = dot(x[:, 128:256], y[:, 640:896], TN)[0:96, 0:192]
    g_up[1] = dot(x[:, 256:384], y[:, 896:1664], TN)[0:96, :]
    g_down[1] = dot(y[:, 1664:1920], x[:, 384:768], TN)[0:192]
    more = dot(x[:, 768:896], y[:, 1920:2688], TN)
    for r in range(2):
        at = slice(r * QR, (r + 1) * QR)
        for c in range(2):
            cols = slice(c * QC, (c + 1) * QC)
            g_up[0, at, cols] = ffn[4 + 2 * r + c] + more[at, cols]
    tall = jnp.concatenate([ffn[0], ffn[1], ffn[2], ffn[3]], axis=0)
    g_down[0] = tall + dot(y[:, 2688:2944], x[:, 896:1280], TN)[0:192]
    even = lax.rem(doc, 2) == 0
    for i in range(3):
        one, two, three, out = att[3 * i], att[3 * i + 1], att[3 * i + 2], att[9 + i]
        slabs = (
            jnp.concatenate([one, two[:, 0:128]], axis=1),
            jnp.concatenate([two[:, 128:384], three[:, 0:256]], axis=1),
        )
        for k in range(2):
            at = slice(32 * i + 16 * k, 32 * i + 16 * k + 16)
            side = slice(256 + 64 * k, 320 + 64 * k)
            whole = out[:, 128 * k : 128 * k + 128]

            @pl.when(even)
            def _():
                g_qkv[0, at, 0:512] = slabs[k]
                g_qkv[0, at, 512:576] = three[:, side]
                g_out[0, at, 0:128] = whole
                g_out[0, at, 128:192] = out[:, side]

            @pl.when(jnp.logical_not(even))
            def _():
                g_qkv[0, at, :] = jnp.concatenate([three[:, side], slabs[k]], axis=1)
                g_out[0, at, :] = jnp.concatenate([out[:, side], whole], axis=1)

    if stride > 1:
        for layer in range(2):
            g_vec[layer] = sums[16 * layer : 16 * layer + 8, 0:96]
            g_bias[layer] = sums[16 * layer + 8 : 16 * layer + 12, 0:96]
    else:
        for layer in range(2):
            g_vec[layer] = sums[pl.ds(16 * layer + 2 * doc, 2), 0:96]
            for i in range(4):
                at = 16 * layer + 8 + i
                g_bias[layer : layer + 1, i * 96 : i * 96 + 96] = sums[at : at + 1, 0:96]
    g_pos[...] = sums[32:, 0:96]


def run_assemble(stride, ffn, att, rows_x, rows_y, sums, output, grad_tok):
    shape = jax.ShapeDtypeStruct
    return pl.pallas_call(
        functools.partial(assemble, stride),
        out_shape=(
            shape((2, 96, 576), F32),
            shape((2, 96, 192), F32),
            shape((2, 96, 768), F32),
            shape((2, 192, 384), F32),
            shape((2, 2, 96) if stride == 1 else (2, 8, 96), F32),
            shape((2, 384) if stride == 1 else (2, 4, 96), F32),
            shape((sums.shape[0] - 32, 96), F32),
            shape(output.shape, BF16),
            shape(grad_tok.shape, F32),
        ),
        in_specs=[VM] * 7,
        out_specs=(VM,) * 9,
        compiler_params=pltpu.CompilerParams(vmem_limit_bytes=LIMIT),
        name="assemble",
    )(ffn, att, rows_x, rows_y, sums, output, grad_tok)


def shards(
    tokens,
    token_mask,
    doc_counts,
    w_qkv,
    w_out,
    w_up,
    w_down,
    vectors,
    ffn_bias,
    pos_embed,
    cotangent,
):
    docs, slots, width = tokens.shape
    seg_dev = slots // SEG
    groups = docs * seg_dev
    count = lax.axis_size("seg")
    stride = count // 8
    rest = lax.rem(lax.axis_index("seg"), stride)
    tok = tokens.reshape(groups * SEG, width)
    cot = cotangent.reshape(groups * SEG, width)
    weights = (w_qkv, w_out, w_up, w_down)
    run = run_whole if groups * count <= 16 else run_halves
    output, grad_tok, ffn, att, rows_x, rows_y, _, sums = run(
        stride, count, doc_counts, tok, token_mask.reshape(groups, SEG), cot, pos_embed, vectors, ffn_bias, weights
    )
    g_qkv, g_out, g_up, g_down, g_vec, g_bias, g_pos, output, grad_tok = run_assemble(
        stride, ffn, att, rows_x, rows_y, sums, output, grad_tok
    )
    g_down = jnp.transpose(g_down, (0, 2, 1))
    if stride > 1:
        lanes = [[i * stride + j for j in range(stride)] for i in range(8)]

        def own(arr, dim):
            low = lax.psum_scatter(arr[0:1], "seg", scatter_dimension=dim, axis_index_groups=lanes, tiled=True)
            size = arr.shape[dim] // stride
            return jnp.concatenate([low, lax.dynamic_slice_in_dim(arr[1:2], rest * size, size, dim)], axis=0)

        g_qkv, g_out, g_up, g_down = own(g_qkv, 1), own(g_out, 1), own(g_up, 1), own(g_down, 1)
        each = 96 // stride
        g_vec = lax.dynamic_slice(g_vec, (0, lax.axis_index("doc") * 2, rest * each), (2, 2, each))
        g_bias = lax.dynamic_slice_in_dim(g_bias.reshape(2, 384), rest * (384 // stride), 384 // stride, 1)
        g_pos = lax.dynamic_slice_in_dim(g_pos, rest * each, each, 1)
    return (
        output.reshape(tokens.shape),
        grad_tok.reshape(tokens.shape),
        g_qkv,
        g_out,
        g_up,
        g_down,
        g_vec,
        g_bias,
        g_pos,
    )


def solution(mesh):
    return jax.shard_map(
        shards,
        mesh=mesh,
        in_specs=(
            P("doc", "seg", None),
            P("doc", "seg"),
            P("doc"),
            P(),
            P(),
            P(),
            P(),
            P(),
            P(),
            P(),
            P("doc", "seg", None),
        ),
        out_specs=(
            P("doc", "seg", None),
            P("doc", "seg", None),
            P(None, "seg", "doc"),
            P(None, "seg", "doc"),
            P(None, "seg", "doc"),
            P(None, "seg", "doc"),
            P(None, "doc", "seg"),
            P(None, "seg"),
            P(None, "seg"),
        ),
        check_vma=False,
    )
```
